32 devices in a mesh: lat: 4 (over z), lon: 8 (over y, x, core).
Axes of the slice: x: 2, y: 2, z: 4, core: 2. Of those that a mesh axis runs over, the one named last changes fastest.
Arguments:
- conc: float32 [64, 128, 1024], P('lat', None, 'lon'), may hold values from 0.1 to 2
- wind_lon: float32 [64, 1024], P('lat', 'lon'), may hold values from 0.1 to 0.35
- wind_lat: float32 [64, 1024], P('lat', 'lon'), may hold values from 0.05 to 0.25
- mixing: float32 [64, 1024], P('lat', 'lon'), may hold values from 0.02 to 0.1
- sun: float32 [64, 1024], replicated, may hold values from 0.1 to 1
- rate: float32 [512], replicated, may hold values from 0.02 to 0.3
- night_loss: float32 [128], replicated, may hold values from 0.05 to 1
- stoich: int32 [4, 512], replicated, may hold values from 0 to 127
- plan: int32 [2, 64, 8], replicated, may hold values from -2 to 4, as said below
Outputs:
- conc_out: float32 [64, 128, 1024], P('lat', None, 'lon')
The draws below stay inside these ranges and needn't reach their ends.
Inputs may be any that keep to these rules, and one draw needn't show every extreme that they name: `plan`: code -2 marks a dark block, -1 a sunlit block computed where it lies; a sunlit block with code k in 0, 1, 2 is computed on the lon sector half the axis plus k - 1 further along (modulo the axis), with code 3 on the next sector, with code 4 on the previous one, always in the same latitude band. A sector sends at most 3 blocks of one band with one code, some exactly 3; a sector that sends receives nothing; the blocks a device keeps plus those it receives in a substep number at most 9, exactly 9 on some device.
All inputs are finite; a program needn't handle non-finite values.
Results may differ from the reference program's by a relative error of at most 0.0003.
Values sent between devices are 32-bit elements; how exact they have to be, the bound alone decides.
No kernel may reach another device: no remote copies, remote signals or barrier semaphores. Data moves between devices by JAX's collectives and lax.ppermute only.
A program may use at most 128 MiB of HBM per device.

```python
import math
import jax
import jax.numpy as jnp
from jax import lax

SPEC = 128
REACT = 512
BLK = 128
LAT_DEV = 16
ADV_STEPS = 2
SUBSTEPS = 2
PICARD = 3
PHOT = 128
CAP = 3
NLAT = 64
SECTORS = 8
NLON = 1024


def draw_plan(key, part):
    key_phase, key_score, key_dark = jax.random.split(key, 3)
    band_count = NLAT // LAT_DEV
    half_axis = SECTORS // 2
    phase_shift = jax.random.randint(key_phase, (), 0, SECTORS)
    step_ids = jnp.arange(SUBSTEPS, dtype=jnp.int32).reshape(SUBSTEPS, 1, 1, 1)
    sector_ids = jnp.arange(SECTORS, dtype=jnp.int32).reshape(1, 1, 1, SECTORS)
    day_place = (sector_ids + phase_shift + step_ids) % SECTORS
    is_day = day_place < half_axis
    draw_shape = (SUBSTEPS, band_count, LAT_DEV, SECTORS)
    row_ids = jnp.arange(LAT_DEV, dtype=jnp.int32).reshape(1, 1, LAT_DEV, 1)
    scores = jax.random.randint(key_score, draw_shape, 0, 1048576) * LAT_DEV + row_ids
    row_rank = jnp.argsort(jnp.argsort(scores, axis=2), axis=2).astype(jnp.int32)
    dark_rows = jax.random.randint(key_dark, (SUBSTEPS, band_count, 1, SECTORS), 0, LAT_DEV // 4 + 1)
    dark_rows = jnp.where(day_place == 0, 0, dark_rows)
    sunlit = is_day & (row_rank >= dark_rows)
    lit_order = row_rank - dark_rows
    helper_group = lit_order // CAP
    first_code = jnp.where(helper_group == 2, 4, helper_group + 1)
    last_code = jnp.where(helper_group == 2, 3, helper_group)
    code_value = jnp.where(day_place == 0, first_code, jnp.where(day_place == half_axis - 1, last_code, helper_group))
    plan_codes = jnp.where(helper_group < 3, code_value, -1)
    plan_codes = jnp.where(sunlit, plan_codes, -2)
    return plan_codes.reshape(SUBSTEPS, NLAT, SECTORS).astype(jnp.int32)


def set_ends(drawn, rng, least, largest):
    longest = drawn.shape.index(max(drawn.shape))
    spots = []
    for shift in (0, 1):
        where = [jax.random.randint(jax.random.fold_in(rng, axis), (), 0, length) for axis, length in enumerate(drawn.shape)]
        where[longest] = (where[longest] + shift) % drawn.shape[longest]
        spots.append(tuple(where))
    return drawn.at[spots[0]].set(least).at[spots[1]].set(largest)


def block_scale(own_key, extent, cuts, smallest, largest):
    factor_of, own = 1.0, jax.random.fold_in(own_key, 6)
    for axis_at, parts in cuts:
        draws = jnp.exp(jax.random.uniform(jax.random.fold_in(own, axis_at), (parts,), jnp.float32, smallest / len(cuts), largest / len(cuts)))
        factor_of = factor_of * jnp.repeat(draws, extent[axis_at] // parts).reshape([-1 if axis == axis_at else 1 for axis in range(len(extent))])
    return factor_of


def setup_inputs(seed: int = 0) -> dict:
    key_of = jax.random.split(jax.random.key(seed), 10)
    conc = jnp.clip(jnp.exp(math.log(2.0) - 2.9957323 * jax.random.uniform(key_of[0], (NLAT, SPEC, NLON), jnp.float32) ** block_scale(key_of[0], (NLAT, SPEC, NLON), ((0, 4), (2, 8)), -0.2, 0.2)), 0.1, 2.0)
    wind_lon = jnp.clip(0.1 + 0.25 * jax.random.uniform(key_of[1], (NLAT, NLON), jnp.float32) ** block_scale(key_of[1], (NLAT, NLON), ((0, 4), (1, 8)), -0.2, 0.2), 0.1, 0.35)
    wind_lat = jnp.clip(0.05 + 0.2 * jax.random.uniform(key_of[2], (NLAT, NLON), jnp.float32) ** block_scale(key_of[2], (NLAT, NLON), ((0, 4), (1, 8)), -0.2, 0.2), 0.05, 0.25)
    mixing = jnp.clip(0.02 + 0.08 * jax.random.uniform(key_of[3], (NLAT, NLON), jnp.float32) ** block_scale(key_of[3], (NLAT, NLON), ((0, 4), (1, 8)), -0.2, 0.2), 0.02, 0.1)
    sun = jnp.clip(jax.random.uniform(key_of[4], (NLAT, NLON), jnp.float32, 0.1, 1.0), 0.1, 1.0)
    rate = jnp.clip(jnp.exp(jax.random.uniform(key_of[5], (REACT,), jnp.float32, math.log(0.02), math.log(0.3))), 0.02, 0.3)
    night_loss = jnp.clip(jax.random.uniform(key_of[6], (SPEC,), jnp.float32, 0.05, 1.0), 0.05, 1.0)
    stoich = set_ends(jax.random.randint(key_of[7], (4, REACT), 0, SPEC), jax.random.fold_in(key_of[7], 1), 0, SPEC - 1).astype(jnp.int32)
    plan = draw_plan(jax.random.fold_in(key_of[9], 71), 0)
    return dict(conc=conc, wind_lon=wind_lon, wind_lat=wind_lat, mixing=mixing, sun=sun, rate=rate, night_loss=night_loss, stoich=stoich, plan=plan)


def advect(state_field, wind_east, wind_north, mixing):
    western = jnp.roll(state_field, 1, axis=2)
    eastern = jnp.roll(state_field, -1, axis=2)
    zero_row = jnp.zeros_like(state_field[:1])
    southern = jnp.concatenate([zero_row, state_field[:-1]], axis=0)
    northern = jnp.concatenate([state_field[1:], zero_row], axis=0)
    east_wind = wind_east[:, None, :]
    north_wind = wind_north[:, None, :]
    spread = mixing[:, None, :]
    return state_field - east_wind * (state_field - western) - north_wind * (state_field - southern) + spread * (eastern + western + northern + southern - 4.0 * state_field)


def chem_tables(stoich):
    species_ids = jnp.arange(SPEC, dtype=jnp.int32)[:, None]
    products = (stoich[2][None, :] == species_ids).astype(jnp.float32) + (stoich[3][None, :] == species_ids).astype(jnp.float32)
    first_loss = (stoich[0][None, :] == species_ids).astype(jnp.float32)
    second_loss = (stoich[1][None, :] == species_ids).astype(jnp.float32)
    return products, first_loss, second_loss


def picard_block(start_state, sun_row, rate, stoich, tables):
    products, first_loss, second_loss = tables
    photolytic = jnp.arange(REACT, dtype=jnp.int32) < PHOT
    speeds = rate[:, None] * jnp.where(photolytic[:, None], sun_row[None, :], 1.0)
    current = start_state
    for sweep_index in range(PICARD):
        first_rows = jnp.take(current, stoich[0], axis=0)
        second_rows = jnp.take(current, stoich[1], axis=0)
        produced = jnp.dot(products, speeds * first_rows * second_rows, precision=lax.Precision.HIGHEST)
        lost_rate = jnp.dot(first_loss, speeds * second_rows, precision=lax.Precision.HIGHEST) + jnp.dot(second_loss, speeds * first_rows, precision=lax.Precision.HIGHEST)
        current = (start_state + produced) / (1.0 + lost_rate)
    return current


def reference(conc, wind_lon, wind_lat, mixing, sun, rate, night_loss, stoich, plan):
    state_field = conc
    for adv_index in range(ADV_STEPS):
        state_field = advect(state_field, wind_lon, wind_lat, mixing)
    tables = chem_tables(stoich)
    night_decay = jnp.exp(-night_loss)[:, None]
    sun_blocks = sun.reshape(NLAT * SECTORS, BLK)
    for substep in range(SUBSTEPS):
        blocks = state_field.reshape(NLAT, SPEC, SECTORS, BLK).transpose(0, 2, 1, 3).reshape(NLAT * SECTORS, SPEC, BLK)
        codes_flat = plan[substep].reshape(NLAT * SECTORS)

        def one_block(inputs):
            block_state, sun_row, block_code = inputs
            return lax.cond(block_code >= -1, lambda: picard_block(block_state, sun_row, rate, stoich, tables), lambda: block_state * night_decay)

        finished = lax.map(one_block, (blocks, sun_blocks, codes_flat))
        state_field = finished.reshape(NLAT, SECTORS, SPEC, BLK).transpose(0, 2, 1, 3).reshape(NLAT, SPEC, NLON)
    return state_field
```

```python
import jax
import jax.numpy as jnp
from jax import lax
from jax.experimental import pallas as pl
from jax.experimental.pallas import tpu as pltpu
from jax.sharding import PartitionSpec as P

SUBSTEPS = 2
PICARD = 3
PHOT = 128
LANES = 128
VMEM_LIMIT = 56 << 20

f32 = jnp.float32
bf16 = jnp.bfloat16


def split(x):
    high = x.astype(bf16)
    return high, (x - high.astype(f32)).astype(bf16)


def twice(x):
    return jnp.concatenate([x, x], axis=1)


def dot(a, b):
    return jnp.dot(a, b, preferred_element_type=f32)


def dot_nt(a, b):
    return lax.dot_general(
        a, b, (((1,), (1,)), ((), ())), precision=lax.Precision.HIGHEST, preferred_element_type=f32
    )


def edge_kernel(conc, wlon, wlat, mix, to_right, to_left, to_north, to_south):
    rows, species, cells = conc.shape
    for g in range(rows):
        turned = conc[g].T
        to_right[0:2, g, :] = turned[cells - 2 : cells]
        to_left[0:2, g, :] = turned[0:2]
    for k, ref in enumerate((wlon, wlat, mix)):
        to_right[2 + k] = jnp.broadcast_to(ref[:, cells - 1 : cells], (rows, species))
        to_left[2 + k] = jnp.broadcast_to(ref[:, 0:1], (rows, species))
    for q in range(2):
        to_north[q * species : (q + 1) * species, :] = conc[rows - 2 + q]
        to_south[q * species : (q + 1) * species, :] = conc[q]
    base = 2 * species
    pad = jnp.zeros((5, cells), f32)
    to_north[base:, :] = jnp.concatenate([r[rows - 1 : rows, :] for r in (wlon, wlat, mix)] + [pad])
    to_south[base:, :] = jnp.concatenate([r[0:1, :] for r in (wlon, wlat, mix)] + [pad])


def table_kernel(
    stoich, rate, night, plan, sun, gather, products, losses, speeds, decay, sun_own, lit, sem
):
    species = decay.shape[0]
    reactions = stoich.shape[1]
    rows = sun_own.shape[0]
    chunks = reactions // LANES
    band = lax.axis_index("lat")
    sector = lax.axis_index("lon")
    fetch = pltpu.make_async_copy(
        sun.at[
            pl.ds(pl.multiple_of(band * rows, 8), rows),
            pl.ds(pl.multiple_of(sector * LANES, LANES), LANES),
        ],
        sun_own,
        sem,
    )
    fetch.start()
    ids = lax.broadcasted_iota(jnp.int32, (species, LANES), 0)
    mats = []
    for k in range(chunks):
        cols = pl.ds(k * LANES, LANES)
        hot = [(stoich[q : q + 1, cols] == ids).astype(f32) for q in range(4)]
        for q in range(2):
            gather[pl.ds(q * reactions + k * LANES, LANES), :] = twice(hot[q].T.astype(bf16))
        products[k] = twice((hot[2] + hot[3]).astype(bf16))
        row = jnp.broadcast_to(rate[0:1, cols], (species, LANES))
        speeds[pl.ds(k * LANES, LANES), :] = row.T
        mats.append(dot_nt(hot[0] * row, hot[1]) + dot_nt(hot[1] * row, hot[0]))
    photo = sum(mats[1 : PHOT // LANES], mats[0])
    dark = sum(mats[PHOT // LANES + 1 :], mats[PHOT // LANES])
    for q, mat in enumerate((dark, photo)):
        high, low = split(mat)
        losses[pl.ds(2 * q * species, species), :] = twice(high)
        losses[pl.ds((2 * q + 1) * species, species), :] = twice(low)
    decay[...] = jnp.broadcast_to(jnp.exp(-night[...]), (species, LANES)).T
    for s in range(SUBSTEPS):
        codes = plan[s, pl.ds(pl.multiple_of(band * rows, 8), rows), :]
        lane = lax.broadcasted_iota(jnp.int32, codes.shape, 1)
        own = jnp.sum(jnp.where(lane == sector, codes, 0).astype(f32), axis=1, keepdims=True)
        lit[s] = jnp.broadcast_to((own >= -1.0).astype(f32), (rows, LANES))
    fetch.wait()


def sweep(start, now, photo, gather, products, losses, speeds):
    reactions = speeds.shape[0]
    species = start.shape[0]
    wide = start.shape[1] // LANES
    weights = jnp.concatenate(split(now), axis=0)
    produced = None
    for k in range(reactions // LANES):
        first = dot(gather[pl.ds(k * LANES, LANES), :], weights)
        second = dot(gather[pl.ds(reactions + k * LANES, LANES), :], weights)
        speed = jnp.concatenate([speeds[pl.ds(k * LANES, LANES), :]] * wide, axis=1)
        made = first * speed * second
        if k < PHOT // LANES:
            made = made * photo
        part = dot(products[k], jnp.concatenate(split(made), axis=0))
        produced = part if produced is None else produced + part
    lost = dot(losses[...], weights)
    s = species
    lost = (lost[0:s] + lost[s : 2 * s]) + photo * (lost[2 * s : 3 * s] + lost[3 * s : 4 * s])
    return (start + produced) / (1.0 + lost)


def chemistry(pairs, suns, lits, decay, tables):
    for s in range(SUBSTEPS):
        now = list(pairs)
        for _ in range(PICARD):
            now = [sweep(p, n, u, *tables) for p, n, u in zip(pairs, now, suns)]
        pairs = [
            jnp.where(l > 0.0, n, p * twice(decay)) for p, n, l in zip(pairs, now, lits[s])
        ]
    return pairs


def step(center, west, east, south, north, wl, wt, mx):
    return (
        center
        - wl * (center - west)
        - wt * (center - south)
        + mx * (east + west + north + south - 4.0 * center)
    )


def block_step(center, west_edge, east_edge, south, north, wl, wt, mx):
    cells = center.shape[1]
    lane = lax.broadcasted_iota(jnp.int32, center.shape, 1)
    west = jnp.where(lane == 0, west_edge, pltpu.roll(center, 1, 1))
    east = jnp.where(lane == cells - 1, east_edge, pltpu.roll(center, cells - 1, 1))
    return step(center, west, east, south, north, wl, wt, mx)


def side_columns(from_left, from_right, to_right, to_left, corners):
    rows = from_left.shape[1]
    far_l, near_l = from_left[0], from_left[1]
    near_r, far_r = from_right[0], from_right[1]
    first, last = to_left[0], to_right[1]
    if corners is None:
        zero = jnp.zeros((1, near_l.shape[1]), f32)
        sl, sr, nl, nr = zero, zero, zero, zero
    else:
        sl, sr, nl, nr = corners
    ls = jnp.concatenate([sl, near_l[:-1]], axis=0)
    ln = jnp.concatenate([near_l[1:], nl], axis=0)
    rs = jnp.concatenate([sr, near_r[:-1]], axis=0)
    rn = jnp.concatenate([near_r[1:], nr], axis=0)
    moved_l = step(near_l, far_l, first, ls, ln, from_left[2], from_left[3], from_left[4])
    moved_r = step(near_r, last, far_r, rs, rn, from_right[2], from_right[3], from_right[4])
    extra = jnp.concatenate([sl, sr, nl, nr], axis=0)
    stack = [near_l, near_r, moved_l, moved_r, extra]
    pad = LANES - 4 * rows - 4
    stack.append(jnp.zeros((pad, near_l.shape[1]), f32))
    return jnp.concatenate(stack, axis=0).T


def inner_kernel(
    conc, wlon, wlat, mix, from_left, from_right, to_right, to_left,
    gather, products, losses, speeds, decay, sun, lit, out, moved,
):
    rows = conc.shape[0]
    group = pl.program_id(0)

    @pl.when(group == 0)
    def _():
        turned = side_columns(from_left, from_right, to_right, to_left, None)

        def col(k, g):
            c = k * rows + g
            return turned[:, c : c + 1]

        def coef(g):
            return wlon[g : g + 1, :], wlat[g : g + 1, :], mix[g : g + 1, :]

        once = {}
        for g in range(1, rows - 1):
            once[g] = block_step(
                conc[g], col(0, g), col(1, g), conc[g - 1], conc[g + 1], *coef(g)
            )
            h = g - 1
            if h >= 2:
                moved[h] = block_step(
                    once[h], col(2, h), col(3, h), once[h - 1], once[h + 1], *coef(h)
                )

    base = 2 + 4 * group
    tables = (gather, products, losses, speeds)

    def row_pair(ref, p):
        return jnp.concatenate([ref[pl.ds(base + 2 * p, 1), :], ref[pl.ds(base + 2 * p + 1, 1), :]], axis=1)

    pairs = [
        jnp.concatenate([moved[base + 2 * p], moved[base + 2 * p + 1]], axis=1) for p in range(2)
    ]
    suns = [row_pair(sun, p) for p in range(2)]
    lits = [[row_pair(lit.at[s], p) for p in range(2)] for s in range(SUBSTEPS)]
    pairs = chemistry(pairs, suns, lits, decay[...], tables)
    for p in range(2):
        out[base + 2 * p] = pairs[p][:, :LANES]
        out[base + 2 * p + 1] = pairs[p][:, LANES:]


def outer_kernel(
    conc, wlon, wlat, mix, from_left, from_right, to_right, to_left,
    from_south, from_north, corner_south, corner_north,
    gather, products, losses, speeds, decay, sun, lit, whole, out,
    halves, sem,
):
    rows, species, cells = conc.shape
    corners = (
        corner_south[0:1, :], corner_south[1:2, :], corner_north[0:1, :], corner_north[1:2, :]
    )
    turned = side_columns(from_left, from_right, to_right, to_left, corners)

    def column(c):
        return turned[:, c : c + 1]

    def field(g):
        if g < 0:
            return from_south[(2 + g) * species : (3 + g) * species, :]
        if g >= rows:
            return from_north[(g - rows) * species : (g - rows + 1) * species, :]
        return conc[g]

    def coef(g):
        base = 2 * species
        if g < 0:
            return [from_south[base + k : base + k + 1, :] for k in range(3)]
        if g >= rows:
            return [from_north[base + k : base + k + 1, :] for k in range(3)]
        return [r[g : g + 1, :] for r in (wlon, wlat, mix)]

    def edge(g, side):
        if g < 0:
            return column(4 * rows + side)
        if g >= rows:
            return column(4 * rows + 2 + side)
        return column(side * rows + g)

    pairs = []
    for low in (0, rows - 2):
        once = {}
        for g in range(low - 1, low + 3):
            once[g] = block_step(
                field(g), edge(g, 0), edge(g, 1), field(g - 1), field(g + 1), *coef(g)
            )
        pairs.append(
            jnp.concatenate(
                [
                    block_step(
                        once[g], column(2 * rows + g), column(3 * rows + g),
                        once[g - 1], once[g + 1], *coef(g),
                    )
                    for g in (low, low + 1)
                ],
                axis=1,
            )
        )

    def row_pair(ref, low):
        return jnp.concatenate([ref[low : low + 1, :], ref[low + 1 : low + 2, :]], axis=1)

    lows = (0, rows - 2)
    suns = [row_pair(sun, low) for low in lows]
    lits = [[row_pair(lit.at[s], low) for low in lows] for s in range(SUBSTEPS)]
    pairs = chemistry(pairs, suns, lits, decay[...], (gather, products, losses, speeds))
    for p in range(2):
        halves[p, 0] = pairs[p][:, :LANES]
        halves[p, 1] = pairs[p][:, LANES:]
    copies = [
        pltpu.make_async_copy(halves.at[p], out.at[pl.ds(lows[p], 2)], sem.at[p]) for p in range(2)
    ]
    for c in copies:
        c.start()
    for c in copies:
        c.wait()


def local(conc, wind_lon, wind_lat, mixing, sun, rate, night_loss, stoich, plan):
    rows, species, cells = conc.shape
    reactions = rate.shape[0]
    lons = lax.axis_size("lon")
    lats = lax.axis_size("lat")
    params = pltpu.CompilerParams(vmem_limit_bytes=VMEM_LIMIT)
    vmem = pl.BlockSpec(memory_space=pltpu.VMEM)
    hbm = pl.BlockSpec(memory_space=pl.ANY)
    shape = jax.ShapeDtypeStruct
    side = shape((5, rows, species), f32)
    ends = shape((2 * species + 8, cells), f32)
    to_right, to_left, to_north, to_south = pl.pallas_call(
        edge_kernel, out_shape=(side, side, ends, ends),
        in_specs=[vmem] * 4, out_specs=[vmem] * 4,
        compiler_params=params, name="edges",
    )(conc, wind_lon, wind_lat, mixing)

    east = [(i, (i + 1) % lons) for i in range(lons)]
    west = [(j, i) for i, j in east]
    north = [(i, i + 1) for i in range(lats - 1)]
    south = [(j, i) for i, j in north]
    from_left = lax.ppermute(to_right, "lon", east)
    from_right = lax.ppermute(to_left, "lon", west)
    from_south = lax.ppermute(to_north, "lat", north)
    from_north = lax.ppermute(to_south, "lat", south)

    tables = pl.pallas_call(
        table_kernel,
        out_shape=(
            shape((2 * reactions, 2 * species), bf16),
            shape((reactions // LANES, species, 2 * LANES), bf16),
            shape((4 * species, 2 * species), bf16),
            shape((reactions, LANES), f32),
            shape((species, LANES), f32),
            shape((rows, LANES), f32),
            shape((SUBSTEPS, rows, LANES), f32),
        ),
        in_specs=[vmem] * 4 + [hbm], out_specs=[vmem] * 7,
        scratch_shapes=[pltpu.SemaphoreType.DMA],
        compiler_params=params, name="tables",
    )(stoich, rate.reshape(1, reactions), night_loss.reshape(1, species), plan, sun)

    def corner(g):
        return jnp.concatenate([from_left[1, g : g + 1], from_right[0, g : g + 1]], axis=0)

    corner_south = lax.ppermute(corner(rows - 1), "lat", north)
    corner_north = lax.ppermute(corner(0), "lat", south)

    inner = pl.pallas_call(
        inner_kernel, grid=((rows - 4) // 4,),
        out_shape=shape(conc.shape, f32),
        in_specs=[vmem] * 15, out_specs=vmem,
        scratch_shapes=[pltpu.VMEM((rows, species, cells), f32)],
        compiler_params=params, name="inner",
    )(conc, wind_lon, wind_lat, mixing, from_left, from_right, to_right, to_left, *tables)

    return pl.pallas_call(
        outer_kernel, out_shape=shape(conc.shape, f32),
        in_specs=[vmem] * 19 + [hbm], out_specs=hbm,
        scratch_shapes=[pltpu.VMEM((2, 2, species, cells), f32), pltpu.SemaphoreType.DMA((2,))],
        input_output_aliases={19: 0},
        compiler_params=params, name="outer",
    )(
        conc, wind_lon, wind_lat, mixing, from_left, from_right, to_right, to_left,
        from_south, from_north, corner_south, corner_north, *tables, inner,
    )


def solution(mesh):
    field = P("lat", None, "lon")
    cell = P("lat", "lon")
    return jax.shard_map(
        local,
        mesh=mesh,
        in_specs=(field, cell, cell, cell, P(), P(), P(), P(), P()),
        out_specs=field,
        check_vma=False,
    )
```

```python
import jax
import jax.numpy as jnp
from jax import lax
from jax.experimental import pallas as pl
from jax.experimental.pallas import tpu as pltpu
from jax.sharding import PartitionSpec as P

SUBSTEPS = 2
PICARD = 3
PHOT = 128
LANES = 128
VMEM_LIMIT = 48 << 20
KEPT = jax.ShapeDtypeStruct

f32 = jnp.float32
bf16 = jnp.bfloat16


def split(x):
    high = x.astype(bf16)
    return high, (x - high.astype(f32)).astype(bf16)


def twice(x):
    return jnp.concatenate([x, x], axis=1)


def dot(a, b):
    return jnp.dot(a, b, preferred_element_type=f32)


def iota(shape, axis):
    return lax.broadcasted_iota(jnp.int32, shape, axis)


def edge_kernel(conc, wlon, wlat, mix, to_pair, to_other, own, to_north, to_south, columns):
    rows, species, cells = conc.shape
    lane = iota((species, cells), 1)
    picked = jnp.zeros((species, cells), f32)
    for g in range(rows):
        turned = pltpu.roll(conc[g], (4 * g + 2) % cells, 1)
        picked = jnp.where((lane >= 4 * g) & (lane < 4 * g + 4), turned, picked)
    columns[...] = picked.T
    last2, last1, first1, first2 = [columns[pl.ds(q, rows, stride=4), :] for q in range(4)]
    even = lax.rem(lax.axis_index("lon"), 2) == 0

    def put(k, right, left):
        to_pair[k] = jnp.where(even, right, left)
        to_other[k] = jnp.where(even, left, right)

    put(0, last1, first1)
    put(1, last2, first2)
    for k, ref in enumerate((wlon, wlat, mix)):
        put(
            2 + k,
            jnp.broadcast_to(ref[:, cells - 1 : cells], (rows, species)),
            jnp.broadcast_to(ref[:, 0:1], (rows, species)),
        )
    own[0] = first1
    own[1] = last1
    for q in range(2):
        to_north[q * species : (q + 1) * species, :] = conc[rows - 2 + q]
        to_south[q * species : (q + 1) * species, :] = conc[q]
    base = 2 * species
    pad = jnp.zeros((5, cells), f32)
    to_north[base : base + 8, :] = jnp.concatenate([r[rows - 1 : rows, :] for r in (wlon, wlat, mix)] + [pad])
    to_south[base : base + 8, :] = jnp.concatenate([r[0:1, :] for r in (wlon, wlat, mix)] + [pad])


def sides(of_pair, of_other):
    even = lax.rem(lax.axis_index("lon"), 2) == 0
    return (
        lambda k: jnp.where(even, of_other[k], of_pair[k]),
        lambda k: jnp.where(even, of_pair[k], of_other[k]),
    )


def corner_kernel(of_pair, of_other, _, __, ___, to_north, to_south, ends, sem):
    rows = of_pair.shape[1]
    left, right = sides(of_pair, of_other)
    near_l, near_r = left(0), right(0)
    pad = jnp.zeros((6, near_l.shape[1]), f32)
    copies = []
    for p, (g, ref) in enumerate(((rows - 1, to_north), (0, to_south))):
        ends[p] = jnp.concatenate([near_l[g : g + 1], near_r[g : g + 1], pad], axis=0)
        dest = ref.at[pl.ds(ref.shape[0] - 8, 8), :]
        copies.append(pltpu.make_async_copy(ends.at[p], dest, sem.at[p]))
        copies[p].start()
    for c in copies:
        c.wait()


def table_kernel(
    stoich, rate, night, plan, sun, gather, products, speeds, decay, sun_own, lit, turned, sem
):
    species = decay.shape[0]
    reactions = stoich.shape[1]
    rows = sun_own.shape[0]
    chunks = reactions // LANES
    band = lax.axis_index("lat")
    sector = lax.axis_index("lon")
    fetch = pltpu.make_async_copy(
        sun.at[
            pl.ds(pl.multiple_of(band * rows, 8), rows),
            pl.ds(pl.multiple_of(sector * LANES, LANES), LANES),
        ],
        sun_own,
        sem,
    )
    fetch.start()
    down = iota((species, LANES), 0)
    across = iota((LANES, species), 1).astype(f32)
    mats = []
    for k in range(chunks):
        cols = pl.ds(k * LANES, LANES)
        codes = stoich[:, cols]
        row = rate[0:1, cols]
        small = jnp.concatenate([codes.astype(f32), row, jnp.zeros((3, LANES), f32)], axis=0).T
        hot = [(codes[q : q + 1, :] == down).astype(f32) for q in range(4)]
        seconds = None
        for q in range(2):
            picks = (small[:, q : q + 1] == across).astype(f32).astype(bf16)
            gather[pl.ds(q * reactions + k * LANES, LANES), :] = twice(picks)
            seconds = picks
        products[:, 2 * k * LANES : (2 * k + 2) * LANES] = twice((hot[2] + hot[3]).astype(bf16))
        speeds[pl.ds(k * LANES, LANES), :] = jnp.broadcast_to(small[:, 4:5], (LANES, LANES))
        parts = jnp.concatenate(split(hot[0] * row), axis=0)
        both = dot(parts, seconds)
        mats.append(both[:species] + both[species:])
    photo = sum(mats[1 : PHOT // LANES], mats[0])
    dark = sum(mats[PHOT // LANES + 1 :], mats[PHOT // LANES])
    for q, mat in enumerate((dark, photo)):
        high, low = split(mat + mat.T)
        base = 2 * reactions + 2 * q * species
        gather[pl.ds(base, species), :] = twice(high)
        gather[pl.ds(base + species, species), :] = twice(low)
    strip = []
    for s in range(SUBSTEPS):
        codes = plan[s]
        own = jnp.where(iota(codes.shape, 0) == sector, codes, 0).astype(f32)
        strip.append(jnp.sum(own, axis=0, keepdims=True))
    lats = plan.shape[2]
    flags = jnp.concatenate(strip + [jnp.zeros((8 - SUBSTEPS, lats), f32)], axis=0)
    flags = jnp.concatenate([flags, jnp.zeros((8, LANES - lats), f32)], axis=1)
    fade = jnp.exp(-night[...])
    spread = jnp.concatenate([flags, fade, jnp.zeros((7, LANES), f32)], axis=0).T
    decay[...] = jnp.broadcast_to(spread[:, 8:9], (species, LANES))
    for s in range(SUBSTEPS):
        turned[...] = jnp.broadcast_to(spread[:, s : s + 1], turned.shape)
        mine = turned[pl.ds(pl.multiple_of(band * rows, 8), rows), :]
        lit[s] = (mine >= -1.0).astype(f32)
    fetch.wait()


def sweep(starts, nows, photos, gather, products, speeds):
    reactions = speeds.shape[0]
    species = starts[0].shape[0]
    weights = [jnp.concatenate(split(now), axis=0) for now in nows]
    losses = [dot(gather[2 * reactions :, :], w) for w in weights]
    made = [[] for _ in nows]
    for k in range(reactions // LANES):
        speed = twice(speeds[k * LANES : (k + 1) * LANES, :])
        for p, w in enumerate(weights):
            first = dot(gather[k * LANES : (k + 1) * LANES, :], w)
            second = dot(gather[reactions + k * LANES : reactions + (k + 1) * LANES, :], w)
            flow = first * speed * second
            if k < PHOT // LANES:
                flow = flow * photos[p]
            made[p].extend(split(flow))
    after = []
    s = species
    for start, flows, loss, photo in zip(starts, made, losses, photos):
        produced = dot(products[...], jnp.concatenate(flows, axis=0))
        lost = (loss[0:s] + loss[s : 2 * s]) + photo * (loss[2 * s : 3 * s] + loss[3 * s :])
        after.append((start + produced) / (1.0 + lost))
    return after


def chemistry(pairs, lows, decay, sun, lit, tables):
    def both(ref, low):
        return jnp.concatenate([ref[low : low + 1, :], ref[low + 1 : low + 2, :]], axis=1)

    photos = [both(sun, low) for low in lows]
    fade = twice(decay[...])
    for s in range(SUBSTEPS):
        now = list(pairs)
        for _ in range(PICARD):
            now = sweep(pairs, now, photos, *tables)
        pairs = [
            jnp.where(both(lit.at[s], low) > 0.0, n, p * fade)
            for p, n, low in zip(pairs, now, lows)
        ]
    return pairs


def step(center, west, east, south, north, wl, wt, mx):
    return (
        center
        - wl * (center - west)
        - wt * (center - south)
        + mx * (east + west + north + south - 4.0 * center)
    )


def block_step(center, west_edge, east_edge, south, north, wl, wt, mx):
    cells = center.shape[1]
    lane = lax.broadcasted_iota(jnp.int32, center.shape, 1)
    west = jnp.where(lane == 0, west_edge, pltpu.roll(center, 1, 1))
    east = jnp.where(lane == cells - 1, east_edge, pltpu.roll(center, cells - 1, 1))
    return step(center, west, east, south, north, wl, wt, mx)


def side_columns(of_pair, of_other, own, corners):
    rows = of_pair.shape[1]
    left, right = sides(of_pair, of_other)
    near_l, near_r = left(0), right(0)
    zero = jnp.zeros((1, near_l.shape[1]), f32)
    sl, sr, nl, nr = corners if corners else (zero, zero, zero, zero)

    def moved(near, west, east, south, north, side):
        south = jnp.concatenate([south, near[:-1]], axis=0)
        north = jnp.concatenate([near[1:], north], axis=0)
        return step(near, west, east, south, north, side(2), side(3), side(4))

    moved_l = moved(near_l, left(1), own[0], sl, nl, left)
    moved_r = moved(near_r, own[1], right(1), sr, nr, right)
    pad = jnp.zeros((LANES - 4 * rows - 4, near_l.shape[1]), f32)
    stack = [near_l, near_r, moved_l, moved_r, sl, sr, nl, nr, pad]
    return jnp.concatenate(stack, axis=0).T


def moved_pairs(runs, field, coef, turned, rows):
    def column(c):
        return turned[:, c : c + 1]

    def edge(g, side):
        if g < 0:
            return column(4 * rows + side)
        if g >= rows:
            return column(4 * rows + 2 + side)
        return column(side * rows + g)

    pairs, lows = [], []
    for low, count in runs:
        once, twofold = {}, {}
        for g in range(low - 1, low + count + 1):
            once[g] = block_step(
                field(g), edge(g, 0), edge(g, 1), field(g - 1), field(g + 1), *coef(g)
            )
            h = g - 1
            if h >= low:
                twofold[h] = block_step(
                    once[h], column(2 * rows + h), column(3 * rows + h),
                    once[h - 1], once[h + 1], *coef(h),
                )
        for h in range(low, low + count, 2):
            lows.append(h)
            pairs.append(jnp.concatenate([twofold[h], twofold[h + 1]], axis=1))
    return pairs, lows


def store_pairs(pairs, lows, out, stage, sem):
    copies = []
    for p, low in enumerate(lows):
        stage[2 * p] = pairs[p][:, :LANES]
        stage[2 * p + 1] = pairs[p][:, LANES:]
        copies.append(
            pltpu.make_async_copy(stage.at[pl.ds(2 * p, 2)], out.at[pl.ds(low, 2)], sem.at[p])
        )
        copies[p].start()
    for c in copies:
        c.wait()


def inner_kernel(
    conc, wlon, wlat, mix, of_pair, of_other, own,
    gather, products, speeds, decay, sun, lit, out, stage, sem,
):
    rows = conc.shape[0]
    turned = side_columns(of_pair, of_other, own, None)

    def coef(g):
        return [r[g : g + 1, :] for r in (wlon, wlat, mix)]

    runs = [(rows // 4, rows // 2)]
    pairs, lows = moved_pairs(runs, lambda g: conc[g], coef, turned, rows)
    pairs = chemistry(pairs, lows, decay, sun, lit, (gather, products, speeds))
    store_pairs(pairs, lows, out, stage, sem)


def outer_kernel(
    conc, wlon, wlat, mix, of_pair, of_other, own, of_south, of_north,
    gather, products, speeds, decay, sun, lit, _, out, stage, sem,
):
    rows, species, cells = conc.shape
    base = 2 * species
    band = lax.axis_index("lat")
    below = jnp.where(band > 0, 1.0, 0.0)
    above = jnp.where(band < lax.axis_size("lat") - 1, 1.0, 0.0)
    corners = [
        r[base + 8 + k : base + 9 + k, :] * inside
        for r, inside in ((of_south, below), (of_north, above))
        for k in range(2)
    ]
    turned = side_columns(of_pair, of_other, own, corners)

    def field(g):
        if g < 0:
            return of_south[(2 + g) * species : (3 + g) * species, :] * below
        if g >= rows:
            return of_north[(g - rows) * species : (g - rows + 1) * species, :] * above
        return conc[g]

    def coef(g):
        if g < 0:
            return [of_south[base + k : base + k + 1, :] * below for k in range(3)]
        if g >= rows:
            return [of_north[base + k : base + k + 1, :] * above for k in range(3)]
        return [r[g : g + 1, :] for r in (wlon, wlat, mix)]

    runs = [(0, rows // 4), (rows - rows // 4, rows // 4)]
    pairs, lows = moved_pairs(runs, field, coef, turned, rows)
    pairs = chemistry(pairs, lows, decay, sun, lit, (gather, products, speeds))
    store_pairs(pairs, lows, out, stage, sem)


def local(conc, wind_lon, wind_lat, mixing, sun, rate, night_loss, stoich, plan):
    rows, species, cells = conc.shape
    reactions = rate.shape[0]
    lons = lax.axis_size("lon")
    lats = lax.axis_size("lat")
    params = pltpu.CompilerParams(vmem_limit_bytes=VMEM_LIMIT)
    vmem = pl.BlockSpec(memory_space=pltpu.VMEM)
    hbm = pl.BlockSpec(memory_space=pl.ANY)

    def shape(*dims, dtype=f32):
        return KEPT(dims, dtype)

    side = shape(5, rows, species)
    ends = shape(2 * species + 16, cells)
    to_pair, to_other, own, to_north, to_south = pl.pallas_call(
        edge_kernel, out_shape=(side, side, shape(2, rows, species), ends, ends),
        in_specs=[vmem] * 4, out_specs=[vmem] * 5,
        scratch_shapes=[pltpu.VMEM((cells, species), f32)],
        compiler_params=params, name="edges",
    )(conc, wind_lon, wind_lat, mixing)

    pair = [(i, i ^ 1) for i in range(lons)]
    other = [(i, (i - 1) % lons if i % 2 == 0 else (i + 1) % lons) for i in range(lons)]
    north = [(i, (i + 1) % lats) for i in range(lats)]
    south = [(j, i) for i, j in north]
    of_pair = lax.ppermute(to_pair, "lon", pair)
    of_other = lax.ppermute(to_other, "lon", other)

    tables = pl.pallas_call(
        table_kernel,
        out_shape=(
            shape(2 * reactions + 4 * species, 2 * species, dtype=bf16),
            shape(species, 2 * reactions, dtype=bf16),
            shape(reactions, LANES),
            shape(species, LANES),
            shape(rows, LANES),
            shape(SUBSTEPS, rows, LANES),
        ),
        in_specs=[vmem] * 4 + [hbm], out_specs=[vmem] * 6,
        scratch_shapes=[pltpu.VMEM((LANES, LANES), f32), pltpu.SemaphoreType.DMA],
        cost_estimate=pl.CostEstimate(flops=10**9, transcendentals=0, bytes_accessed=2 * 10**6),
        compiler_params=params, name="tables",
    )(
        stoich, rate.reshape(1, reactions), night_loss.reshape(1, species),
        jnp.swapaxes(plan, 1, 2), sun,
    )

    to_north, to_south = pl.pallas_call(
        corner_kernel, out_shape=(ends, ends),
        in_specs=[vmem] * 2 + [hbm] * 3, out_specs=[hbm] * 2,
        scratch_shapes=[pltpu.VMEM((2, 8, species), f32), pltpu.SemaphoreType.DMA((2,))],
        input_output_aliases={2: 0, 3: 1},
        compiler_params=params, name="corners",
    )(of_pair, of_other, to_north, to_south, tables[4])
    of_south = lax.ppermute(to_north, "lat", north)
    of_north = lax.ppermute(to_south, "lat", south)

    shared = (conc, wind_lon, wind_lat, mixing, of_pair, of_other, own)
    scratch = [pltpu.VMEM((rows // 2, species, cells), f32), pltpu.SemaphoreType.DMA((rows // 4,))]
    inner = pl.pallas_call(
        inner_kernel, out_shape=jax.ShapeDtypeStruct(conc.shape, f32),
        in_specs=[vmem] * 13, out_specs=hbm, scratch_shapes=scratch,
        compiler_params=params, name="inner",
    )(*shared, *tables)
    return pl.pallas_call(
        outer_kernel, out_shape=jax.ShapeDtypeStruct(conc.shape, f32),
        in_specs=[vmem] * 15 + [hbm], out_specs=hbm, scratch_shapes=scratch,
        input_output_aliases={15: 0},
        compiler_params=params, name="outer",
    )(*shared, of_south, of_north, *tables, inner)


def solution(mesh):
    field = P("lat", None, "lon")
    cell = P("lat", "lon")
    return jax.shard_map(
        local,
        mesh=mesh,
        in_specs=(field, cell, cell, cell, P(), P(), P(), P(), P()),
        out_specs=field,
        check_vma=False,
    )
```

```python
import jax
import jax.numpy as jnp
from jax import lax
from jax.experimental import pallas as pl
from jax.experimental.pallas import tpu as pltpu
from jax.sharding import PartitionSpec as P

SUBSTEPS = 2
PICARD = 3
PHOT = 128
LANES = 128
VMEM_LIMIT = 48 << 20
KEPT = jax.ShapeDtypeStruct
CHUNK = 256
STAGGER = 2

f32 = jnp.float32
bf16 = jnp.bfloat16


def split(x):
    high = x.astype(bf16)
    return high, (x - high.astype(f32)).astype(bf16)


def twice(x):
    return jnp.concatenate([x, x], axis=1)


def dot(a, b):
    return jnp.dot(a, b, preferred_element_type=f32)


def iota(shape, axis):
    return lax.broadcasted_iota(jnp.int32, shape, axis)


def edge_kernel(
    conc_in, wlon_in, wlat_in, mix_in, to_pair, to_other, own, to_north, to_south,
    conc, winds, columns, sem,
):
    rows, species, cells = conc.shape
    fetches = [
        pltpu.make_async_copy(ref, winds.at[k], sem.at[k])
        for k, ref in enumerate((wlon_in, wlat_in, mix_in))
    ]
    fetches.append(pltpu.make_async_copy(conc_in, conc, sem.at[3]))
    for fetch in fetches:
        fetch.start()
    for fetch in fetches:
        fetch.wait()
    wlon, wlat, mix = [winds.at[k] for k in range(3)]
    lane = iota((species, cells), 1)
    picked = jnp.zeros((species, cells), f32)
    for g in range(rows):
        turned = pltpu.roll(conc[g], (4 * g + 2) % cells, 1)
        picked = jnp.where((lane >= 4 * g) & (lane < 4 * g + 4), turned, picked)
    columns[...] = picked.T
    last2, last1, first1, first2 = [columns[pl.ds(q, rows, stride=4), :] for q in range(4)]
    even = lax.rem(lax.axis_index("lon"), 2) == 0

    def put(k, right, left):
        to_pair[k] = jnp.where(even, right, left)
        to_other[k] = jnp.where(even, left, right)

    put(0, last1, first1)
    put(1, last2, first2)
    for k, ref in enumerate((wlon, wlat, mix)):
        put(
            2 + k,
            jnp.broadcast_to(ref[:, cells - 1 : cells], (rows, species)),
            jnp.broadcast_to(ref[:, 0:1], (rows, species)),
        )
    own[0] = first1
    own[1] = last1
    for q in range(2):
        to_north[q * species : (q + 1) * species, :] = conc[rows - 2 + q]
        to_south[q * species : (q + 1) * species, :] = conc[q]
    base = 2 * species
    pad = jnp.zeros((5, cells), f32)
    to_north[base : base + 8, :] = jnp.concatenate([r[rows - 1 : rows, :] for r in (wlon, wlat, mix)] + [pad])
    to_south[base : base + 8, :] = jnp.concatenate([r[0:1, :] for r in (wlon, wlat, mix)] + [pad])


def sides(of_pair, of_other):
    even = lax.rem(lax.axis_index("lon"), 2) == 0
    return (
        lambda k: jnp.where(even, of_other[k], of_pair[k]),
        lambda k: jnp.where(even, of_pair[k], of_other[k]),
    )


def corner_kernel(of_pair, of_other, _, __, ___, to_north, to_south, ends, sem):
    rows = of_pair.shape[1]
    left, right = sides(of_pair, of_other)
    near_l, near_r = left(0), right(0)
    pad = jnp.zeros((6, near_l.shape[1]), f32)
    copies = []
    for p, (g, ref) in enumerate(((rows - 1, to_north), (0, to_south))):
        ends[p] = jnp.concatenate([near_l[g : g + 1], near_r[g : g + 1], pad], axis=0)
        dest = ref.at[pl.ds(ref.shape[0] - 8, 8), :]
        copies.append(pltpu.make_async_copy(ends.at[p], dest, sem.at[p]))
        copies[p].start()
    for c in copies:
        c.wait()


def table_kernel(
    stoich, rate, plan, night_in, sun, gather, products, losses, speeds, decay, sun_own, lit,
    night, turned, sem,
):
    species = decay.shape[0]
    reactions = stoich.shape[1]
    rows = sun_own.shape[0]
    chunks = reactions // LANES
    band = lax.axis_index("lat")
    sector = lax.axis_index("lon")
    fetch = pltpu.make_async_copy(
        sun.at[
            pl.ds(pl.multiple_of(band * rows, 8), rows),
            pl.ds(pl.multiple_of(sector * LANES, LANES), LANES),
        ],
        sun_own,
        sem.at[0],
    )
    fetch.start()
    fetch_night = pltpu.make_async_copy(night_in, night, sem.at[1])
    fetch_night.start()
    down = iota((species, LANES), 0)
    across = iota((LANES, species), 1).astype(f32)
    mats = []
    for k in range(chunks):
        cols = pl.ds(k * LANES, LANES)
        codes = stoich[:, cols]
        row = rate[0:1, cols]
        small = jnp.concatenate([codes.astype(f32), row, jnp.zeros((3, LANES), f32)], axis=0).T
        hot = [(codes[q : q + 1, :] == down).astype(f32) for q in range(4)]
        seconds = None
        for q in range(2):
            picks = (small[:, q : q + 1] == across).astype(f32).astype(bf16)
            gather[pl.ds(q * reactions + k * LANES, LANES), :] = twice(picks)
            seconds = picks
        products[:, 2 * k * LANES : (2 * k + 2) * LANES] = twice((hot[2] + hot[3]).astype(bf16))
        speeds[pl.ds(k * LANES, LANES), :] = jnp.broadcast_to(small[:, 4:5], (LANES, LANES))
        parts = jnp.concatenate(split(hot[0] * row), axis=0)
        both = dot(parts, seconds)
        mats.append(both[:species] + both[species:])
    photo = sum(mats[1 : PHOT // LANES], mats[0])
    dark = sum(mats[PHOT // LANES + 1 :], mats[PHOT // LANES])
    for q, mat in enumerate((dark, photo)):
        high, low = split(mat + mat.T)
        losses[:, 2 * q * species : 2 * (q + 1) * species] = twice(high)
        losses[:, (4 + q) * species : (5 + q) * species] = low
    strip = []
    for s in range(SUBSTEPS):
        codes = plan[s]
        own = jnp.where(iota(codes.shape, 0) == sector, codes, 0).astype(f32)
        strip.append(jnp.sum(own, axis=0, keepdims=True))
    lats = plan.shape[2]
    flags = jnp.concatenate(strip + [jnp.zeros((8 - SUBSTEPS, lats), f32)], axis=0)
    flags = jnp.concatenate([flags, jnp.zeros((8, LANES - lats), f32)], axis=1)
    fetch_night.wait()
    fade = jnp.exp(-night[...])
    spread = jnp.concatenate([flags, fade, jnp.zeros((7, LANES), f32)], axis=0).T
    decay[...] = jnp.broadcast_to(spread[:, 8:9], (species, LANES))
    for s in range(SUBSTEPS):
        turned[...] = jnp.broadcast_to(spread[:, s : s + 1], turned.shape)
        mine = turned[pl.ds(pl.multiple_of(band * rows, 8), rows), :]
        lit[s] = (mine >= -1.0).astype(f32)
    fetch.wait()


def pair_steps(field, low, store, decay, sun, lit, gather, products, losses, speeds):
    reactions, species = speeds.shape[0], decay.shape[0]

    def both(ref):
        return jnp.concatenate([ref[low : low + 1, :], ref[low + 1 : low + 2, :]], axis=1)

    def begin(d):
        d["start"] = d["now"] = jnp.concatenate([field(low), field(low + 1)], axis=1)

    def prepare(d):
        photo = both(sun)
        high, low_part = split(d["now"])
        sun_high, sun_low = split(d["now"] * photo)
        d["weights"] = jnp.concatenate([high, low_part], axis=0)
        d["all"] = jnp.concatenate([high, low_part, sun_high, sun_low, high, sun_high], axis=0)
        d["made"] = []

    def lose(d):
        d["lost"] = dot(losses[...], d["all"])

    def react(k):
        def run(d):
            rows = slice(k * CHUNK, (k + 1) * CHUNK)
            later = slice(reactions + k * CHUNK, reactions + (k + 1) * CHUNK)
            first, second = dot(gather[rows, :], d["weights"]), dot(gather[later, :], d["weights"])
            for q in range(CHUNK // LANES):
                part = slice(q * LANES, (q + 1) * LANES)
                base = k * CHUNK + q * LANES
                flow = first[part] * twice(speeds[base : base + LANES, :]) * second[part]
                if base < PHOT:
                    flow = flow * both(sun)
                d["made"].extend(split(flow))

        return run

    def produce(d):
        d["produced"] = dot(products[...], jnp.concatenate(d["made"], axis=0))

    def close(s, last):
        def run(d):
            d["now"] = (d["start"] + d["produced"]) / (1.0 + d["lost"])
            if last:
                dark = d["start"] * twice(decay[...])
                d["now"] = d["start"] = jnp.where(both(lit.at[s]) > 0.0, d["now"], dark)

        return run

    steps = [begin]
    for s in range(SUBSTEPS):
        for sweep in range(PICARD):
            steps += [prepare, react(0), lose]
            steps += [react(k) for k in range(1, reactions // CHUNK)]
            steps += [produce, close(s, sweep == PICARD - 1)]
    steps.append(lambda d: store(low, d["now"]))
    return steps


def chemistry(lows, field, store, *refs):
    lists = [pair_steps(field, low, store, *refs) for low in lows]
    state = [{} for _ in lows]
    for t in range(len(lists[0]) + STAGGER * (len(lows) - 1)):
        for p, steps in enumerate(lists):
            at = t - STAGGER * p
            if 0 <= at < len(steps):
                steps[at](state[p])


def step(center, west, east, south, north, wl, wt, mx):
    return (
        center
        - wl * (center - west)
        - wt * (center - south)
        + mx * (east + west + north + south - 4.0 * center)
    )


def block_step(center, west_edge, east_edge, south, north, wl, wt, mx):
    cells = center.shape[1]
    lane = lax.broadcasted_iota(jnp.int32, center.shape, 1)
    west = jnp.where(lane == 0, west_edge, pltpu.roll(center, 1, 1))
    east = jnp.where(lane == cells - 1, east_edge, pltpu.roll(center, cells - 1, 1))
    return step(center, west, east, south, north, wl, wt, mx)


def side_columns(of_pair, of_other, own, corners):
    rows = of_pair.shape[1]
    left, right = sides(of_pair, of_other)
    near_l, near_r = left(0), right(0)
    zero = jnp.zeros((1, near_l.shape[1]), f32)
    sl, sr, nl, nr = corners if corners else (zero, zero, zero, zero)

    def moved(near, west, east, south, north, side):
        south = jnp.concatenate([south, near[:-1]], axis=0)
        north = jnp.concatenate([near[1:], north], axis=0)
        return step(near, west, east, south, north, side(2), side(3), side(4))

    moved_l = moved(near_l, left(1), own[0], sl, nl, left)
    moved_r = moved(near_r, own[1], right(1), sr, nr, right)
    pad = jnp.zeros((LANES - 4 * rows - 4, near_l.shape[1]), f32)
    stack = [near_l, near_r, moved_l, moved_r, sl, sr, nl, nr, pad]
    return jnp.concatenate(stack, axis=0).T


def mover(field, coef, turned, rows):
    def column(c):
        return turned[:, c : c + 1]

    def edge(g, side):
        if g < 0:
            return column(4 * rows + side)
        if g >= rows:
            return column(4 * rows + 2 + side)
        return column(side * rows + g)

    known = {}

    def once(g):
        if g not in known:
            known[g] = block_step(
                field(g), edge(g, 0), edge(g, 1), field(g - 1), field(g + 1), *coef(g)
            )
        return known[g]

    def moved(g):
        sides = column(2 * rows + g), column(3 * rows + g)
        return block_step(once(g), *sides, once(g - 1), once(g + 1), *coef(g))

    return moved


def storer(lows, out, stage, sem):
    copies = []

    def store(low, pair):
        p = lows.index(low)
        stage[2 * p] = pair[:, :LANES]
        stage[2 * p + 1] = pair[:, LANES:]
        copies.append(
            pltpu.make_async_copy(stage.at[pl.ds(2 * p, 2)], out.at[pl.ds(low, 2)], sem.at[p])
        )
        copies[-1].start()

    return store, copies


def finish(lows, moved, refs, out, stage, sem):
    store, copies = storer(lows, out, stage, sem)
    chemistry(lows, moved, store, *refs)
    for c in copies:
        c.wait()


def inner_kernel(
    conc, wlon, wlat, mix, of_pair, of_other, own,
    gather, products, losses, speeds, decay, sun, lit, out, stage, sem,
):
    rows = conc.shape[0]
    turned = side_columns(of_pair, of_other, own, None)

    def coef(g):
        return [r[g : g + 1, :] for r in (wlon, wlat, mix)]

    lows = list(range(rows // 4, rows - rows // 4, 2))
    moved = mover(lambda g: conc[g], coef, turned, rows)
    finish(lows, moved, (decay, sun, lit, gather, products, losses, speeds), out, stage, sem)


def outer_kernel(
    conc, wlon, wlat, mix, of_pair, of_other, own, of_south, of_north,
    gather, products, losses, speeds, decay, sun, lit, _, out, stage, sem,
):
    rows, species, cells = conc.shape
    base = 2 * species
    band = lax.axis_index("lat")
    below = jnp.where(band > 0, 1.0, 0.0)
    above = jnp.where(band < lax.axis_size("lat") - 1, 1.0, 0.0)
    corners = [
        r[base + 8 + k : base + 9 + k, :] * inside
        for r, inside in ((of_south, below), (of_north, above))
        for k in range(2)
    ]
    turned = side_columns(of_pair, of_other, own, corners)

    def field(g):
        if g < 0:
            return of_south[(2 + g) * species : (3 + g) * species, :] * below
        if g >= rows:
            return of_north[(g - rows) * species : (g - rows + 1) * species, :] * above
        return conc[g]

    def coef(g):
        if g < 0:
            return [of_south[base + k : base + k + 1, :] * below for k in range(3)]
        if g >= rows:
            return [of_north[base + k : base + k + 1, :] * above for k in range(3)]
        return [r[g : g + 1, :] for r in (wlon, wlat, mix)]

    lows = list(range(0, rows // 4, 2)) + list(range(rows - rows // 4, rows, 2))
    moved = mover(field, coef, turned, rows)
    finish(lows, moved, (decay, sun, lit, gather, products, losses, speeds), out, stage, sem)


def local(conc, wind_lon, wind_lat, mixing, sun, rate, night_loss, stoich, plan):
    rows, species, cells = conc.shape
    reactions = rate.shape[0]
    lons = lax.axis_size("lon")
    lats = lax.axis_size("lat")
    params = pltpu.CompilerParams(vmem_limit_bytes=VMEM_LIMIT)
    vmem = pl.BlockSpec(memory_space=pltpu.VMEM)
    hbm = pl.BlockSpec(memory_space=pl.ANY)
    far = pl.BlockSpec(memory_space=pltpu.HBM)

    def pinned(x):
        return pltpu.with_memory_space_constraint(x, pltpu.HBM)

    def shape(*dims, dtype=f32):
        return KEPT(dims, dtype)

    side = shape(5, rows, species)
    ends = shape(2 * species + 16, cells)
    to_pair, to_other, own, to_north, to_south = pl.pallas_call(
        edge_kernel, out_shape=(side, side, shape(2, rows, species), ends, ends),
        in_specs=[far] * 4, out_specs=[vmem] * 5,
        scratch_shapes=[
            pltpu.VMEM(conc.shape, f32),
            pltpu.VMEM((3, rows, cells), f32),
            pltpu.VMEM((cells, species), f32),
            pltpu.SemaphoreType.DMA((4,)),
        ],
        compiler_params=params, name="edges",
    )(*[pinned(x) for x in (conc, wind_lon, wind_lat, mixing)])

    pair = [(i, i ^ 1) for i in range(lons)]
    other = [(i, (i - 1) % lons if i % 2 == 0 else (i + 1) % lons) for i in range(lons)]
    north = [(i, (i + 1) % lats) for i in range(lats)]
    south = [(j, i) for i, j in north]
    of_pair = lax.ppermute(to_pair, "lon", pair)
    of_other = lax.ppermute(to_other, "lon", other)

    tables = pl.pallas_call(
        table_kernel,
        out_shape=(
            shape(2 * reactions, 2 * species, dtype=bf16),
            shape(species, 2 * reactions, dtype=bf16),
            shape(species, 6 * species, dtype=bf16),
            shape(reactions, LANES),
            shape(species, LANES),
            shape(rows, LANES),
            shape(SUBSTEPS, rows, LANES),
        ),
        in_specs=[vmem] * 3 + [far] * 2, out_specs=[vmem] * 7,
        scratch_shapes=[
            pltpu.VMEM((1, species), f32),
            pltpu.VMEM((LANES, LANES), f32),
            pltpu.SemaphoreType.DMA((2,)),
        ],
        cost_estimate=pl.CostEstimate(flops=10**9, transcendentals=0, bytes_accessed=2 * 10**6),
        compiler_params=params, name="tables",
    )(
        stoich, rate.reshape(1, reactions), jnp.swapaxes(plan, 1, 2),
        pinned(night_loss.reshape(1, species)), pinned(sun),
    )

    to_north, to_south = pl.pallas_call(
        corner_kernel, out_shape=(ends, ends),
        in_specs=[vmem] * 2 + [hbm] * 3, out_specs=[hbm] * 2,
        scratch_shapes=[pltpu.VMEM((2, 8, species), f32), pltpu.SemaphoreType.DMA((2,))],
        input_output_aliases={2: 0, 3: 1},
        compiler_params=params, name="corners",
    )(of_pair, of_other, to_north, to_south, tables[5])
    of_south = lax.ppermute(to_north, "lat", north)
    of_north = lax.ppermute(to_south, "lat", south)

    shared = (conc, wind_lon, wind_lat, mixing, of_pair, of_other, own)
    scratch = [pltpu.VMEM((rows // 2, species, cells), f32), pltpu.SemaphoreType.DMA((rows // 4,))]
    inner = pl.pallas_call(
        inner_kernel, out_shape=jax.ShapeDtypeStruct(conc.shape, f32),
        in_specs=[vmem] * 14, out_specs=hbm, scratch_shapes=scratch,
        compiler_params=params, name="inner",
    )(*shared, *tables)
    return pl.pallas_call(
        outer_kernel, out_shape=jax.ShapeDtypeStruct(conc.shape, f32),
        in_specs=[vmem] * 16 + [hbm], out_specs=hbm, scratch_shapes=scratch,
        input_output_aliases={16: 0},
        compiler_params=params, name="outer",
    )(*shared, of_south, of_north, *tables, inner)


def solution(mesh):
    field = P("lat", None, "lon")
    cell = P("lat", "lon")
    return jax.shard_map(
        local,
        mesh=mesh,
        in_specs=(field, cell, cell, cell, P(), P(), P(), P(), P()),
        out_specs=field,
        check_vma=False,
    )
```

```python
import jax
import jax.numpy as jnp
from jax import lax
from jax.experimental import pallas as pl
from jax.experimental.pallas import tpu as pltpu
from jax.sharding import PartitionSpec as P

SUBSTEPS = 2
PICARD = 3
PHOT = 128
LANES = 128
VMEM_LIMIT = 48 << 20
KEPT = jax.ShapeDtypeStruct
CHUNK = 256
STAGGER = 2

f32 = jnp.float32
bf16 = jnp.bfloat16


def split(x):
    high = x.astype(bf16)
    return high, (x - high.astype(f32)).astype(bf16)


def twice(x):
    return jnp.concatenate([x, x], axis=1)


def dot(a, b):
    return jnp.dot(a, b, preferred_element_type=f32)


def iota(shape, axis):
    return lax.broadcasted_iota(jnp.int32, shape, axis)


def edge_kernel(
    conc_in, wlon_in, wlat_in, mix_in, to_pair, to_other, own, to_north, to_south, conc, coefs,
    winds, columns, sem,
):
    rows, species, cells = conc.shape
    fetches = [
        pltpu.make_async_copy(ref, winds.at[k], sem.at[k])
        for k, ref in enumerate((wlon_in, wlat_in, mix_in))
    ]
    fetches.append(pltpu.make_async_copy(conc_in, conc, sem.at[3]))
    for fetch in fetches:
        fetch.start()
    for fetch in fetches[:3]:
        fetch.wait()
    wlon, wlat, mix = [winds[k] for k in range(3)]
    place = iota((rows, cells), 1)
    stay = 1.0 - wlon - wlat - 4.0 * mix
    west, south = wlon + mix, wlat + mix
    coefs[0] = stay
    coefs[1] = jnp.where(place == 0, 0.0, west)
    coefs[2] = south
    coefs[3] = jnp.where(place == cells - 1, 0.0, mix)
    coefs[4] = mix
    coefs[5] = jnp.where(place == 0, west, jnp.where(place == cells - 1, mix, 0.0))
    even = lax.rem(lax.axis_index("lon"), 2) == 0

    def put(k, right, left):
        to_pair[k] = jnp.where(even, right, left)
        to_other[k] = jnp.where(even, left, right)

    for k, ref in enumerate((stay, west, south, mix)):
        put(
            2 + k,
            jnp.broadcast_to(ref[:, cells - 1 : cells], (rows, species)),
            jnp.broadcast_to(ref[:, 0:1], (rows, species)),
        )
    base = 2 * species
    pad = jnp.zeros((2, cells), f32)
    for ref, g in ((to_north, rows - 1), (to_south, 0)):
        ref[base : base + 8, :] = jnp.concatenate([coefs[k, g : g + 1] for k in range(6)] + [pad])
    fetches[3].wait()
    lane = iota((species, cells), 1)
    picked = jnp.zeros((species, cells), f32)
    for g in range(rows):
        turned = pltpu.roll(conc[g], (4 * g + 2) % cells, 1)
        picked = jnp.where((lane >= 4 * g) & (lane < 4 * g + 4), turned, picked)
    columns[...] = picked.T
    last2, last1, first1, first2 = [columns[pl.ds(q, rows, stride=4), :] for q in range(4)]
    put(0, last1, first1)
    put(1, last2, first2)
    own[0] = first1
    own[1] = last1
    for q in range(2):
        to_north[q * species : (q + 1) * species, :] = conc[rows - 2 + q]
        to_south[q * species : (q + 1) * species, :] = conc[q]


def sides(of_pair, of_other):
    even = lax.rem(lax.axis_index("lon"), 2) == 0
    return (
        lambda k: jnp.where(even, of_other[k], of_pair[k]),
        lambda k: jnp.where(even, of_pair[k], of_other[k]),
    )


def corner_kernel(of_pair, of_other, _, __, ___, to_north, to_south, ends, sem):
    rows = of_pair.shape[1]
    left, right = sides(of_pair, of_other)
    near_l, near_r = left(0), right(0)
    pad = jnp.zeros((6, near_l.shape[1]), f32)
    copies = []
    for p, (g, ref) in enumerate(((rows - 1, to_north), (0, to_south))):
        ends[p] = jnp.concatenate([near_l[g : g + 1], near_r[g : g + 1], pad], axis=0)
        dest = ref.at[pl.ds(ref.shape[0] - 8, 8), :]
        copies.append(pltpu.make_async_copy(ends.at[p], dest, sem.at[p]))
        copies[p].start()
    for c in copies:
        c.wait()


def table_kernel(
    conc, coefs, stoich_in, rate_in, plan_in, night_in, sun, once, gather, products, losses, speeds, decay, sun_own, lit,
    stoich, rate, plan, night, turned, sem,
):
    species = decay.shape[0]
    reactions = stoich_in.shape[1]
    rows = sun_own.shape[0]
    chunks = reactions // LANES
    band = lax.axis_index("lat")
    sector = lax.axis_index("lon")
    here = sun.at[
        pl.ds(pl.multiple_of(band * rows, 8), rows),
        pl.ds(pl.multiple_of(sector * LANES, LANES), LANES),
    ]
    moves = (
        (here, sun_own), (stoich_in, stoich), (rate_in, rate), (plan_in, plan), (night_in, night)
    )
    fetches = [pltpu.make_async_copy(a, b, sem.at[k]) for k, (a, b) in enumerate(moves)]
    for fetch in fetches:
        fetch.start()
    for g in range(rows):
        row = inner_step(conc[g], coefs, g)
        if g > 0:
            row = row + coefs[2, g : g + 1, :] * conc[g - 1]
        if g < rows - 1:
            row = row + coefs[4, g : g + 1, :] * conc[g + 1]
        once[g] = row
    for fetch in fetches:
        fetch.wait()
    down = iota((species, LANES), 0)
    across = iota((LANES, species), 1).astype(f32)
    mats = []
    for k in range(chunks):
        cols = pl.ds(k * LANES, LANES)
        codes = stoich[:, cols]
        row = rate[0:1, cols]
        small = jnp.concatenate([codes.astype(f32), row, jnp.zeros((3, LANES), f32)], axis=0).T
        hot = [(codes[q : q + 1, :] == down).astype(f32) for q in range(4)]
        seconds = None
        for q in range(2):
            picks = (small[:, q : q + 1] == across).astype(f32).astype(bf16)
            gather[pl.ds(q * reactions + k * LANES, LANES), :] = twice(picks)
            seconds = picks
        products[:, 2 * k * LANES : (2 * k + 2) * LANES] = twice((hot[2] + hot[3]).astype(bf16))
        speeds[pl.ds(k * LANES, LANES), :] = jnp.broadcast_to(small[:, 4:5], (LANES, LANES))
        parts = jnp.concatenate(split(hot[0] * row), axis=0)
        both = dot(parts, seconds)
        mats.append(both[:species] + both[species:])
    photo = sum(mats[1 : PHOT // LANES], mats[0])
    dark = sum(mats[PHOT // LANES + 1 :], mats[PHOT // LANES])
    for q, mat in enumerate((dark, photo)):
        high, low = split(mat + mat.T)
        losses[:, 2 * q * species : 2 * (q + 1) * species] = twice(high)
        losses[:, (4 + q) * species : (5 + q) * species] = low
    strip = []
    for s in range(SUBSTEPS):
        codes = plan[s]
        own = jnp.where(iota(codes.shape, 0) == sector, codes, 0).astype(f32)
        strip.append(jnp.sum(own, axis=0, keepdims=True))
    lats = plan.shape[2]
    flags = jnp.concatenate(strip + [jnp.zeros((8 - SUBSTEPS, lats), f32)], axis=0)
    flags = jnp.concatenate([flags, jnp.zeros((8, LANES - lats), f32)], axis=1)
    fade = jnp.exp(-night[...])
    spread = jnp.concatenate([flags, fade, jnp.zeros((7, LANES), f32)], axis=0).T
    decay[...] = jnp.broadcast_to(spread[:, 8:9], (species, LANES))
    for s in range(SUBSTEPS):
        turned[...] = jnp.broadcast_to(spread[:, s : s + 1], turned.shape)
        mine = turned[pl.ds(pl.multiple_of(band * rows, 8), rows), :]
        lit[s] = (mine >= -1.0).astype(f32)


def pair_steps(field, low, store, decay, sun, lit, gather, products, losses, speeds):
    reactions, species = speeds.shape[0], decay.shape[0]

    def both(ref):
        return jnp.concatenate([ref[low : low + 1, :], ref[low + 1 : low + 2, :]], axis=1)

    def begin(d):
        d["start"] = d["now"] = jnp.concatenate([field(low), field(low + 1)], axis=1)

    def prepare(d):
        photo = both(sun)
        high, low_part = split(d["now"])
        sun_high, sun_low = split(d["now"] * photo)
        d["weights"] = jnp.concatenate([high, low_part], axis=0)
        d["all"] = jnp.concatenate([high, low_part, sun_high, sun_low, high, sun_high], axis=0)
        d["made"] = []

    def lose(d):
        d["lost"] = dot(losses[...], d["all"])

    def react(k):
        def run(d):
            rows = slice(k * CHUNK, (k + 1) * CHUNK)
            later = slice(reactions + k * CHUNK, reactions + (k + 1) * CHUNK)
            first, second = dot(gather[rows, :], d["weights"]), dot(gather[later, :], d["weights"])
            for q in range(CHUNK // LANES):
                part = slice(q * LANES, (q + 1) * LANES)
                base = k * CHUNK + q * LANES
                flow = first[part] * twice(speeds[base : base + LANES, :]) * second[part]
                if base < PHOT:
                    flow = flow * both(sun)
                d["made"].extend(split(flow))

        return run

    def produce(d):
        d["produced"] = dot(products[...], jnp.concatenate(d["made"], axis=0))

    def close(s, last):
        def run(d):
            d["now"] = (d["start"] + d["produced"]) / (1.0 + d["lost"])
            if last:
                dark = d["start"] * twice(decay[...])
                d["now"] = d["start"] = jnp.where(both(lit.at[s]) > 0.0, d["now"], dark)

        return run

    steps = [begin]
    for s in range(SUBSTEPS):
        for sweep in range(PICARD):
            steps += [prepare, react(0), lose]
            steps += [react(k) for k in range(1, reactions // CHUNK)]
            steps += [produce, close(s, sweep == PICARD - 1)]
    steps.append(lambda d: store(low, d["now"]))
    return steps


def chemistry(lows, field, store, *refs):
    lists = [pair_steps(field, low, store, *refs) for low in lows]
    state = [{} for _ in lows]
    for t in range(len(lists[0]) + STAGGER * (len(lows) - 1)):
        for p, steps in enumerate(lists):
            at = t - STAGGER * p
            if 0 <= at < len(steps):
                steps[at](state[p])


def inner_step(center, coefs, g):
    cells = center.shape[1]
    stay, west, _, east = [coefs[k, g : g + 1, :] for k in range(4)]
    return stay * center + west * pltpu.roll(center, 1, 1) + east * pltpu.roll(center, cells - 1, 1)


def side_columns(of_pair, of_other, own, corners, columns):
    rows = of_pair.shape[1]
    left, right = sides(of_pair, of_other)
    near_l, near_r = left(0), right(0)
    zero = jnp.zeros((1, near_l.shape[1]), f32)
    sl, sr, nl, nr = corners if corners else (zero, zero, zero, zero)

    def moved(near, west, east, south, north, side):
        south = jnp.concatenate([south, near[:-1]], axis=0)
        north = jnp.concatenate([near[1:], north], axis=0)
        return side(2) * near + side(3) * west + side(4) * south + side(5) * (east + north)

    columns[...] = jnp.zeros_like(columns)
    columns[pl.ds(0, rows, stride=2), :] = near_r
    columns[pl.ds(1, rows, stride=2), :] = near_l
    columns[pl.ds(2 * rows, rows, stride=2), :] = moved(near_r, own[1], right(1), sr, nr, right)
    columns[pl.ds(2 * rows + 1, rows, stride=2), :] = moved(near_l, left(1), own[0], sl, nl, left)
    for k, row in enumerate((sr, sl, nr, nl)):
        columns[4 * rows + k : 4 * rows + k + 1, :] = row
    return columns[...].T


def mover(first, coefs, turned, rows):
    def beside(i):
        return pltpu.roll(turned, LANES - 2 * i - 1, 1)

    known = {}

    def once(g):
        if g not in known:
            i = 2 * rows if g < 0 else 2 * rows + 1 if g >= rows else g
            row, side = first(g)
            known[g] = row + side * beside(i)
        return known[g]

    def moved(g):
        row = inner_step(once(g), coefs, g) + coefs[2, g : g + 1, :] * once(g - 1)
        row = row + coefs[4, g : g + 1, :] * once(g + 1)
        return row + coefs[5, g : g + 1, :] * beside(rows + g)

    return moved


def storer(lows, out, stage, sem):
    copies = []

    def store(low, pair):
        p = lows.index(low)
        stage[2 * p] = pair[:, :LANES]
        stage[2 * p + 1] = pair[:, LANES:]
        copies.append(
            pltpu.make_async_copy(stage.at[pl.ds(2 * p, 2)], out.at[pl.ds(low, 2)], sem.at[p])
        )
        copies[-1].start()

    return store, copies


def finish(lows, moved, refs, out, stage, sem):
    store, copies = storer(lows, out, stage, sem)
    chemistry(lows, moved, store, *refs)
    for c in copies:
        c.wait()


def inner_kernel(
    once, coefs, of_pair, of_other, own,
    gather, products, losses, speeds, decay, sun, lit, out, stage, columns, sem,
):
    rows = once.shape[0]
    turned = side_columns(of_pair, of_other, own, None, columns)
    lows = list(range(rows // 4, rows - rows // 4, 2))
    moved = mover(lambda g: (once[g], coefs[5, g : g + 1, :]), coefs, turned, rows)
    finish(lows, moved, (decay, sun, lit, gather, products, losses, speeds), out, stage, sem)


def outer_kernel(
    once, coefs, of_pair, of_other, own, conc, of_south, of_north,
    gather, products, losses, speeds, decay, sun, lit, _, out, stage, columns, sem,
):
    rows, species, cells = conc.shape
    base = 2 * species
    band = lax.axis_index("lat")
    below = jnp.where(band > 0, 1.0, 0.0)
    above = jnp.where(band < lax.axis_size("lat") - 1, 1.0, 0.0)
    corners = [
        r[base + 8 + k : base + 9 + k, :] * inside
        for r, inside in ((of_south, below), (of_north, above))
        for k in range(2)
    ]
    turned = side_columns(of_pair, of_other, own, corners, columns)

    def halo(ref, q, inside):
        return ref[q * species : (q + 1) * species, :] * inside

    def across(ref, k, inside):
        return ref[base + k : base + k + 1, :] * inside

    def outside(ref, near, far, beyond, home, back, inside):
        center = halo(ref, near, inside)
        stay, west, east = [across(ref, k, inside) for k in (0, 1, 3)]
        row = stay * center + west * pltpu.roll(center, 1, 1)
        row = row + east * pltpu.roll(center, cells - 1, 1)
        row = row + across(ref, beyond, inside) * halo(ref, far, inside)
        return row + across(ref, back, inside) * home, across(ref, 5, inside)

    def first(g):
        if g < 0:
            return outside(of_south, 1, 0, 2, conc[0], 4, below)
        if g >= rows:
            return outside(of_north, 0, 1, 4, conc[rows - 1], 2, above)
        row, side = once[g], coefs[5, g : g + 1, :]
        if g == 0:
            row = row + coefs[2, g : g + 1, :] * halo(of_south, 1, below)
        if g == rows - 1:
            row = row + coefs[4, g : g + 1, :] * halo(of_north, 0, above)
        return row, side

    lows = list(range(0, rows // 4, 2)) + list(range(rows - rows // 4, rows, 2))
    moved = mover(first, coefs, turned, rows)
    finish(lows, moved, (decay, sun, lit, gather, products, losses, speeds), out, stage, sem)


def local(conc, wind_lon, wind_lat, mixing, sun, rate, night_loss, stoich, plan):
    rows, species, cells = conc.shape
    reactions = rate.shape[0]
    lons = lax.axis_size("lon")
    lats = lax.axis_size("lat")
    params = pltpu.CompilerParams(vmem_limit_bytes=VMEM_LIMIT)
    vmem = pl.BlockSpec(memory_space=pltpu.VMEM)
    hbm = pl.BlockSpec(memory_space=pl.ANY)
    far = pl.BlockSpec(memory_space=pltpu.HBM)

    def pinned(x):
        return pltpu.with_memory_space_constraint(x, pltpu.HBM)

    def shape(*dims, dtype=f32):
        return KEPT(dims, dtype)

    side = shape(6, rows, species)
    ends = shape(2 * species + 16, cells)
    to_pair, to_other, own, to_north, to_south, held, coefs = pl.pallas_call(
        edge_kernel,
        out_shape=(
            side, side, shape(2, rows, species), ends, ends,
            shape(rows, species, cells), shape(6, rows, cells),
        ),
        in_specs=[far] * 4, out_specs=[vmem] * 7,
        scratch_shapes=[
            pltpu.VMEM((3, rows, cells), f32),
            pltpu.VMEM((cells, species), f32),
            pltpu.SemaphoreType.DMA((4,)),
        ],
        compiler_params=params, name="edges",
    )(*[pinned(x) for x in (conc, wind_lon, wind_lat, mixing)])

    pair = [(i, i ^ 1) for i in range(lons)]
    other = [(i, (i - 1) % lons if i % 2 == 0 else (i + 1) % lons) for i in range(lons)]
    north = [(i, (i + 1) % lats) for i in range(lats)]
    south = [(j, i) for i, j in north]
    of_pair = lax.ppermute(to_pair, "lon", pair)
    of_other = lax.ppermute(to_other, "lon", other)

    once, *tables = pl.pallas_call(
        table_kernel,
        out_shape=(
            shape(rows, species, cells),
            shape(2 * reactions, 2 * species, dtype=bf16),
            shape(species, 2 * reactions, dtype=bf16),
            shape(species, 6 * species, dtype=bf16),
            shape(reactions, LANES),
            shape(species, LANES),
            shape(rows, LANES),
            shape(SUBSTEPS, rows, LANES),
        ),
        in_specs=[vmem] * 2 + [far] * 5, out_specs=[vmem] * 8,
        scratch_shapes=[
            pltpu.VMEM(stoich.shape, jnp.int32),
            pltpu.VMEM((1, reactions), f32),
            pltpu.VMEM((plan.shape[0], plan.shape[2], plan.shape[1]), jnp.int32),
            pltpu.VMEM((1, species), f32),
            pltpu.VMEM((LANES, LANES), f32),
            pltpu.SemaphoreType.DMA((5,)),
        ],
        cost_estimate=pl.CostEstimate(flops=10**9, transcendentals=0, bytes_accessed=2 * 10**6),
        compiler_params=params, name="tables",
    )(
        held, coefs, pinned(stoich), pinned(rate.reshape(1, reactions)),
        pinned(jnp.swapaxes(plan, 1, 2)), pinned(night_loss.reshape(1, species)), pinned(sun),
    )

    to_north, to_south = pl.pallas_call(
        corner_kernel, out_shape=(ends, ends),
        in_specs=[vmem] * 2 + [hbm] * 3, out_specs=[hbm] * 2,
        scratch_shapes=[pltpu.VMEM((2, 8, species), f32), pltpu.SemaphoreType.DMA((2,))],
        input_output_aliases={2: 0, 3: 1},
        compiler_params=params, name="corners",
    )(of_pair, of_other, to_north, to_south, tables[5])
    of_south = lax.ppermute(to_north, "lat", north)
    of_north = lax.ppermute(to_south, "lat", south)

    shared = (once, coefs, of_pair, of_other, own)
    scratch = [
        pltpu.VMEM((rows // 2, species, cells), f32),
        pltpu.VMEM((LANES, species), f32),
        pltpu.SemaphoreType.DMA((rows // 4,)),
    ]
    inner = pl.pallas_call(
        inner_kernel, out_shape=jax.ShapeDtypeStruct(conc.shape, f32),
        in_specs=[vmem] * 12, out_specs=hbm, scratch_shapes=scratch,
        compiler_params=params, name="inner",
    )(*shared, *tables)
    return pl.pallas_call(
        outer_kernel, out_shape=jax.ShapeDtypeStruct(conc.shape, f32),
        in_specs=[vmem] * 15 + [hbm], out_specs=hbm, scratch_shapes=scratch,
        input_output_aliases={15: 0},
        compiler_params=params, name="outer",
    )(*shared, held, of_south, of_north, *tables, inner)


def solution(mesh):
    field = P("lat", None, "lon")
    cell = P("lat", "lon")
    return jax.shard_map(
        local,
        mesh=mesh,
        in_specs=(field, cell, cell, cell, P(), P(), P(), P(), P()),
        out_specs=field,
        check_vma=False,
    )
```

```python
import jax
import jax.numpy as jnp
from jax import lax
from jax.experimental import pallas as pl
from jax.experimental.pallas import tpu as pltpu
from jax.sharding import PartitionSpec as P

SUBSTEPS = 2
PICARD = 3
PHOT = 128
LANES = 128
VMEM_LIMIT = 48 << 20
KEPT = jax.ShapeDtypeStruct
CHUNK = 256
STAGGER = 2

f32 = jnp.float32
bf16 = jnp.bfloat16


def split(x):
    high = x.astype(bf16)
    return high, (x - high.astype(f32)).astype(bf16)


def twice(x):
    return jnp.concatenate([x, x], axis=1)


def dot(a, b):
    return jnp.dot(a, b, preferred_element_type=f32)


def iota(shape, axis):
    return lax.broadcasted_iota(jnp.int32, shape, axis)


def edge_kernel(
    conc_in, wlon_in, wlat_in, mix_in, to_pair, to_other, own, to_near, to_next, conc, coefs,
    winds, columns, sem,
):
    rows, species, cells = conc.shape
    fetches = [
        pltpu.make_async_copy(ref, winds.at[k], sem.at[k])
        for k, ref in enumerate((wlon_in, wlat_in, mix_in))
    ]
    fetches.append(pltpu.make_async_copy(conc_in, conc, sem.at[3]))
    for fetch in fetches:
        fetch.start()
    for fetch in fetches[:3]:
        fetch.wait()
    wlon, wlat, mix = [winds[k] for k in range(3)]
    place = iota((rows, cells), 1)
    stay = 1.0 - wlon - wlat - 4.0 * mix
    west, south = wlon + mix, wlat + mix
    coefs[0] = stay
    coefs[1] = jnp.where(place == 0, 0.0, west)
    coefs[2] = south
    coefs[3] = jnp.where(place == cells - 1, 0.0, mix)
    coefs[4] = mix
    coefs[5] = jnp.where(place == 0, west, jnp.where(place == cells - 1, mix, 0.0))
    even = lax.rem(lax.axis_index("lon"), 2) == 0

    def put(k, right, left):
        to_pair[k] = jnp.where(even, right, left)
        to_other[k] = jnp.where(even, left, right)

    for k, ref in enumerate((stay, west, south, mix)):
        put(
            2 + k,
            jnp.broadcast_to(ref[:, cells - 1 : cells], (rows, species)),
            jnp.broadcast_to(ref[:, 0:1], (rows, species)),
        )
    base = 2 * species
    pad = jnp.zeros((2, cells), f32)
    even_band = lax.rem(lax.axis_index("lat"), 2) == 0

    def send(span, north, south):
        to_near[span, :] = jnp.where(even_band, north, south)
        to_next[span, :] = jnp.where(even_band, south, north)

    send(
        slice(base, base + 8),
        *[
            jnp.concatenate([coefs[k, g : g + 1] for k in range(6)] + [pad])
            for g in (rows - 1, 0)
        ],
    )
    fetches[3].wait()
    lane = iota((species, cells), 1)
    picked = jnp.zeros((species, cells), f32)
    for g in range(rows):
        turned = pltpu.roll(conc[g], (4 * g + 2) % cells, 1)
        picked = jnp.where((lane >= 4 * g) & (lane < 4 * g + 4), turned, picked)
    columns[...] = picked.T
    last2, last1, first1, first2 = [columns[pl.ds(q, rows, stride=4), :] for q in range(4)]
    put(0, last1, first1)
    put(1, last2, first2)
    own[0] = first1
    own[1] = last1
    for q in range(2):
        send(slice(q * species, (q + 1) * species), conc[rows - 2 + q], conc[q])


def sides(of_pair, of_other):
    even = lax.rem(lax.axis_index("lon"), 2) == 0
    return (
        lambda k: jnp.where(even, of_other[k], of_pair[k]),
        lambda k: jnp.where(even, of_pair[k], of_other[k]),
    )


def corner_kernel(of_pair, of_other, _, __, ___, to_near, to_next, ends, sem):
    rows = of_pair.shape[1]
    left, right = sides(of_pair, of_other)
    near_l, near_r = left(0), right(0)
    pad = jnp.zeros((6, near_l.shape[1]), f32)
    north, south = [
        jnp.concatenate([near_l[g : g + 1], near_r[g : g + 1], pad], axis=0) for g in (rows - 1, 0)
    ]
    even_band = lax.rem(lax.axis_index("lat"), 2) == 0
    ends[0] = jnp.where(even_band, north, south)
    ends[1] = jnp.where(even_band, south, north)
    copies = []
    for p, ref in enumerate((to_near, to_next)):
        dest = ref.at[pl.ds(ref.shape[0] - 8, 8), :]
        copies.append(pltpu.make_async_copy(ends.at[p], dest, sem.at[p]))
        copies[p].start()
    for c in copies:
        c.wait()


def table_kernel(
    conc, coefs, stoich_in, rate_in, plan_in, night_in, sun, once, gather, products, losses, speeds, decay, sun_own, lit,
    stoich, rate, plan, night, turned, sem,
):
    species = decay.shape[0]
    reactions = stoich_in.shape[1]
    rows = sun_own.shape[0]
    chunks = reactions // LANES
    band = lax.axis_index("lat")
    sector = lax.axis_index("lon")
    here = sun.at[
        pl.ds(pl.multiple_of(band * rows, 8), rows),
        pl.ds(pl.multiple_of(sector * LANES, LANES), LANES),
    ]
    moves = (
        (here, sun_own), (stoich_in, stoich), (rate_in, rate), (plan_in, plan), (night_in, night)
    )
    fetches = [pltpu.make_async_copy(a, b, sem.at[k]) for k, (a, b) in enumerate(moves)]
    for fetch in fetches:
        fetch.start()
    for g in range(rows):
        row = inner_step(conc[g], coefs, g)
        if g > 0:
            row = row + coefs[2, g : g + 1, :] * conc[g - 1]
        if g < rows - 1:
            row = row + coefs[4, g : g + 1, :] * conc[g + 1]
        once[g] = row
    for fetch in fetches:
        fetch.wait()
    down = iota((species, LANES), 0)
    across = iota((LANES, species), 1).astype(f32)
    mats = []
    for k in range(chunks):
        cols = pl.ds(k * LANES, LANES)
        codes = stoich[:, cols]
        row = rate[0:1, cols]
        small = jnp.concatenate([codes.astype(f32), row, jnp.zeros((3, LANES), f32)], axis=0).T
        hot = [(codes[q : q + 1, :] == down).astype(f32) for q in range(4)]
        seconds = None
        for q in range(2):
            picks = (small[:, q : q + 1] == across).astype(f32).astype(bf16)
            gather[pl.ds(q * reactions + k * LANES, LANES), :] = twice(picks)
            seconds = picks
        products[:, 2 * k * LANES : (2 * k + 2) * LANES] = twice((hot[2] + hot[3]).astype(bf16))
        speeds[pl.ds(k * LANES, LANES), :] = jnp.broadcast_to(small[:, 4:5], (LANES, LANES))
        parts = jnp.concatenate(split(hot[0] * row), axis=0)
        both = dot(parts, seconds)
        mats.append(both[:species] + both[species:])
    photo = sum(mats[1 : PHOT // LANES], mats[0])
    dark = sum(mats[PHOT // LANES + 1 :], mats[PHOT // LANES])
    for q, mat in enumerate((dark, photo)):
        high, low = split(mat + mat.T)
        losses[:, 2 * q * species : 2 * (q + 1) * species] = twice(high)
        losses[:, (4 + q) * species : (5 + q) * species] = low
    strip = []
    for s in range(SUBSTEPS):
        codes = plan[s]
        own = jnp.where(iota(codes.shape, 0) == sector, codes, 0).astype(f32)
        strip.append(jnp.sum(own, axis=0, keepdims=True))
    lats = plan.shape[2]
    flags = jnp.concatenate(strip + [jnp.zeros((8 - SUBSTEPS, lats), f32)], axis=0)
    flags = jnp.concatenate([flags, jnp.zeros((8, LANES - lats), f32)], axis=1)
    fade = jnp.exp(-night[...])
    spread = jnp.concatenate([flags, fade, jnp.zeros((7, LANES), f32)], axis=0).T
    decay[...] = jnp.broadcast_to(spread[:, 8:9], (species, LANES))
    for s in range(SUBSTEPS):
        turned[...] = jnp.broadcast_to(spread[:, s : s + 1], turned.shape)
        mine = turned[pl.ds(pl.multiple_of(band * rows, 8), rows), :]
        lit[s] = (mine >= -1.0).astype(f32)


def pair_steps(field, low, store, decay, sun, lit, gather, products, losses, speeds):
    reactions, species = speeds.shape[0], decay.shape[0]

    def both(ref):
        return jnp.concatenate([ref[low : low + 1, :], ref[low + 1 : low + 2, :]], axis=1)

    def begin(d):
        d["start"] = d["now"] = jnp.concatenate([field(low), field(low + 1)], axis=1)

    def prepare(d):
        photo = both(sun)
        high, low_part = split(d["now"])
        sun_high, sun_low = split(d["now"] * photo)
        d["weights"] = jnp.concatenate([high, low_part], axis=0)
        d["all"] = jnp.concatenate([high, low_part, sun_high, sun_low, high, sun_high], axis=0)
        d["made"] = []

    def lose(d):
        d["lost"] = dot(losses[...], d["all"])

    def react(k):
        def run(d):
            rows = slice(k * CHUNK, (k + 1) * CHUNK)
            later = slice(reactions + k * CHUNK, reactions + (k + 1) * CHUNK)
            first, second = dot(gather[rows, :], d["weights"]), dot(gather[later, :], d["weights"])
            for q in range(CHUNK // LANES):
                part = slice(q * LANES, (q + 1) * LANES)
                base = k * CHUNK + q * LANES
                flow = first[part] * twice(speeds[base : base + LANES, :]) * second[part]
                if base < PHOT:
                    flow = flow * both(sun)
                d["made"].extend(split(flow))

        return run

    def produce(d):
        d["produced"] = dot(products[...], jnp.concatenate(d["made"], axis=0))

    def close(s, last):
        def run(d):
            d["now"] = (d["start"] + d["produced"]) / (1.0 + d["lost"])
            if last:
                dark = d["start"] * twice(decay[...])
                d["now"] = d["start"] = jnp.where(both(lit.at[s]) > 0.0, d["now"], dark)

        return run

    steps = [begin]
    for s in range(SUBSTEPS):
        for sweep in range(PICARD):
            steps += [prepare, react(0), lose]
            steps += [react(k) for k in range(1, reactions // CHUNK)]
            steps += [produce, close(s, sweep == PICARD - 1)]
    steps.append(lambda d: store(low, d["now"]))
    return steps


def chemistry(lows, field, store, *refs):
    lists = [pair_steps(field, low, store, *refs) for low in lows]
    state = [{} for _ in lows]
    for t in range(len(lists[0]) + STAGGER * (len(lows) - 1)):
        for p, steps in enumerate(lists):
            at = t - STAGGER * p
            if 0 <= at < len(steps):
                steps[at](state[p])


def inner_step(center, coefs, g):
    cells = center.shape[1]
    stay, west, _, east = [coefs[k, g : g + 1, :] for k in range(4)]
    return stay * center + west * pltpu.roll(center, 1, 1) + east * pltpu.roll(center, cells - 1, 1)


def side_columns(of_pair, of_other, own, corners, columns):
    rows = of_pair.shape[1]
    left, right = sides(of_pair, of_other)
    near_l, near_r = left(0), right(0)
    zero = jnp.zeros((1, near_l.shape[1]), f32)
    sl, sr, nl, nr = corners if corners else (zero, zero, zero, zero)

    def moved(near, west, east, south, north, side):
        south = jnp.concatenate([south, near[:-1]], axis=0)
        north = jnp.concatenate([near[1:], north], axis=0)
        return side(2) * near + side(3) * west + side(4) * south + side(5) * (east + north)

    columns[...] = jnp.zeros_like(columns)
    columns[pl.ds(0, rows, stride=2), :] = near_r
    columns[pl.ds(1, rows, stride=2), :] = near_l
    columns[pl.ds(2 * rows, rows, stride=2), :] = moved(near_r, own[1], right(1), sr, nr, right)
    columns[pl.ds(2 * rows + 1, rows, stride=2), :] = moved(near_l, left(1), own[0], sl, nl, left)
    for k, row in enumerate((sr, sl, nr, nl)):
        columns[4 * rows + k : 4 * rows + k + 1, :] = row
    return columns[...].T


def mover(first, coefs, turned, rows):
    def beside(i):
        return pltpu.roll(turned, LANES - 2 * i - 1, 1)

    known = {}

    def once(g):
        if g not in known:
            i = 2 * rows if g < 0 else 2 * rows + 1 if g >= rows else g
            row, side = first(g)
            known[g] = row + side * beside(i)
        return known[g]

    def moved(g):
        row = inner_step(once(g), coefs, g) + coefs[2, g : g + 1, :] * once(g - 1)
        row = row + coefs[4, g : g + 1, :] * once(g + 1)
        return row + coefs[5, g : g + 1, :] * beside(rows + g)

    return moved


def storer(lows, out, stage, sem):
    copies = []

    def store(low, pair):
        p = lows.index(low)
        stage[2 * p] = pair[:, :LANES]
        stage[2 * p + 1] = pair[:, LANES:]
        copies.append(
            pltpu.make_async_copy(stage.at[pl.ds(2 * p, 2)], out.at[pl.ds(low, 2)], sem.at[p])
        )
        copies[-1].start()

    return store, copies


def finish(lows, moved, refs, out, stage, sem):
    store, copies = storer(lows, out, stage, sem)
    chemistry(lows, moved, store, *refs)
    for c in copies:
        c.wait()


def inner_kernel(
    once, coefs, of_pair, of_other, own,
    gather, products, losses, speeds, decay, sun, lit, out, stage, columns, sem,
):
    rows = once.shape[0]
    turned = side_columns(of_pair, of_other, own, None, columns)
    lows = list(range(rows // 4, rows - rows // 4, 2))
    moved = mover(lambda g: (once[g], coefs[5, g : g + 1, :]), coefs, turned, rows)
    finish(lows, moved, (decay, sun, lit, gather, products, losses, speeds), out, stage, sem)


def outer_kernel(
    once, coefs, of_pair, of_other, own, conc, of_near, of_next,
    gather, products, losses, speeds, decay, sun, lit, _, out, stage, columns, sem,
):
    rows, species, cells = conc.shape
    base = 2 * species
    band = lax.axis_index("lat")
    below = jnp.where(band > 0, 1.0, 0.0)
    above = jnp.where(band < lax.axis_size("lat") - 1, 1.0, 0.0)
    even_band = lax.rem(band, 2) == 0

    def of_south(span):
        return jnp.where(even_band, of_next[span, :], of_near[span, :])

    def of_north(span):
        return jnp.where(even_band, of_near[span, :], of_next[span, :])

    corners = [
        got(slice(base + 8 + k, base + 9 + k)) * inside
        for got, inside in ((of_south, below), (of_north, above))
        for k in range(2)
    ]
    turned = side_columns(of_pair, of_other, own, corners, columns)

    def halo(got, q, inside):
        return got(slice(q * species, (q + 1) * species)) * inside

    def across(got, k, inside):
        return got(slice(base + k, base + k + 1)) * inside

    def outside(got, near, far, beyond, home, back, inside):
        center = halo(got, near, inside)
        stay, west, east = [across(got, k, inside) for k in (0, 1, 3)]
        row = stay * center + west * pltpu.roll(center, 1, 1)
        row = row + east * pltpu.roll(center, cells - 1, 1)
        row = row + across(got, beyond, inside) * halo(got, far, inside)
        return row + across(got, back, inside) * home, across(got, 5, inside)

    def first(g):
        if g < 0:
            return outside(of_south, 1, 0, 2, conc[0], 4, below)
        if g >= rows:
            return outside(of_north, 0, 1, 4, conc[rows - 1], 2, above)
        row, side = once[g], coefs[5, g : g + 1, :]
        if g == 0:
            row = row + coefs[2, g : g + 1, :] * halo(of_south, 1, below)
        if g == rows - 1:
            row = row + coefs[4, g : g + 1, :] * halo(of_north, 0, above)
        return row, side

    lows = list(range(0, rows // 4, 2)) + list(range(rows - rows // 4, rows, 2))
    moved = mover(first, coefs, turned, rows)
    finish(lows, moved, (decay, sun, lit, gather, products, losses, speeds), out, stage, sem)


def local(conc, wind_lon, wind_lat, mixing, sun, rate, night_loss, stoich, plan):
    rows, species, cells = conc.shape
    reactions = rate.shape[0]
    lons = lax.axis_size("lon")
    lats = lax.axis_size("lat")
    params = pltpu.CompilerParams(vmem_limit_bytes=VMEM_LIMIT)
    vmem = pl.BlockSpec(memory_space=pltpu.VMEM)
    hbm = pl.BlockSpec(memory_space=pl.ANY)
    far = pl.BlockSpec(memory_space=pltpu.HBM)

    def pinned(x):
        return pltpu.with_memory_space_constraint(x, pltpu.HBM)

    def shape(*dims, dtype=f32):
        return KEPT(dims, dtype)

    side = shape(6, rows, species)
    ends = shape(2 * species + 16, cells)
    to_pair, to_other, own, to_near, to_next, held, coefs = pl.pallas_call(
        edge_kernel,
        out_shape=(
            side, side, shape(2, rows, species), ends, ends,
            shape(rows, species, cells), shape(6, rows, cells),
        ),
        in_specs=[far] * 4, out_specs=[vmem] * 7,
        scratch_shapes=[
            pltpu.VMEM((3, rows, cells), f32),
            pltpu.VMEM((cells, species), f32),
            pltpu.SemaphoreType.DMA((4,)),
        ],
        compiler_params=params, name="edges",
    )(*[pinned(x) for x in (conc, wind_lon, wind_lat, mixing)])

    pair = [(i, i ^ 1) for i in range(lons)]
    other = [(i, (i - 1) % lons if i % 2 == 0 else (i + 1) % lons) for i in range(lons)]
    near = [(i, i ^ 1 if i ^ 1 < lats else i) for i in range(lats)]
    after = [i - 1 if i % 2 == 0 else i + 1 for i in range(lats)]
    after = [(i, j if 0 <= j < lats else i) for i, j in enumerate(after)]
    of_pair = lax.ppermute(to_pair, "lon", pair)
    of_other = lax.ppermute(to_other, "lon", other)

    once, *tables = pl.pallas_call(
        table_kernel,
        out_shape=(
            shape(rows, species, cells),
            shape(2 * reactions, 2 * species, dtype=bf16),
            shape(species, 2 * reactions, dtype=bf16),
            shape(species, 6 * species, dtype=bf16),
            shape(reactions, LANES),
            shape(species, LANES),
            shape(rows, LANES),
            shape(SUBSTEPS, rows, LANES),
        ),
        in_specs=[vmem] * 2 + [far] * 5, out_specs=[vmem] * 8,
        scratch_shapes=[
            pltpu.VMEM(stoich.shape, jnp.int32),
            pltpu.VMEM((1, reactions), f32),
            pltpu.VMEM((plan.shape[0], plan.shape[2], plan.shape[1]), jnp.int32),
            pltpu.VMEM((1, species), f32),
            pltpu.VMEM((LANES, LANES), f32),
            pltpu.SemaphoreType.DMA((5,)),
        ],
        cost_estimate=pl.CostEstimate(flops=10**9, transcendentals=0, bytes_accessed=2 * 10**6),
        compiler_params=params, name="tables",
    )(
        held, coefs, pinned(stoich), pinned(rate.reshape(1, reactions)),
        pinned(jnp.swapaxes(plan, 1, 2)), pinned(night_loss.reshape(1, species)), pinned(sun),
    )

    to_near, to_next = pl.pallas_call(
        corner_kernel, out_shape=(ends, ends),
        in_specs=[vmem] * 2 + [hbm] * 3, out_specs=[hbm] * 2,
        scratch_shapes=[pltpu.VMEM((2, 8, species), f32), pltpu.SemaphoreType.DMA((2,))],
        input_output_aliases={2: 0, 3: 1},
        compiler_params=params, name="corners",
    )(of_pair, of_other, to_near, to_next, tables[5])
    of_near = lax.ppermute(to_near, "lat", near)
    of_next = lax.ppermute(to_next, "lat", after)

    shared = (once, coefs, of_pair, of_other, own)
    scratch = [
        pltpu.VMEM((rows // 2, species, cells), f32),
        pltpu.VMEM((LANES, species), f32),
        pltpu.SemaphoreType.DMA((rows // 4,)),
    ]
    inner = pl.pallas_call(
        inner_kernel, out_shape=jax.ShapeDtypeStruct(conc.shape, f32),
        in_specs=[vmem] * 12, out_specs=hbm, scratch_shapes=scratch,
        compiler_params=params, name="inner",
    )(*shared, *tables)
    return pl.pallas_call(
        outer_kernel, out_shape=jax.ShapeDtypeStruct(conc.shape, f32),
        in_specs=[vmem] * 15 + [hbm], out_specs=hbm, scratch_shapes=scratch,
        input_output_aliases={15: 0},
        compiler_params=params, name="outer",
    )(*shared, held, of_near, of_next, *tables, inner)


def solution(mesh):
    field = P("lat", None, "lon")
    cell = P("lat", "lon")
    return jax.shard_map(
        local,
        mesh=mesh,
        in_specs=(field, cell, cell, cell, P(), P(), P(), P(), P()),
        out_specs=field,
        check_vma=False,
    )
```

```python
import jax
import jax.numpy as jnp
from jax import lax
from jax.experimental import pallas as pl
from jax.experimental.pallas import tpu as pltpu
from jax.sharding import PartitionSpec as P

SUBSTEPS = 2
PICARD = 3
PHOT = 128
LANES = 128
VMEM_LIMIT = 48 << 20
KEPT = jax.ShapeDtypeStruct
CHUNK = 256
STAGGER = 2

f32 = jnp.float32
bf16 = jnp.bfloat16


def split(x):
    high = x.astype(bf16)
    return high, (x - high.astype(f32)).astype(bf16)


def twice(x):
    return jnp.concatenate([x, x], axis=1)


def dot(a, b):
    return jnp.dot(a, b, preferred_element_type=f32)


def iota(shape, axis):
    return lax.broadcasted_iota(jnp.int32, shape, axis)


def edge_kernel(
    conc_in, wlon_in, wlat_in, mix_in, to_pair, to_other, own, to_near, to_next, conc, coefs,
    winds, columns, sem,
):
    rows, species, cells = conc.shape
    fetches = [
        pltpu.make_async_copy(ref, winds.at[k], sem.at[k])
        for k, ref in enumerate((wlon_in, wlat_in, mix_in))
    ]
    fetches.append(pltpu.make_async_copy(conc_in, conc, sem.at[3]))
    for fetch in fetches:
        fetch.start()
    for fetch in fetches[:3]:
        fetch.wait()
    wlon, wlat, mix = [winds[k] for k in range(3)]
    place = iota((rows, cells), 1)
    stay = 1.0 - wlon - wlat - 4.0 * mix
    west, south = wlon + mix, wlat + mix
    coefs[0] = stay
    coefs[1] = jnp.where(place == 0, 0.0, west)
    coefs[2] = south
    coefs[3] = jnp.where(place == cells - 1, 0.0, mix)
    coefs[4] = mix
    coefs[5] = jnp.where(place == 0, west, jnp.where(place == cells - 1, mix, 0.0))
    even = lax.rem(lax.axis_index("lon"), 2) == 0

    def put(k, right, left):
        to_pair[k] = jnp.where(even, right, left)
        to_other[k] = jnp.where(even, left, right)

    for k, ref in enumerate((stay, west, south, mix)):
        put(
            2 + k,
            jnp.broadcast_to(ref[:, cells - 1 : cells], (rows, species)),
            jnp.broadcast_to(ref[:, 0:1], (rows, species)),
        )
    base = 2 * species
    pad = jnp.zeros((2, cells), f32)
    even_band = lax.rem(lax.axis_index("lat"), 2) == 0

    def send(span, north, south):
        to_near[span, :] = jnp.where(even_band, north, south)
        to_next[span, :] = jnp.where(even_band, south, north)

    send(
        slice(base, base + 8),
        *[
            jnp.concatenate([coefs[k, g : g + 1] for k in range(6)] + [pad])
            for g in (rows - 1, 0)
        ],
    )
    fetches[3].wait()
    lane = iota((species, cells), 1)
    picked = jnp.zeros((species, cells), f32)
    for g in range(rows):
        turned = pltpu.roll(conc[g], (4 * g + 2) % cells, 1)
        picked = jnp.where((lane >= 4 * g) & (lane < 4 * g + 4), turned, picked)
    columns[...] = picked.T
    last2, last1, first1, first2 = [columns[pl.ds(q, rows, stride=4), :] for q in range(4)]
    put(0, last1, first1)
    put(1, last2, first2)
    own[0] = first1
    own[1] = last1
    for q in range(2):
        send(slice(q * species, (q + 1) * species), conc[rows - 2 + q], conc[q])


def sides(of_pair, of_other):
    even = lax.rem(lax.axis_index("lon"), 2) == 0
    return (
        lambda k: jnp.where(even, of_other[k], of_pair[k]),
        lambda k: jnp.where(even, of_pair[k], of_other[k]),
    )


def corner_kernel(of_pair, of_other, _, __, ___, to_near, to_next, ends, sem):
    rows = of_pair.shape[1]
    left, right = sides(of_pair, of_other)
    near_l, near_r = left(0), right(0)
    pad = jnp.zeros((6, near_l.shape[1]), f32)
    north, south = [
        jnp.concatenate([near_l[g : g + 1], near_r[g : g + 1], pad], axis=0) for g in (rows - 1, 0)
    ]
    even_band = lax.rem(lax.axis_index("lat"), 2) == 0
    ends[0] = jnp.where(even_band, north, south)
    ends[1] = jnp.where(even_band, south, north)
    copies = []
    for p, ref in enumerate((to_near, to_next)):
        dest = ref.at[pl.ds(ref.shape[0] - 8, 8), :]
        copies.append(pltpu.make_async_copy(ends.at[p], dest, sem.at[p]))
        copies[p].start()
    for c in copies:
        c.wait()


def table_kernel(
    conc, coefs, stoich_in, rate_in, plan_in, night_in, sun, once, gather, products, losses, speeds, decay, sun_own, lit,
    stoich, rate, plan, night, turned, sem,
):
    species = decay.shape[0]
    reactions = stoich_in.shape[1]
    rows = sun_own.shape[0]
    chunks = reactions // LANES
    band = lax.axis_index("lat")
    sector = lax.axis_index("lon")
    here = sun.at[
        pl.ds(pl.multiple_of(band * rows, 8), rows),
        pl.ds(pl.multiple_of(sector * LANES, LANES), LANES),
    ]
    moves = (
        (here, sun_own), (stoich_in, stoich), (rate_in, rate), (plan_in, plan), (night_in, night)
    )
    fetches = [pltpu.make_async_copy(a, b, sem.at[k]) for k, (a, b) in enumerate(moves)]
    for fetch in fetches:
        fetch.start()
    for g in range(rows):
        row = inner_step(conc[g], coefs, g)
        if g > 0:
            row = row + coefs[2, g : g + 1, :] * conc[g - 1]
        if g < rows - 1:
            row = row + coefs[4, g : g + 1, :] * conc[g + 1]
        once[g] = row
    for fetch in fetches:
        fetch.wait()
    down = iota((species, LANES), 0)
    across = iota((LANES, species), 1).astype(f32)
    mats = []
    for k in range(chunks):
        cols = pl.ds(k * LANES, LANES)
        codes = stoich[:, cols]
        row = rate[0:1, cols]
        small = jnp.concatenate([codes.astype(f32), row, jnp.zeros((3, LANES), f32)], axis=0).T
        hot = [(codes[q : q + 1, :] == down).astype(f32) for q in range(4)]
        seconds = None
        for q in range(2):
            picks = (small[:, q : q + 1] == across).astype(f32).astype(bf16)
            gather[pl.ds(q * reactions + k * LANES, LANES), :] = twice(picks)
            seconds = picks
        products[:, 2 * k * LANES : (2 * k + 2) * LANES] = twice((hot[2] + hot[3]).astype(bf16))
        speeds[pl.ds(k * LANES, LANES), :] = jnp.broadcast_to(small[:, 4:5], (LANES, LANES))
        parts = jnp.concatenate(split(hot[0] * row), axis=0)
        both = dot(parts, seconds)
        mats.append(both[:species] + both[species:])
    photo = sum(mats[1 : PHOT // LANES], mats[0])
    dark = sum(mats[PHOT // LANES + 1 :], mats[PHOT // LANES])
    for q, mat in enumerate((dark, photo)):
        high, low = split(mat + mat.T)
        losses[:, 2 * q * species : 2 * (q + 1) * species] = twice(high)
        losses[:, (4 + q) * species : (5 + q) * species] = low
    strip = []
    for s in range(SUBSTEPS):
        codes = plan[s]
        own = jnp.where(iota(codes.shape, 0) == sector, codes, 0).astype(f32)
        strip.append(jnp.sum(own, axis=0, keepdims=True))
    lats = plan.shape[2]
    flags = jnp.concatenate(strip + [jnp.zeros((8 - SUBSTEPS, lats), f32)], axis=0)
    flags = jnp.concatenate([flags, jnp.zeros((8, LANES - lats), f32)], axis=1)
    fade = jnp.exp(-night[...])
    spread = jnp.concatenate([flags, fade, jnp.zeros((7, LANES), f32)], axis=0).T
    decay[...] = jnp.broadcast_to(spread[:, 8:9], (species, LANES))
    for s in range(SUBSTEPS):
        turned[...] = jnp.broadcast_to(spread[:, s : s + 1], turned.shape)
        mine = turned[pl.ds(pl.multiple_of(band * rows, 8), rows), :]
        lit[s] = (mine >= -1.0).astype(f32)


def pair_steps(field, low, store, decay, sun, lit, gather, products, losses, speeds):
    reactions, species = speeds.shape[0], decay.shape[0]

    def both(ref):
        return jnp.concatenate([ref[low : low + 1, :], ref[low + 1 : low + 2, :]], axis=1)

    def begin(d):
        d["start"] = d["now"] = jnp.concatenate([field(low), field(low + 1)], axis=1)

    def prepare(d):
        photo = both(sun)
        high, low_part = split(d["now"])
        sun_high, sun_low = split(d["now"] * photo)
        d["weights"] = jnp.concatenate([high, low_part], axis=0)
        d["all"] = jnp.concatenate([high, low_part, sun_high, sun_low, high, sun_high], axis=0)
        d["made"] = []

    def lose(d):
        d["lost"] = dot(losses[...], d["all"])

    def react(k):
        def run(d):
            rows = slice(k * CHUNK, (k + 1) * CHUNK)
            later = slice(reactions + k * CHUNK, reactions + (k + 1) * CHUNK)
            first, second = dot(gather[rows, :], d["weights"]), dot(gather[later, :], d["weights"])
            for q in range(CHUNK // LANES):
                part = slice(q * LANES, (q + 1) * LANES)
                base = k * CHUNK + q * LANES
                flow = first[part] * twice(speeds[base : base + LANES, :]) * second[part]
                if base < PHOT:
                    flow = flow * both(sun)
                d["made"].extend(split(flow))

        return run

    def produce(d):
        d["produced"] = dot(products[...], jnp.concatenate(d["made"], axis=0))

    def close(s, last):
        def run(d):
            d["now"] = (d["start"] + d["produced"]) / (1.0 + d["lost"])
            if last:
                dark = d["start"] * twice(decay[...])
                d["now"] = d["start"] = jnp.where(both(lit.at[s]) > 0.0, d["now"], dark)

        return run

    steps = [begin]
    for s in range(SUBSTEPS):
        for sweep in range(PICARD):
            steps += [prepare, react(0), lose]
            steps += [react(k) for k in range(1, reactions // CHUNK)]
            steps += [produce, close(s, sweep == PICARD - 1)]
    steps.append(lambda d: store(low, d["now"]))
    return steps


def chemistry(lows, field, store, *refs):
    lists = [pair_steps(field, low, store, *refs) for low in lows]
    state = [{} for _ in lows]
    for t in range(len(lists[0]) + STAGGER * (len(lows) - 1)):
        for p, steps in enumerate(lists):
            at = t - STAGGER * p
            if 0 <= at < len(steps):
                steps[at](state[p])


def inner_step(center, coefs, g):
    cells = center.shape[1]
    stay, west, _, east = [coefs[k, g : g + 1, :] for k in range(4)]
    return stay * center + west * pltpu.roll(center, 1, 1) + east * pltpu.roll(center, cells - 1, 1)


def side_columns(of_pair, of_other, own, corners, columns):
    rows = of_pair.shape[1]
    left, right = sides(of_pair, of_other)
    near_l, near_r = left(0), right(0)
    zero = jnp.zeros((1, near_l.shape[1]), f32)
    sl, sr, nl, nr = corners if corners else (zero, zero, zero, zero)

    def moved(near, west, east, south, north, side):
        south = jnp.concatenate([south, near[:-1]], axis=0)
        north = jnp.concatenate([near[1:], north], axis=0)
        return side(2) * near + side(3) * west + side(4) * south + side(5) * (east + north)

    columns[...] = jnp.zeros_like(columns)
    columns[pl.ds(0, rows, stride=2), :] = near_r
    columns[pl.ds(1, rows, stride=2), :] = near_l
    columns[pl.ds(2 * rows, rows, stride=2), :] = moved(near_r, own[1], right(1), sr, nr, right)
    columns[pl.ds(2 * rows + 1, rows, stride=2), :] = moved(near_l, left(1), own[0], sl, nl, left)
    for k, row in enumerate((sr, sl, nr, nl)):
        columns[4 * rows + k : 4 * rows + k + 1, :] = row
    return columns[...].T


def mover(first, coefs, turned, rows):
    def beside(i):
        return pltpu.roll(turned, LANES - 2 * i - 1, 1)

    known = {}

    def once(g):
        if g not in known:
            i = 2 * rows if g < 0 else 2 * rows + 1 if g >= rows else g
            row, side = first(g)
            known[g] = row + side * beside(i)
        return known[g]

    def moved(g):
        row = inner_step(once(g), coefs, g) + coefs[2, g : g + 1, :] * once(g - 1)
        row = row + coefs[4, g : g + 1, :] * once(g + 1)
        return row + coefs[5, g : g + 1, :] * beside(rows + g)

    return moved


def storer(lows, out, stage, sem):
    copies = []

    def store(low, pair):
        p = lows.index(low)
        stage[2 * p] = pair[:, :LANES]
        stage[2 * p + 1] = pair[:, LANES:]
        copies.append(
            pltpu.make_async_copy(stage.at[pl.ds(2 * p, 2)], out.at[pl.ds(low, 2)], sem.at[p])
        )
        copies[-1].start()

    return store, copies


def finish(lows, moved, refs, out, stage, sem):
    store, copies = storer(lows, out, stage, sem)
    chemistry(lows, moved, store, *refs)
    for c in copies:
        c.wait()


def inner_kernel(
    once, coefs, of_pair, of_other, own,
    gather, products, losses, speeds, decay, sun, lit, out, stage, columns, sem,
):
    rows = once.shape[0]
    turned = side_columns(of_pair, of_other, own, None, columns)
    lows = list(range(rows // 4, rows - rows // 4, 2))
    moved = mover(lambda g: (once[g], coefs[5, g : g + 1, :]), coefs, turned, rows)
    finish(lows, moved, (decay, sun, lit, gather, products, losses, speeds), out, stage, sem)


def outer_kernel(
    once, coefs, of_pair, of_other, own, conc, of_near, of_next,
    gather, products, losses, speeds, decay, sun, lit, _, out, stage, columns, sem,
):
    rows, species, cells = conc.shape
    base = 2 * species
    band = lax.axis_index("lat")
    below = jnp.where(band > 0, 1.0, 0.0)
    above = jnp.where(band < lax.axis_size("lat") - 1, 1.0, 0.0)
    even_band = lax.rem(band, 2) == 0

    def of_south(span):
        return jnp.where(even_band, of_next[span, :], of_near[span, :])

    def of_north(span):
        return jnp.where(even_band, of_near[span, :], of_next[span, :])

    corners = [
        got(slice(base + 8 + k, base + 9 + k)) * inside
        for got, inside in ((of_south, below), (of_north, above))
        for k in range(2)
    ]
    turned = side_columns(of_pair, of_other, own, corners, columns)

    def halo(got, q, inside):
        return got(slice(q * species, (q + 1) * species)) * inside

    def across(got, k, inside):
        return got(slice(base + k, base + k + 1)) * inside

    def outside(got, near, far, beyond, home, back, inside):
        center = halo(got, near, inside)
        stay, west, east = [across(got, k, inside) for k in (0, 1, 3)]
        row = stay * center + west * pltpu.roll(center, 1, 1)
        row = row + east * pltpu.roll(center, cells - 1, 1)
        row = row + across(got, beyond, inside) * halo(got, far, inside)
        return row + across(got, back, inside) * home, across(got, 5, inside)

    def first(g):
        if g < 0:
            return outside(of_south, 1, 0, 2, conc[0], 4, below)
        if g >= rows:
            return outside(of_north, 0, 1, 4, conc[rows - 1], 2, above)
        row, side = once[g], coefs[5, g : g + 1, :]
        if g == 0:
            row = row + coefs[2, g : g + 1, :] * halo(of_south, 1, below)
        if g == rows - 1:
            row = row + coefs[4, g : g + 1, :] * halo(of_north, 0, above)
        return row, side

    lows = list(range(0, rows // 4, 2)) + list(range(rows - rows // 4, rows, 2))
    moved = mover(first, coefs, turned, rows)
    finish(lows, moved, (decay, sun, lit, gather, products, losses, speeds), out, stage, sem)


def local(conc, wind_lon, wind_lat, mixing, sun, rate, night_loss, stoich, plan):
    rows, species, cells = conc.shape
    reactions = rate.shape[0]
    lons = lax.axis_size("lon")
    lats = lax.axis_size("lat")
    params = pltpu.CompilerParams(vmem_limit_bytes=VMEM_LIMIT)
    vmem = pl.BlockSpec(memory_space=pltpu.VMEM)
    hbm = pl.BlockSpec(memory_space=pl.ANY)
    far = pl.BlockSpec(memory_space=pltpu.HBM)

    def pinned(x):
        return pltpu.with_memory_space_constraint(x, pltpu.HBM)

    def shape(*dims, dtype=f32):
        return KEPT(dims, dtype)

    side = shape(6, rows, species)
    ends = shape(2 * species + 16, cells)
    to_pair, to_other, own, to_near, to_next, held, coefs = pl.pallas_call(
        edge_kernel,
        out_shape=(
            side, side, shape(2, rows, species), ends, ends,
            shape(rows, species, cells), shape(6, rows, cells),
        ),
        in_specs=[far] * 4, out_specs=[vmem] * 7,
        scratch_shapes=[
            pltpu.VMEM((3, rows, cells), f32),
            pltpu.VMEM((cells, species), f32),
            pltpu.SemaphoreType.DMA((4,)),
        ],
        compiler_params=params, name="edges",
    )(*[pinned(x) for x in (conc, wind_lon, wind_lat, mixing)])

    pair = [(i, i ^ 1) for i in range(lons)]
    other = [(i, (i - 1) % lons if i % 2 == 0 else (i + 1) % lons) for i in range(lons)]
    near, after = [], []
    for b in range(lats):
        step_near, step_after = (1, -1) if b % 2 == 0 else (-1, 1)
        for perm, c in ((near, b + step_near), (after, b + step_after)):
            for i in range(lons):
                target = (c, i) if 0 <= c < lats else (b, i ^ 1)
                perm.append((b * lons + i, target[0] * lons + target[1]))
    of_pair = lax.ppermute(to_pair, "lon", pair)
    of_other = lax.ppermute(to_other, "lon", other)

    once, *tables = pl.pallas_call(
        table_kernel,
        out_shape=(
            shape(rows, species, cells),
            shape(2 * reactions, 2 * species, dtype=bf16),
            shape(species, 2 * reactions, dtype=bf16),
            shape(species, 6 * species, dtype=bf16),
            shape(reactions, LANES),
            shape(species, LANES),
            shape(rows, LANES),
            shape(SUBSTEPS, rows, LANES),
        ),
        in_specs=[vmem] * 2 + [far] * 5, out_specs=[vmem] * 8,
        scratch_shapes=[
            pltpu.VMEM(stoich.shape, jnp.int32),
            pltpu.VMEM((1, reactions), f32),
            pltpu.VMEM((plan.shape[0], plan.shape[2], plan.shape[1]), jnp.int32),
            pltpu.VMEM((1, species), f32),
            pltpu.VMEM((LANES, LANES), f32),
            pltpu.SemaphoreType.DMA((5,)),
        ],
        cost_estimate=pl.CostEstimate(flops=10**9, transcendentals=0, bytes_accessed=2 * 10**6),
        compiler_params=params, name="tables",
    )(
        held, coefs, pinned(stoich), pinned(rate.reshape(1, reactions)),
        pinned(jnp.swapaxes(plan, 1, 2)), pinned(night_loss.reshape(1, species)), pinned(sun),
    )

    to_near, to_next = pl.pallas_call(
        corner_kernel, out_shape=(ends, ends),
        in_specs=[vmem] * 2 + [hbm] * 3, out_specs=[hbm] * 2,
        scratch_shapes=[pltpu.VMEM((2, 8, species), f32), pltpu.SemaphoreType.DMA((2,))],
        input_output_aliases={2: 0, 3: 1},
        compiler_params=params, name="corners",
    )(of_pair, of_other, to_near, to_next, tables[5])
    of_near = lax.ppermute(to_near, ("lat", "lon"), near)
    of_next = lax.ppermute(to_next, ("lat", "lon"), after)

    shared = (once, coefs, of_pair, of_other, own)
    scratch = [
        pltpu.VMEM((rows // 2, species, cells), f32),
        pltpu.VMEM((LANES, species), f32),
        pltpu.SemaphoreType.DMA((rows // 4,)),
    ]
    inner = pl.pallas_call(
        inner_kernel, out_shape=jax.ShapeDtypeStruct(conc.shape, f32),
        in_specs=[vmem] * 12, out_specs=hbm, scratch_shapes=scratch,
        compiler_params=params, name="inner",
    )(*shared, *tables)
    return pl.pallas_call(
        outer_kernel, out_shape=jax.ShapeDtypeStruct(conc.shape, f32),
        in_specs=[vmem] * 15 + [hbm], out_specs=hbm, scratch_shapes=scratch,
        input_output_aliases={15: 0},
        compiler_params=params, name="outer",
    )(*shared, held, of_near, of_next, *tables, inner)


def solution(mesh):
    field = P("lat", None, "lon")
    cell = P("lat", "lon")
    return jax.shard_map(
        local,
        mesh=mesh,
        in_specs=(field, cell, cell, cell, P(), P(), P(), P(), P()),
        out_specs=field,
        check_vma=False,
    )
```

```python
import jax
import jax.numpy as jnp
from jax import lax
from jax.experimental import pallas as pl
from jax.experimental.pallas import tpu as pltpu
from jax.sharding import PartitionSpec as P

SUBSTEPS = 2
PICARD = 3
PHOT = 128
LANES = 128
VMEM_LIMIT = 48 << 20
KEPT = jax.ShapeDtypeStruct
CHUNK = 256
STAGGER = 2

f32 = jnp.float32
bf16 = jnp.bfloat16


def split(x):
    high = x.astype(bf16)
    return high, (x - high.astype(f32)).astype(bf16)


def twice(x):
    return jnp.concatenate([x, x], axis=1)


def dot(a, b):
    return jnp.dot(a, b, preferred_element_type=f32)


def iota(shape, axis):
    return lax.broadcasted_iota(jnp.int32, shape, axis)


def edge_kernel(
    conc_in, wlon_in, wlat_in, mix_in, to_pair, to_other, own, to_near, to_next, conc, coefs,
    winds, columns, sem,
):
    rows, species, cells = conc.shape
    fetches = [
        pltpu.make_async_copy(ref, winds.at[k], sem.at[k])
        for k, ref in enumerate((wlon_in, wlat_in, mix_in))
    ]
    part = rows // 4
    fetches += [
        pltpu.make_async_copy(
            conc_in.at[pl.ds(q * part, part)], conc.at[pl.ds(q * part, part)], sem.at[3 + q]
        )
        for q in range(4)
    ]
    for fetch in fetches:
        fetch.start()
    for fetch in fetches[:3]:
        fetch.wait()
    wlon, wlat, mix = [winds[k] for k in range(3)]
    place = iota((rows, cells), 1)
    stay = 1.0 - wlon - wlat - 4.0 * mix
    west, south = wlon + mix, wlat + mix
    coefs[0] = stay
    coefs[1] = jnp.where(place == 0, 0.0, west)
    coefs[2] = south
    coefs[3] = jnp.where(place == cells - 1, 0.0, mix)
    coefs[4] = mix
    coefs[5] = jnp.where(place == 0, west, jnp.where(place == cells - 1, mix, 0.0))
    even = lax.rem(lax.axis_index("lon"), 2) == 0

    def put(k, right, left):
        to_pair[k] = jnp.where(even, right, left)
        to_other[k] = jnp.where(even, left, right)

    right, left = jnp.zeros((rows, cells), f32), jnp.zeros((rows, cells), f32)
    for k, ref in enumerate((stay, west, south, mix)):
        right = jnp.where(place == k, ref[:, cells - 1 : cells], right)
        left = jnp.where(place == k, ref[:, 0:1], left)
    put(2, right, left)
    base = 2 * species
    pad = jnp.zeros((2, cells), f32)
    even_band = lax.rem(lax.axis_index("lat"), 2) == 0

    def send(span, north, south):
        to_near[span, :] = jnp.where(even_band, north, south)
        to_next[span, :] = jnp.where(even_band, south, north)

    send(
        slice(base, base + 8),
        *[
            jnp.concatenate([coefs[k, g : g + 1] for k in range(6)] + [pad])
            for g in (rows - 1, 0)
        ],
    )
    lane = iota((species, cells), 1)
    picked = jnp.zeros((species, cells), f32)
    for g in range(rows):
        if g % part == 0:
            fetches[3 + g // part].wait()
        turned = pltpu.roll(conc[g], (4 * g + 2) % cells, 1)
        picked = jnp.where((lane >= 4 * g) & (lane < 4 * g + 4), turned, picked)
    columns[...] = picked.T
    last2, last1, first1, first2 = [columns[pl.ds(q, rows, stride=4), :] for q in range(4)]
    put(0, last1, first1)
    put(1, last2, first2)
    own[0] = first1
    own[1] = last1
    for q in range(2):
        send(slice(q * species, (q + 1) * species), conc[rows - 2 + q], conc[q])


def sides(of_pair, of_other):
    even = lax.rem(lax.axis_index("lon"), 2) == 0
    return (
        lambda k: jnp.where(even, of_other[k], of_pair[k]),
        lambda k: jnp.where(even, of_pair[k], of_other[k]),
    )


def corner_kernel(of_pair, of_other, _, __, ___, to_near, to_next, ends, sem):
    rows = of_pair.shape[1]
    left, right = sides(of_pair, of_other)
    near_l, near_r = left(0), right(0)
    pad = jnp.zeros((6, near_l.shape[1]), f32)
    north, south = [
        jnp.concatenate([near_l[g : g + 1], near_r[g : g + 1], pad], axis=0) for g in (rows - 1, 0)
    ]
    even_band = lax.rem(lax.axis_index("lat"), 2) == 0
    ends[0] = jnp.where(even_band, north, south)
    ends[1] = jnp.where(even_band, south, north)
    copies = []
    for p, ref in enumerate((to_near, to_next)):
        dest = ref.at[pl.ds(ref.shape[0] - 8, 8), :]
        copies.append(pltpu.make_async_copy(ends.at[p], dest, sem.at[p]))
        copies[p].start()
    for c in copies:
        c.wait()


def table_kernel(
    conc, coefs, stoich_in, rate_in, plan_in, night_in, sun, once, gather, products, losses, speeds, decay, sun_own, lit,
    stoich, rate, plan, night, turned, sem,
):
    species = decay.shape[0]
    reactions = stoich_in.shape[1]
    rows = sun_own.shape[0]
    chunks = reactions // LANES
    band = lax.axis_index("lat")
    sector = lax.axis_index("lon")
    here = sun.at[
        pl.ds(pl.multiple_of(band * rows, 8), rows),
        pl.ds(pl.multiple_of(sector * LANES, LANES), LANES),
    ]
    moves = (
        (here, sun_own), (stoich_in, stoich), (rate_in, rate), (plan_in, plan), (night_in, night)
    )
    fetches = [pltpu.make_async_copy(a, b, sem.at[k]) for k, (a, b) in enumerate(moves)]
    for fetch in fetches:
        fetch.start()
    for g in range(rows):
        row = inner_step(conc[g], coefs, g)
        if g > 0:
            row = row + coefs[2, g : g + 1, :] * conc[g - 1]
        if g < rows - 1:
            row = row + coefs[4, g : g + 1, :] * conc[g + 1]
        once[g] = row
    for fetch in fetches:
        fetch.wait()
    down = iota((species, LANES), 0)
    across = iota((LANES, species), 1).astype(f32)
    mats = []
    for k in range(chunks):
        cols = pl.ds(k * LANES, LANES)
        codes = stoich[:, cols]
        row = rate[0:1, cols]
        small = jnp.concatenate([codes.astype(f32), row, jnp.zeros((3, LANES), f32)], axis=0).T
        hot = [(codes[q : q + 1, :] == down).astype(f32) for q in range(4)]
        seconds = None
        for q in range(2):
            picks = (small[:, q : q + 1] == across).astype(f32).astype(bf16)
            gather[pl.ds(q * reactions + k * LANES, LANES), :] = twice(picks)
            seconds = picks
        products[:, 2 * k * LANES : (2 * k + 2) * LANES] = twice((hot[2] + hot[3]).astype(bf16))
        speeds[pl.ds(k * LANES, LANES), :] = jnp.broadcast_to(small[:, 4:5], (LANES, LANES))
        parts = jnp.concatenate(split(hot[0] * row), axis=0)
        both = dot(parts, seconds)
        mats.append(both[:species] + both[species:])
    photo = sum(mats[1 : PHOT // LANES], mats[0])
    dark = sum(mats[PHOT // LANES + 1 :], mats[PHOT // LANES])
    for q, mat in enumerate((dark, photo)):
        high, low = split(mat + mat.T)
        losses[:, 2 * q * species : 2 * (q + 1) * species] = twice(high)
        losses[:, (4 + q) * species : (5 + q) * species] = low
    strip = []
    for s in range(SUBSTEPS):
        codes = plan[s]
        own = jnp.where(iota(codes.shape, 0) == sector, codes, 0).astype(f32)
        strip.append(jnp.sum(own, axis=0, keepdims=True))
    lats = plan.shape[2]
    flags = jnp.concatenate(strip + [jnp.zeros((8 - SUBSTEPS, lats), f32)], axis=0)
    flags = jnp.concatenate([flags, jnp.zeros((8, LANES - lats), f32)], axis=1)
    fade = jnp.exp(-night[...])
    spread = jnp.concatenate([flags, fade, jnp.zeros((7, LANES), f32)], axis=0).T
    decay[...] = jnp.broadcast_to(spread[:, 8:9], (species, LANES))
    for s in range(SUBSTEPS):
        turned[...] = jnp.broadcast_to(spread[:, s : s + 1], turned.shape)
        mine = turned[pl.ds(pl.multiple_of(band * rows, 8), rows), :]
        lit[s] = (mine >= -1.0).astype(f32)


def pair_steps(field, low, store, decay, sun, lit, gather, products, losses, speeds):
    reactions, species = speeds.shape[0], decay.shape[0]

    def both(ref):
        return jnp.concatenate([ref[low : low + 1, :], ref[low + 1 : low + 2, :]], axis=1)

    def begin(d):
        d["start"] = d["now"] = jnp.concatenate([field(low), field(low + 1)], axis=1)

    def prepare(d):
        photo = both(sun)
        high, low_part = split(d["now"])
        sun_high, sun_low = split(d["now"] * photo)
        d["weights"] = jnp.concatenate([high, low_part], axis=0)
        d["all"] = jnp.concatenate([high, low_part, sun_high, sun_low, high, sun_high], axis=0)
        d["made"] = []

    def lose(d):
        d["lost"] = dot(losses[...], d["all"])

    def react(k):
        def run(d):
            rows = slice(k * CHUNK, (k + 1) * CHUNK)
            later = slice(reactions + k * CHUNK, reactions + (k + 1) * CHUNK)
            first, second = dot(gather[rows, :], d["weights"]), dot(gather[later, :], d["weights"])
            for q in range(CHUNK // LANES):
                part = slice(q * LANES, (q + 1) * LANES)
                base = k * CHUNK + q * LANES
                flow = first[part] * twice(speeds[base : base + LANES, :]) * second[part]
                if base < PHOT:
                    flow = flow * both(sun)
                d["made"].extend(split(flow))

        return run

    def produce(d):
        d["produced"] = dot(products[...], jnp.concatenate(d["made"], axis=0))

    def close(s, last):
        def run(d):
            d["now"] = (d["start"] + d["produced"]) / (1.0 + d["lost"])
            if last:
                dark = d["start"] * twice(decay[...])
                d["now"] = d["start"] = jnp.where(both(lit.at[s]) > 0.0, d["now"], dark)

        return run

    steps = [begin]
    for s in range(SUBSTEPS):
        for sweep in range(PICARD):
            steps += [prepare, react(0), lose]
            steps += [react(k) for k in range(1, reactions // CHUNK)]
            steps += [produce, close(s, sweep == PICARD - 1)]
    steps.append(lambda d: store(low, d["now"]))
    return steps


def chemistry(lows, field, store, *refs):
    lists = [pair_steps(field, low, store, *refs) for low in lows]
    state = [{} for _ in lows]
    for t in range(len(lists[0]) + STAGGER * (len(lows) - 1)):
        for p, steps in enumerate(lists):
            at = t - STAGGER * p
            if 0 <= at < len(steps):
                steps[at](state[p])


def inner_step(center, coefs, g):
    cells = center.shape[1]
    stay, west, _, east = [coefs[k, g : g + 1, :] for k in range(4)]
    return stay * center + west * pltpu.roll(center, 1, 1) + east * pltpu.roll(center, cells - 1, 1)


def side_columns(of_pair, of_other, own, corners, columns):
    rows = of_pair.shape[1]
    left, right = sides(of_pair, of_other)
    near_l, near_r = left(0), right(0)
    zero = jnp.zeros((1, near_l.shape[1]), f32)
    sl, sr, nl, nr = corners if corners else (zero, zero, zero, zero)

    def moved(near, west, east, south, north, side):
        south = jnp.concatenate([south, near[:-1]], axis=0)
        north = jnp.concatenate([near[1:], north], axis=0)
        stay, w, s, e = [side(2)[:, k : k + 1] for k in range(4)]
        return stay * near + w * west + s * south + e * (east + north)

    columns[...] = jnp.zeros_like(columns)
    columns[pl.ds(0, rows, stride=2), :] = near_r
    columns[pl.ds(1, rows, stride=2), :] = near_l
    columns[pl.ds(2 * rows, rows, stride=2), :] = moved(near_r, own[1], right(1), sr, nr, right)
    columns[pl.ds(2 * rows + 1, rows, stride=2), :] = moved(near_l, left(1), own[0], sl, nl, left)
    for k, row in enumerate((sr, sl, nr, nl)):
        columns[4 * rows + k : 4 * rows + k + 1, :] = row
    return columns[...].T


def mover(first, coefs, turned, rows):
    def beside(i):
        return pltpu.roll(turned, LANES - 2 * i - 1, 1)

    known = {}

    def once(g):
        if g not in known:
            i = 2 * rows if g < 0 else 2 * rows + 1 if g >= rows else g
            row, side = first(g)
            known[g] = row + side * beside(i)
        return known[g]

    def moved(g):
        row = inner_step(once(g), coefs, g) + coefs[2, g : g + 1, :] * once(g - 1)
        row = row + coefs[4, g : g + 1, :] * once(g + 1)
        return row + coefs[5, g : g + 1, :] * beside(rows + g)

    return moved


def storer(lows, out, stage, sem):
    copies = []

    def store(low, pair):
        p = lows.index(low)
        stage[2 * p] = pair[:, :LANES]
        stage[2 * p + 1] = pair[:, LANES:]
        copies.append(
            pltpu.make_async_copy(stage.at[pl.ds(2 * p, 2)], out.at[pl.ds(low, 2)], sem.at[p])
        )
        copies[-1].start()

    return store, copies


def finish(lows, moved, refs, out, stage, sem):
    store, copies = storer(lows, out, stage, sem)
    chemistry(lows, moved, store, *refs)
    for c in copies:
        c.wait()


def inner_kernel(
    once, coefs, of_pair, of_other, own,
    gather, products, losses, speeds, decay, sun, lit, out, stage, columns, sem,
):
    rows = once.shape[0]
    turned = side_columns(of_pair, of_other, own, None, columns)
    lows = list(range(rows // 4, rows - rows // 4, 2))
    moved = mover(lambda g: (once[g], coefs[5, g : g + 1, :]), coefs, turned, rows)
    finish(lows, moved, (decay, sun, lit, gather, products, losses, speeds), out, stage, sem)


def outer_kernel(
    once, coefs, of_pair, of_other, own, conc, of_near, of_next,
    gather, products, losses, speeds, decay, sun, lit, _, out, stage, columns, sem,
):
    rows, species, cells = conc.shape
    base = 2 * species
    band = lax.axis_index("lat")
    below = jnp.where(band > 0, 1.0, 0.0)
    above = jnp.where(band < lax.axis_size("lat") - 1, 1.0, 0.0)
    even_band = lax.rem(band, 2) == 0

    def of_south(span):
        return jnp.where(even_band, of_next[span, :], of_near[span, :])

    def of_north(span):
        return jnp.where(even_band, of_near[span, :], of_next[span, :])

    corners = [
        got(slice(base + 8 + k, base + 9 + k)) * inside
        for got, inside in ((of_south, below), (of_north, above))
        for k in range(2)
    ]
    turned = side_columns(of_pair, of_other, own, corners, columns)

    def halo(got, q, inside):
        return got(slice(q * species, (q + 1) * species)) * inside

    def across(got, k, inside):
        return got(slice(base + k, base + k + 1)) * inside

    def outside(got, near, far, beyond, home, back, inside):
        center = halo(got, near, inside)
        stay, west, east = [across(got, k, inside) for k in (0, 1, 3)]
        row = stay * center + west * pltpu.roll(center, 1, 1)
        row = row + east * pltpu.roll(center, cells - 1, 1)
        row = row + across(got, beyond, inside) * halo(got, far, inside)
        return row + across(got, back, inside) * home, across(got, 5, inside)

    def first(g):
        if g < 0:
            return outside(of_south, 1, 0, 2, conc[0], 4, below)
        if g >= rows:
            return outside(of_north, 0, 1, 4, conc[rows - 1], 2, above)
        row, side = once[g], coefs[5, g : g + 1, :]
        if g == 0:
            row = row + coefs[2, g : g + 1, :] * halo(of_south, 1, below)
        if g == rows - 1:
            row = row + coefs[4, g : g + 1, :] * halo(of_north, 0, above)
        return row, side

    lows = list(range(0, rows // 4, 2)) + list(range(rows - rows // 4, rows, 2))
    moved = mover(first, coefs, turned, rows)
    finish(lows, moved, (decay, sun, lit, gather, products, losses, speeds), out, stage, sem)


def local(conc, wind_lon, wind_lat, mixing, sun, rate, night_loss, stoich, plan):
    rows, species, cells = conc.shape
    reactions = rate.shape[0]
    lons = lax.axis_size("lon")
    lats = lax.axis_size("lat")
    params = pltpu.CompilerParams(vmem_limit_bytes=VMEM_LIMIT)
    vmem = pl.BlockSpec(memory_space=pltpu.VMEM)
    hbm = pl.BlockSpec(memory_space=pl.ANY)
    far = pl.BlockSpec(memory_space=pltpu.HBM)

    def pinned(x):
        return pltpu.with_memory_space_constraint(x, pltpu.HBM)

    def shape(*dims, dtype=f32):
        return KEPT(dims, dtype)

    side = shape(3, rows, species)
    ends = shape(2 * species + 16, cells)
    to_pair, to_other, own, to_near, to_next, held, coefs = pl.pallas_call(
        edge_kernel,
        out_shape=(
            side, side, shape(2, rows, species), ends, ends,
            shape(rows, species, cells), shape(6, rows, cells),
        ),
        in_specs=[far] * 4, out_specs=[vmem] * 7,
        scratch_shapes=[
            pltpu.VMEM((3, rows, cells), f32),
            pltpu.VMEM((cells, species), f32),
            pltpu.SemaphoreType.DMA((7,)),
        ],
        compiler_params=params, name="edges",
    )(*[pinned(x) for x in (conc, wind_lon, wind_lat, mixing)])

    pair = [(i, i ^ 1) for i in range(lons)]
    other = [(i, (i - 1) % lons if i % 2 == 0 else (i + 1) % lons) for i in range(lons)]
    near, after = [], []
    for b in range(lats):
        step_near, step_after = (1, -1) if b % 2 == 0 else (-1, 1)
        for perm, c in ((near, b + step_near), (after, b + step_after)):
            for i in range(lons):
                target = (c, i) if 0 <= c < lats else (b, i ^ 1)
                perm.append((b * lons + i, target[0] * lons + target[1]))
    of_pair = lax.ppermute(to_pair, "lon", pair)
    of_other = lax.ppermute(to_other, "lon", other)

    once, *tables = pl.pallas_call(
        table_kernel,
        out_shape=(
            shape(rows, species, cells),
            shape(2 * reactions, 2 * species, dtype=bf16),
            shape(species, 2 * reactions, dtype=bf16),
            shape(species, 6 * species, dtype=bf16),
            shape(reactions, LANES),
            shape(species, LANES),
            shape(rows, LANES),
            shape(SUBSTEPS, rows, LANES),
        ),
        in_specs=[vmem] * 2 + [far] * 5, out_specs=[vmem] * 8,
        scratch_shapes=[
            pltpu.VMEM(stoich.shape, jnp.int32),
            pltpu.VMEM((1, reactions), f32),
            pltpu.VMEM((plan.shape[0], plan.shape[2], plan.shape[1]), jnp.int32),
            pltpu.VMEM((1, species), f32),
            pltpu.VMEM((LANES, LANES), f32),
            pltpu.SemaphoreType.DMA((5,)),
        ],
        cost_estimate=pl.CostEstimate(flops=10**9, transcendentals=0, bytes_accessed=2 * 10**6),
        compiler_params=params, name="tables",
    )(
        held, coefs, pinned(stoich), pinned(rate.reshape(1, reactions)),
        pinned(jnp.swapaxes(plan, 1, 2)), pinned(night_loss.reshape(1, species)), pinned(sun),
    )

    to_near, to_next = pl.pallas_call(
        corner_kernel, out_shape=(ends, ends),
        in_specs=[vmem] * 2 + [hbm] * 3, out_specs=[hbm] * 2,
        scratch_shapes=[pltpu.VMEM((2, 8, species), f32), pltpu.SemaphoreType.DMA((2,))],
        input_output_aliases={2: 0, 3: 1},
        compiler_params=params, name="corners",
    )(of_pair, of_other, to_near, to_next, tables[5])
    of_near = lax.ppermute(to_near, ("lat", "lon"), near)
    of_next = lax.ppermute(to_next, ("lat", "lon"), after)

    shared = (once, coefs, of_pair, of_other, own)
    scratch = [
        pltpu.VMEM((rows // 2, species, cells), f32),
        pltpu.VMEM((LANES, species), f32),
        pltpu.SemaphoreType.DMA((rows // 4,)),
    ]
    inner = pl.pallas_call(
        inner_kernel, out_shape=jax.ShapeDtypeStruct(conc.shape, f32),
        in_specs=[vmem] * 12, out_specs=hbm, scratch_shapes=scratch,
        compiler_params=params, name="inner",
    )(*shared, *tables)
    return pl.pallas_call(
        outer_kernel, out_shape=jax.ShapeDtypeStruct(conc.shape, f32),
        in_specs=[vmem] * 15 + [hbm], out_specs=hbm, scratch_shapes=scratch,
        input_output_aliases={15: 0},
        compiler_params=params, name="outer",
    )(*shared, held, of_near, of_next, *tables, inner)


def solution(mesh):
    field = P("lat", None, "lon")
    cell = P("lat", "lon")
    return jax.shard_map(
        local,
        mesh=mesh,
        in_specs=(field, cell, cell, cell, P(), P(), P(), P(), P()),
        out_specs=field,
        check_vma=False,
    )
```

```python
import jax
import jax.numpy as jnp
from jax import lax
from jax.experimental import pallas as pl
from jax.experimental.pallas import tpu as pltpu
from jax.sharding import PartitionSpec as P

SUBSTEPS = 2
PICARD = 3
PHOT = 128
LANES = 128
VMEM_LIMIT = 48 << 20
KEPT = jax.ShapeDtypeStruct
CHUNK = 256
STAGGER = 2

f32 = jnp.float32
bf16 = jnp.bfloat16


def split(x):
    high = x.astype(bf16)
    return high, (x - high.astype(f32)).astype(bf16)


def twice(x):
    return jnp.concatenate([x, x], axis=1)


def dot(a, b):
    return jnp.dot(a, b, preferred_element_type=f32)


def iota(shape, axis):
    return lax.broadcasted_iota(jnp.int32, shape, axis)


def edge_kernel(
    conc_in, wlon_in, wlat_in, mix_in, to_other, to_pair, own, to_next, to_near, conc, coefs,
    winds, columns, sem,
):
    rows, species, cells = conc.shape
    fetches = [
        pltpu.make_async_copy(ref, winds.at[k], sem.at[k])
        for k, ref in enumerate((wlon_in, wlat_in, mix_in))
    ]
    part = rows // 4
    fetches += [
        pltpu.make_async_copy(
            conc_in.at[pl.ds(q * part, part)], conc.at[pl.ds(q * part, part)], sem.at[3 + q]
        )
        for q in range(4)
    ]
    for fetch in fetches:
        fetch.start()
    for fetch in fetches[:3]:
        fetch.wait()
    wlon, wlat, mix = [winds[k] for k in range(3)]
    place = iota((rows, cells), 1)
    stay = 1.0 - wlon - wlat - 4.0 * mix
    west, south = wlon + mix, wlat + mix
    coefs[0] = stay
    coefs[1] = jnp.where(place == 0, 0.0, west)
    coefs[2] = south
    coefs[3] = jnp.where(place == cells - 1, 0.0, mix)
    coefs[4] = mix
    coefs[5] = jnp.where(place == 0, west, jnp.where(place == cells - 1, mix, 0.0))
    even = lax.rem(lax.axis_index("lon"), 2) == 0

    def put(k, right, left):
        to_pair[k] = jnp.where(even, right, left)
        to_other[k] = jnp.where(even, left, right)

    right, left = jnp.zeros((rows, cells), f32), jnp.zeros((rows, cells), f32)
    for k, ref in enumerate((stay, west, south, mix)):
        right = jnp.where(place == k, ref[:, cells - 1 : cells], right)
        left = jnp.where(place == k, ref[:, 0:1], left)
    put(2, right, left)
    base = 2 * species
    pad = jnp.zeros((2, cells), f32)
    even_band = lax.rem(lax.axis_index("lat"), 2) == 0

    def send(span, north, south):
        to_near[span, :] = jnp.where(even_band, north, south)
        to_next[span, :] = jnp.where(even_band, south, north)

    send(
        slice(base, base + 8),
        *[
            jnp.concatenate([coefs[k, g : g + 1] for k in range(6)] + [pad])
            for g in (rows - 1, 0)
        ],
    )
    lane = iota((species, cells), 1)
    picked = jnp.zeros((species, cells), f32)
    for g in range(rows):
        if g % part == 0:
            fetches[3 + g // part].wait()
        turned = pltpu.roll(conc[g], (4 * g + 2) % cells, 1)
        picked = jnp.where((lane >= 4 * g) & (lane < 4 * g + 4), turned, picked)
    columns[...] = picked.T
    last2, last1, first1, first2 = [columns[pl.ds(q, rows, stride=4), :] for q in range(4)]
    put(0, last1, first1)
    put(1, last2, first2)
    own[0] = first1
    own[1] = last1
    for q in range(2):
        send(slice(q * species, (q + 1) * species), conc[rows - 2 + q], conc[q])


def sides(of_pair, of_other):
    even = lax.rem(lax.axis_index("lon"), 2) == 0
    return (
        lambda k: jnp.where(even, of_other[k], of_pair[k]),
        lambda k: jnp.where(even, of_pair[k], of_other[k]),
    )


def corner_kernel(of_other, of_pair, _, __, ___, to_next, to_near, ends, sem):
    rows = of_pair.shape[1]
    left, right = sides(of_pair, of_other)
    near_l, near_r = left(0), right(0)
    pad = jnp.zeros((6, near_l.shape[1]), f32)
    north, south = [
        jnp.concatenate([near_l[g : g + 1], near_r[g : g + 1], pad], axis=0) for g in (rows - 1, 0)
    ]
    even_band = lax.rem(lax.axis_index("lat"), 2) == 0
    ends[0] = jnp.where(even_band, south, north)
    ends[1] = jnp.where(even_band, north, south)
    copies = []
    for p, ref in enumerate((to_next, to_near)):
        dest = ref.at[pl.ds(ref.shape[0] - 8, 8), :]
        copies.append(pltpu.make_async_copy(ends.at[p], dest, sem.at[p]))
        copies[p].start()
    for c in copies:
        c.wait()


def table_kernel(
    conc, coefs, stoich_in, rate_in, plan_in, night_in, sun, once, gather, products, losses, speeds, decay, sun_own, lit,
    stoich, rate, plan, night, turned, sem,
):
    species = decay.shape[0]
    reactions = stoich_in.shape[1]
    rows = sun_own.shape[0]
    chunks = reactions // LANES
    band = lax.axis_index("lat")
    sector = lax.axis_index("lon")
    here = sun.at[
        pl.ds(pl.multiple_of(band * rows, 8), rows),
        pl.ds(pl.multiple_of(sector * LANES, LANES), LANES),
    ]
    moves = (
        (here, sun_own), (stoich_in, stoich), (rate_in, rate), (plan_in, plan), (night_in, night)
    )
    fetches = [pltpu.make_async_copy(a, b, sem.at[k]) for k, (a, b) in enumerate(moves)]
    for fetch in fetches:
        fetch.start()
    for g in range(rows):
        row = inner_step(conc[g], coefs, g)
        if g > 0:
            row = row + coefs[2, g : g + 1, :] * conc[g - 1]
        if g < rows - 1:
            row = row + coefs[4, g : g + 1, :] * conc[g + 1]
        once[g] = row
    for fetch in fetches:
        fetch.wait()
    down = iota((species, LANES), 0)
    across = iota((LANES, species), 1).astype(f32)
    mats = []
    for k in range(chunks):
        cols = pl.ds(k * LANES, LANES)
        codes = stoich[:, cols]
        row = rate[0:1, cols]
        small = jnp.concatenate([codes.astype(f32), row, jnp.zeros((3, LANES), f32)], axis=0).T
        hot = [(codes[q : q + 1, :] == down).astype(f32) for q in range(4)]
        seconds = None
        for q in range(2):
            picks = (small[:, q : q + 1] == across).astype(f32).astype(bf16)
            gather[pl.ds(q * reactions + k * LANES, LANES), :] = twice(picks)
            seconds = picks
        products[:, 2 * k * LANES : (2 * k + 2) * LANES] = twice((hot[2] + hot[3]).astype(bf16))
        speeds[pl.ds(k * LANES, LANES), :] = jnp.broadcast_to(small[:, 4:5], (LANES, LANES))
        parts = jnp.concatenate(split(hot[0] * row), axis=0)
        both = dot(parts, seconds)
        mats.append(both[:species] + both[species:])
    photo = sum(mats[1 : PHOT // LANES], mats[0])
    dark = sum(mats[PHOT // LANES + 1 :], mats[PHOT // LANES])
    for q, mat in enumerate((dark, photo)):
        high, low = split(mat + mat.T)
        losses[:, 2 * q * species : 2 * (q + 1) * species] = twice(high)
        losses[:, (4 + q) * species : (5 + q) * species] = low
    strip = []
    for s in range(SUBSTEPS):
        codes = plan[s]
        own = jnp.where(iota(codes.shape, 0) == sector, codes, 0).astype(f32)
        strip.append(jnp.sum(own, axis=0, keepdims=True))
    lats = plan.shape[2]
    flags = jnp.concatenate(strip + [jnp.zeros((8 - SUBSTEPS, lats), f32)], axis=0)
    flags = jnp.concatenate([flags, jnp.zeros((8, LANES - lats), f32)], axis=1)
    fade = jnp.exp(-night[...])
    spread = jnp.concatenate([flags, fade, jnp.zeros((7, LANES), f32)], axis=0).T
    decay[...] = jnp.broadcast_to(spread[:, 8:9], (species, LANES))
    for s in range(SUBSTEPS):
        turned[...] = jnp.broadcast_to(spread[:, s : s + 1], turned.shape)
        mine = turned[pl.ds(pl.multiple_of(band * rows, 8), rows), :]
        lit[s] = (mine >= -1.0).astype(f32)


def pair_steps(field, low, store, decay, sun, lit, gather, products, losses, speeds):
    reactions, species = speeds.shape[0], decay.shape[0]

    def both(ref):
        return jnp.concatenate([ref[low : low + 1, :], ref[low + 1 : low + 2, :]], axis=1)

    def begin(d):
        d["start"] = d["now"] = jnp.concatenate([field(low), field(low + 1)], axis=1)

    def prepare(d):
        photo = both(sun)
        high, low_part = split(d["now"])
        sun_high, sun_low = split(d["now"] * photo)
        d["weights"] = jnp.concatenate([high, low_part], axis=0)
        d["all"] = jnp.concatenate([high, low_part, sun_high, sun_low, high, sun_high], axis=0)
        d["made"] = []

    def lose(d):
        d["lost"] = dot(losses[...], d["all"])

    def react(k):
        def run(d):
            rows = slice(k * CHUNK, (k + 1) * CHUNK)
            later = slice(reactions + k * CHUNK, reactions + (k + 1) * CHUNK)
            first, second = dot(gather[rows, :], d["weights"]), dot(gather[later, :], d["weights"])
            for q in range(CHUNK // LANES):
                part = slice(q * LANES, (q + 1) * LANES)
                base = k * CHUNK + q * LANES
                flow = first[part] * twice(speeds[base : base + LANES, :]) * second[part]
                if base < PHOT:
                    flow = flow * both(sun)
                d["made"].extend(split(flow))

        return run

    def produce(d):
        d["produced"] = dot(products[...], jnp.concatenate(d["made"], axis=0))

    def close(s, last):
        def run(d):
            d["now"] = (d["start"] + d["produced"]) / (1.0 + d["lost"])
            if last:
                dark = d["start"] * twice(decay[...])
                d["now"] = d["start"] = jnp.where(both(lit.at[s]) > 0.0, d["now"], dark)

        return run

    steps = [begin]
    for s in range(SUBSTEPS):
        for sweep in range(PICARD):
            steps += [prepare, react(0), lose]
            steps += [react(k) for k in range(1, reactions // CHUNK)]
            steps += [produce, close(s, sweep == PICARD - 1)]
    steps.append(lambda d: store(low, d["now"]))
    return steps


def chemistry(lows, field, store, *refs):
    lists = [pair_steps(field, low, store, *refs) for low in lows]
    state = [{} for _ in lows]
    for t in range(len(lists[0]) + STAGGER * (len(lows) - 1)):
        for p, steps in enumerate(lists):
            at = t - STAGGER * p
            if 0 <= at < len(steps):
                steps[at](state[p])


def inner_step(center, coefs, g):
    cells = center.shape[1]
    stay, west, _, east = [coefs[k, g : g + 1, :] for k in range(4)]
    return stay * center + west * pltpu.roll(center, 1, 1) + east * pltpu.roll(center, cells - 1, 1)


def side_columns(of_pair, of_other, own, corners, columns):
    rows = of_pair.shape[1]
    left, right = sides(of_pair, of_other)
    near_l, near_r = left(0), right(0)
    zero = jnp.zeros((1, near_l.shape[1]), f32)
    sl, sr, nl, nr = corners if corners else (zero, zero, zero, zero)

    def moved(near, west, east, south, north, side):
        south = jnp.concatenate([south, near[:-1]], axis=0)
        north = jnp.concatenate([near[1:], north], axis=0)
        stay, w, s, e = [side(2)[:, k : k + 1] for k in range(4)]
        return stay * near + w * west + s * south + e * (east + north)

    columns[...] = jnp.zeros_like(columns)
    columns[pl.ds(0, rows, stride=2), :] = near_r
    columns[pl.ds(1, rows, stride=2), :] = near_l
    columns[pl.ds(2 * rows, rows, stride=2), :] = moved(near_r, own[1], right(1), sr, nr, right)
    columns[pl.ds(2 * rows + 1, rows, stride=2), :] = moved(near_l, left(1), own[0], sl, nl, left)
    for k, row in enumerate((sr, sl, nr, nl)):
        columns[4 * rows + k : 4 * rows + k + 1, :] = row
    return columns[...].T


def mover(first, coefs, turned, rows):
    def beside(i):
        return pltpu.roll(turned, LANES - 2 * i - 1, 1)

    known = {}

    def once(g):
        if g not in known:
            i = 2 * rows if g < 0 else 2 * rows + 1 if g >= rows else g
            row, side = first(g)
            known[g] = row + side * beside(i)
        return known[g]

    def moved(g):
        row = inner_step(once(g), coefs, g) + coefs[2, g : g + 1, :] * once(g - 1)
        row = row + coefs[4, g : g + 1, :] * once(g + 1)
        return row + coefs[5, g : g + 1, :] * beside(rows + g)

    return moved


def storer(lows, out, stage, sem):
    copies = []

    def store(low, pair):
        p = lows.index(low)
        stage[2 * p] = pair[:, :LANES]
        stage[2 * p + 1] = pair[:, LANES:]
        copies.append(
            pltpu.make_async_copy(stage.at[pl.ds(2 * p, 2)], out.at[pl.ds(low, 2)], sem.at[p])
        )
        copies[-1].start()

    return store, copies


def finish(lows, moved, refs, out, stage, sem):
    store, copies = storer(lows, out, stage, sem)
    chemistry(lows, moved, store, *refs)
    for c in copies:
        c.wait()


def inner_kernel(
    once, coefs, of_pair, of_other, own,
    gather, products, losses, speeds, decay, sun, lit, out, stage, columns, sem,
):
    rows = once.shape[0]
    turned = side_columns(of_pair, of_other, own, None, columns)
    lows = list(range(rows // 4, rows - rows // 4, 2))
    moved = mover(lambda g: (once[g], coefs[5, g : g + 1, :]), coefs, turned, rows)
    finish(lows, moved, (decay, sun, lit, gather, products, losses, speeds), out, stage, sem)


def outer_kernel(
    once, coefs, of_pair, of_other, own, conc, of_near, of_next,
    gather, products, losses, speeds, decay, sun, lit, _, out, stage, columns, sem,
):
    rows, species, cells = conc.shape
    base = 2 * species
    band = lax.axis_index("lat")
    below = jnp.where(band > 0, 1.0, 0.0)
    above = jnp.where(band < lax.axis_size("lat") - 1, 1.0, 0.0)
    even_band = lax.rem(band, 2) == 0

    def of_south(span):
        return jnp.where(even_band, of_next[span, :], of_near[span, :])

    def of_north(span):
        return jnp.where(even_band, of_near[span, :], of_next[span, :])

    corners = [
        got(slice(base + 8 + k, base + 9 + k)) * inside
        for got, inside in ((of_south, below), (of_north, above))
        for k in range(2)
    ]
    turned = side_columns(of_pair, of_other, own, corners, columns)

    def halo(got, q, inside):
        return got(slice(q * species, (q + 1) * species)) * inside

    def across(got, k, inside):
        return got(slice(base + k, base + k + 1)) * inside

    def outside(got, near, far, beyond, home, back, inside):
        center = halo(got, near, inside)
        stay, west, east = [across(got, k, inside) for k in (0, 1, 3)]
        row = stay * center + west * pltpu.roll(center, 1, 1)
        row = row + east * pltpu.roll(center, cells - 1, 1)
        row = row + across(got, beyond, inside) * halo(got, far, inside)
        return row + across(got, back, inside) * home, across(got, 5, inside)

    def first(g):
        if g < 0:
            return outside(of_south, 1, 0, 2, conc[0], 4, below)
        if g >= rows:
            return outside(of_north, 0, 1, 4, conc[rows - 1], 2, above)
        row, side = once[g], coefs[5, g : g + 1, :]
        if g == 0:
            row = row + coefs[2, g : g + 1, :] * halo(of_south, 1, below)
        if g == rows - 1:
            row = row + coefs[4, g : g + 1, :] * halo(of_north, 0, above)
        return row, side

    lows = list(range(0, rows // 4, 2)) + list(range(rows - rows // 4, rows, 2))
    moved = mover(first, coefs, turned, rows)
    finish(lows, moved, (decay, sun, lit, gather, products, losses, speeds), out, stage, sem)


def local(conc, wind_lon, wind_lat, mixing, sun, rate, night_loss, stoich, plan):
    rows, species, cells = conc.shape
    reactions = rate.shape[0]
    lons = lax.axis_size("lon")
    lats = lax.axis_size("lat")
    params = pltpu.CompilerParams(vmem_limit_bytes=VMEM_LIMIT)
    vmem = pl.BlockSpec(memory_space=pltpu.VMEM)
    hbm = pl.BlockSpec(memory_space=pl.ANY)
    far = pl.BlockSpec(memory_space=pltpu.HBM)

    def pinned(x):
        return pltpu.with_memory_space_constraint(x, pltpu.HBM)

    def shape(*dims, dtype=f32):
        return KEPT(dims, dtype)

    side = shape(3, rows, species)
    ends = shape(2 * species + 16, cells)
    to_other, to_pair, own, to_next, to_near, held, coefs = pl.pallas_call(
        edge_kernel,
        out_shape=(
            side, side, shape(2, rows, species), ends, ends,
            shape(rows, species, cells), shape(6, rows, cells),
        ),
        in_specs=[far] * 4, out_specs=[vmem] * 7,
        scratch_shapes=[
            pltpu.VMEM((3, rows, cells), f32),
            pltpu.VMEM((cells, species), f32),
            pltpu.SemaphoreType.DMA((7,)),
        ],
        compiler_params=params, name="edges",
    )(*[pinned(x) for x in (conc, wind_lon, wind_lat, mixing)])

    pair = [(i, i ^ 1) for i in range(lons)]
    other = [(i, (i - 1) % lons if i % 2 == 0 else (i + 1) % lons) for i in range(lons)]
    near, after = [], []
    for b in range(lats):
        step_near, step_after = (1, -1) if b % 2 == 0 else (-1, 1)
        for perm, c in ((near, b + step_near), (after, b + step_after)):
            for i in range(lons):
                target = (c, i) if 0 <= c < lats else (b, i ^ 1)
                perm.append((b * lons + i, target[0] * lons + target[1]))
    of_other = lax.ppermute(to_other, "lon", other)
    of_pair = lax.ppermute(to_pair, "lon", pair)

    once, *tables = pl.pallas_call(
        table_kernel,
        out_shape=(
            shape(rows, species, cells),
            shape(2 * reactions, 2 * species, dtype=bf16),
            shape(species, 2 * reactions, dtype=bf16),
            shape(species, 6 * species, dtype=bf16),
            shape(reactions, LANES),
            shape(species, LANES),
            shape(rows, LANES),
            shape(SUBSTEPS, rows, LANES),
        ),
        in_specs=[vmem] * 2 + [far] * 5, out_specs=[vmem] * 8,
        scratch_shapes=[
            pltpu.VMEM(stoich.shape, jnp.int32),
            pltpu.VMEM((1, reactions), f32),
            pltpu.VMEM((plan.shape[0], plan.shape[2], plan.shape[1]), jnp.int32),
            pltpu.VMEM((1, species), f32),
            pltpu.VMEM((LANES, LANES), f32),
            pltpu.SemaphoreType.DMA((5,)),
        ],
        cost_estimate=pl.CostEstimate(flops=10**9, transcendentals=0, bytes_accessed=2 * 10**6),
        compiler_params=params, name="tables",
    )(
        held, coefs, pinned(stoich), pinned(rate.reshape(1, reactions)),
        pinned(jnp.swapaxes(plan, 1, 2)), pinned(night_loss.reshape(1, species)), pinned(sun),
    )

    to_next, to_near = pl.pallas_call(
        corner_kernel, out_shape=(ends, ends),
        in_specs=[vmem] * 2 + [hbm] * 3, out_specs=[hbm] * 2,
        scratch_shapes=[pltpu.VMEM((2, 8, species), f32), pltpu.SemaphoreType.DMA((2,))],
        input_output_aliases={2: 0, 3: 1},
        compiler_params=params, name="corners",
    )(of_other, of_pair, to_next, to_near, tables[5])
    of_next = lax.ppermute(to_next, ("lat", "lon"), after)
    of_near = lax.ppermute(to_near, ("lat", "lon"), near)

    shared = (once, coefs, of_pair, of_other, own)
    scratch = [
        pltpu.VMEM((rows // 2, species, cells), f32),
        pltpu.VMEM((LANES, species), f32),
        pltpu.SemaphoreType.DMA((rows // 4,)),
    ]
    inner = pl.pallas_call(
        inner_kernel, out_shape=jax.ShapeDtypeStruct(conc.shape, f32),
        in_specs=[vmem] * 12, out_specs=hbm, scratch_shapes=scratch,
        compiler_params=params, name="inner",
    )(*shared, *tables)
    return pl.pallas_call(
        outer_kernel, out_shape=jax.ShapeDtypeStruct(conc.shape, f32),
        in_specs=[vmem] * 15 + [hbm], out_specs=hbm, scratch_shapes=scratch,
        input_output_aliases={15: 0},
        compiler_params=params, name="outer",
    )(*shared, held, of_near, of_next, *tables, inner)


def solution(mesh):
    field = P("lat", None, "lon")
    cell = P("lat", "lon")
    return jax.shard_map(
        local,
        mesh=mesh,
        in_specs=(field, cell, cell, cell, P(), P(), P(), P(), P()),
        out_specs=field,
        check_vma=False,
    )
```

```python
import jax
import jax.numpy as jnp
from jax import lax
from jax.experimental import pallas as pl
from jax.experimental.pallas import tpu as pltpu
from jax.sharding import PartitionSpec as P

SUBSTEPS = 2
PICARD = 3
PHOT = 128
LANES = 128
VMEM_LIMIT = 48 << 20
KEPT = jax.ShapeDtypeStruct
CHUNK = 256
STAGGER = 2

f32 = jnp.float32
bf16 = jnp.bfloat16


def split(x):
    high = x.astype(bf16)
    return high, (x - high.astype(f32)).astype(bf16)


def twice(x):
    return jnp.concatenate([x, x], axis=1)


def dot(a, b):
    return jnp.dot(a, b, preferred_element_type=f32)


def iota(shape, axis):
    return lax.broadcasted_iota(jnp.int32, shape, axis)


def edge_kernel(
    conc_in, wlon_in, wlat_in, mix_in, to_other, to_pair, own, to_next, to_near, conc, coefs,
    winds, columns, sem,
):
    rows, species, cells = conc.shape
    fetches = [
        pltpu.make_async_copy(ref, winds.at[k], sem.at[k])
        for k, ref in enumerate((wlon_in, wlat_in, mix_in))
    ]
    part = rows // 4
    fetches += [
        pltpu.make_async_copy(
            conc_in.at[pl.ds(q * part, part)], conc.at[pl.ds(q * part, part)], sem.at[3 + q]
        )
        for q in range(4)
    ]
    for fetch in fetches:
        fetch.start()
    for fetch in fetches[:3]:
        fetch.wait()
    wlon, wlat, mix = [winds[k] for k in range(3)]
    place = iota((rows, cells), 1)
    stay = 1.0 - wlon - wlat - 4.0 * mix
    west, south = wlon + mix, wlat + mix
    coefs[0] = stay
    coefs[1] = jnp.where(place == 0, 0.0, west)
    coefs[2] = south
    coefs[3] = jnp.where(place == cells - 1, 0.0, mix)
    coefs[4] = mix
    coefs[5] = jnp.where(place == 0, west, jnp.where(place == cells - 1, mix, 0.0))
    even = lax.rem(lax.axis_index("lon"), 2) == 0

    def put(k, right, left):
        to_pair[k] = jnp.where(even, right, left)
        to_other[k] = jnp.where(even, left, right)

    right, left = jnp.zeros((rows, cells), f32), jnp.zeros((rows, cells), f32)
    for k, ref in enumerate((stay, west, south, mix)):
        right = jnp.where(place == k, ref[:, cells - 1 : cells], right)
        left = jnp.where(place == k, ref[:, 0:1], left)
    put(2, right, left)
    base = 2 * species
    pad = jnp.zeros((2, cells), f32)
    even_band = lax.rem(lax.axis_index("lat"), 2) == 0

    def send(span, north, south):
        to_near[span, :] = jnp.where(even_band, north, south)
        to_next[span, :] = jnp.where(even_band, south, north)

    send(
        slice(base, base + 8),
        *[
            jnp.concatenate([coefs[k, g : g + 1] for k in range(6)] + [pad])
            for g in (rows - 1, 0)
        ],
    )
    lane = iota((species, cells), 1)
    picked = jnp.zeros((species, cells), f32)
    for g in range(rows):
        if g % part == 0:
            fetches[3 + g // part].wait()
        turned = pltpu.roll(conc[g], (4 * g + 2) % cells, 1)
        picked = jnp.where((lane >= 4 * g) & (lane < 4 * g + 4), turned, picked)
    columns[...] = picked.T
    last2, last1, first1, first2 = [columns[pl.ds(q, rows, stride=4), :] for q in range(4)]
    put(0, last1, first1)
    put(1, last2, first2)
    own[0] = first1
    own[1] = last1
    for q in range(2):
        send(slice(q * species, (q + 1) * species), conc[rows - 2 + q], conc[q])


def sides(of_pair, of_other):
    even = lax.rem(lax.axis_index("lon"), 2) == 0
    return (
        lambda k: jnp.where(even, of_other[k], of_pair[k]),
        lambda k: jnp.where(even, of_pair[k], of_other[k]),
    )


def corner_kernel(of_other, of_pair, _, __, ___, to_next, to_near, ends, sem):
    rows = of_pair.shape[1]
    left, right = sides(of_pair, of_other)
    near_l, near_r = left(0), right(0)
    pad = jnp.zeros((6, near_l.shape[1]), f32)
    north, south = [
        jnp.concatenate([near_l[g : g + 1], near_r[g : g + 1], pad], axis=0) for g in (rows - 1, 0)
    ]
    even_band = lax.rem(lax.axis_index("lat"), 2) == 0
    ends[0] = jnp.where(even_band, south, north)
    ends[1] = jnp.where(even_band, north, south)
    copies = []
    for p, ref in enumerate((to_next, to_near)):
        dest = ref.at[pl.ds(ref.shape[0] - 8, 8), :]
        copies.append(pltpu.make_async_copy(ends.at[p], dest, sem.at[p]))
        copies[p].start()
    for c in copies:
        c.wait()


def table_kernel(
    conc, coefs, stoich_in, rate_in, plan_in, night_in, sun, once, gather, products, losses, speeds, decay, sun_own, lit,
    stoich, rate, plan, night, turned, sem,
):
    species = decay.shape[0]
    reactions = stoich_in.shape[1]
    rows = sun_own.shape[0]
    chunks = reactions // LANES
    band = lax.axis_index("lat")
    sector = lax.axis_index("lon")
    here = sun.at[
        pl.ds(pl.multiple_of(band * rows, 8), rows),
        pl.ds(pl.multiple_of(sector * LANES, LANES), LANES),
    ]
    moves = (
        (here, sun_own), (stoich_in, stoich), (rate_in, rate), (plan_in, plan), (night_in, night)
    )
    fetches = [pltpu.make_async_copy(a, b, sem.at[k]) for k, (a, b) in enumerate(moves)]
    for fetch in fetches:
        fetch.start()
    for g in range(rows):
        row = inner_step(conc[g], coefs, g)
        if g > 0:
            row = row + coefs[2, g : g + 1, :] * conc[g - 1]
        if g < rows - 1:
            row = row + coefs[4, g : g + 1, :] * conc[g + 1]
        once[g] = row
    for fetch in fetches:
        fetch.wait()
    down = iota((species, LANES), 0)
    across = iota((LANES, species), 1).astype(f32)
    mats = []
    for k in range(chunks):
        cols = pl.ds(k * LANES, LANES)
        codes = stoich[:, cols]
        row = rate[0:1, cols]
        small = jnp.concatenate([codes.astype(f32), row, jnp.zeros((3, LANES), f32)], axis=0).T
        hot = [(codes[q : q + 1, :] == down).astype(f32) for q in range(4)]
        seconds = None
        for q in range(2):
            picks = (small[:, q : q + 1] == across).astype(f32).astype(bf16)
            gather[pl.ds(q * reactions + k * LANES, LANES), :] = twice(picks)
            seconds = picks
        products[:, 2 * k * LANES : (2 * k + 2) * LANES] = twice((hot[2] + hot[3]).astype(bf16))
        speeds[pl.ds(k * LANES, LANES), :] = jnp.broadcast_to(small[:, 4:5], (LANES, LANES))
        parts = jnp.concatenate(split(hot[0] * row), axis=0)
        both = dot(parts, seconds)
        mats.append(both[:species] + both[species:])
    photo = sum(mats[1 : PHOT // LANES], mats[0])
    dark = sum(mats[PHOT // LANES + 1 :], mats[PHOT // LANES])
    for q, mat in enumerate((dark, photo)):
        high, low = split(mat + mat.T)
        losses[:, 2 * q * species : 2 * (q + 1) * species] = twice(high)
        losses[:, (4 + q) * species : (5 + q) * species] = low
    strip = []
    for s in range(SUBSTEPS):
        codes = plan[s]
        own = jnp.where(iota(codes.shape, 0) == sector, codes, 0).astype(f32)
        strip.append(jnp.sum(own, axis=0, keepdims=True))
    lats = plan.shape[2]
    flags = jnp.concatenate(strip + [jnp.zeros((8 - SUBSTEPS, lats), f32)], axis=0)
    flags = jnp.concatenate([flags, jnp.zeros((8, LANES - lats), f32)], axis=1)
    fade = jnp.exp(-night[...])
    spread = jnp.concatenate([flags, fade, jnp.zeros((7, LANES), f32)], axis=0).T
    decay[...] = jnp.broadcast_to(spread[:, 8:9], (species, LANES))
    for s in range(SUBSTEPS):
        turned[...] = jnp.broadcast_to(spread[:, s : s + 1], turned.shape)
        mine = turned[pl.ds(pl.multiple_of(band * rows, 8), rows), :]
        lit[s] = (mine >= -1.0).astype(f32)


def pair_steps(field, low, store, decay, sun, lit, gather, products, losses, speeds):
    reactions, species = speeds.shape[0], decay.shape[0]

    def both(ref):
        return jnp.concatenate([ref[low : low + 1, :], ref[low + 1 : low + 2, :]], axis=1)

    def begin(d):
        d["start"] = d["now"] = jnp.concatenate([field(low), field(low + 1)], axis=1)

    def prepare(d):
        photo = both(sun)
        high, low_part = split(d["now"])
        sun_high, sun_low = split(d["now"] * photo)
        d["weights"] = jnp.concatenate([high, low_part], axis=0)
        d["all"] = jnp.concatenate([high, low_part, sun_high, sun_low, high, sun_high], axis=0)
        d["made"] = []

    def lose(d):
        d["lost"] = dot(losses[...], d["all"])

    def react(k):
        def run(d):
            rows = slice(k * CHUNK, (k + 1) * CHUNK)
            later = slice(reactions + k * CHUNK, reactions + (k + 1) * CHUNK)
            first, second = dot(gather[rows, :], d["weights"]), dot(gather[later, :], d["weights"])
            for q in range(CHUNK // LANES):
                part = slice(q * LANES, (q + 1) * LANES)
                base = k * CHUNK + q * LANES
                flow = first[part] * twice(speeds[base : base + LANES, :]) * second[part]
                if base < PHOT:
                    flow = flow * both(sun)
                d["made"].extend(split(flow))

        return run

    def produce(d):
        d["produced"] = dot(products[...], jnp.concatenate(d["made"], axis=0))

    def close(s, last):
        def run(d):
            d["now"] = (d["start"] + d["produced"]) / (1.0 + d["lost"])
            if last:
                dark = d["start"] * twice(decay[...])
                d["now"] = d["start"] = jnp.where(both(lit.at[s]) > 0.0, d["now"], dark)

        return run

    steps = [begin]
    for s in range(SUBSTEPS):
        for sweep in range(PICARD):
            steps += [prepare, react(0), lose]
            steps += [react(k) for k in range(1, reactions // CHUNK)]
            steps += [produce, close(s, sweep == PICARD - 1)]
    steps.append(lambda d: store(low, d["now"]))
    return steps


def chemistry(lows, field, store, *refs):
    lists = [pair_steps(field, low, store, *refs) for low in lows]
    state = [{} for _ in lows]
    for t in range(len(lists[0]) + STAGGER * (len(lows) - 1)):
        for p, steps in enumerate(lists):
            at = t - STAGGER * p
            if 0 <= at < len(steps):
                steps[at](state[p])


def inner_step(center, coefs, g):
    cells = center.shape[1]
    stay, west, _, east = [coefs[k, g : g + 1, :] for k in range(4)]
    return stay * center + west * pltpu.roll(center, 1, 1) + east * pltpu.roll(center, cells - 1, 1)


def side_columns(of_pair, of_other, own, corners, columns):
    rows = of_pair.shape[1]
    left, right = sides(of_pair, of_other)
    near_l, near_r = left(0), right(0)
    zero = jnp.zeros((1, near_l.shape[1]), f32)
    sl, sr, nl, nr = corners if corners else (zero, zero, zero, zero)

    def moved(near, west, east, south, north, side):
        south = jnp.concatenate([south, near[:-1]], axis=0)
        north = jnp.concatenate([near[1:], north], axis=0)
        stay, w, s, e = [side(2)[:, k : k + 1] for k in range(4)]
        return stay * near + w * west + s * south + e * (east + north)

    columns[...] = jnp.zeros_like(columns)
    columns[pl.ds(0, rows, stride=2), :] = near_r
    columns[pl.ds(1, rows, stride=2), :] = near_l
    columns[pl.ds(2 * rows, rows, stride=2), :] = moved(near_r, own[1], right(1), sr, nr, right)
    columns[pl.ds(2 * rows + 1, rows, stride=2), :] = moved(near_l, left(1), own[0], sl, nl, left)
    for k, row in enumerate((sr, sl, nr, nl)):
        columns[4 * rows + k : 4 * rows + k + 1, :] = row
    return columns[...].T


def mover(first, coefs, turned, rows):
    def beside(i):
        return pltpu.roll(turned, LANES - 2 * i - 1, 1)

    known = {}

    def once(g):
        if g not in known:
            i = 2 * rows if g < 0 else 2 * rows + 1 if g >= rows else g
            row, side = first(g)
            known[g] = row + side * beside(i)
        return known[g]

    def moved(g):
        row = inner_step(once(g), coefs, g) + coefs[2, g : g + 1, :] * once(g - 1)
        row = row + coefs[4, g : g + 1, :] * once(g + 1)
        return row + coefs[5, g : g + 1, :] * beside(rows + g)

    return moved


def storer(lows, out, stage, sem):
    copies = []

    def store(low, pair):
        p = lows.index(low)
        stage[2 * p] = pair[:, :LANES]
        stage[2 * p + 1] = pair[:, LANES:]
        copies.append(
            pltpu.make_async_copy(stage.at[pl.ds(2 * p, 2)], out.at[pl.ds(low, 2)], sem.at[p])
        )
        copies[-1].start()

    return store, copies


def finish(lows, moved, refs, out, stage, sem):
    store, copies = storer(lows, out, stage, sem)
    chemistry(lows, moved, store, *refs)
    for c in copies:
        c.wait()


def inner_kernel(
    once, coefs, of_other, of_pair, own,
    gather, products, losses, speeds, decay, sun, lit, out, stage, columns, sem,
):
    rows = once.shape[0]
    turned = side_columns(of_pair, of_other, own, None, columns)
    lows = list(range(rows // 4, rows - rows // 4, 2))
    moved = mover(lambda g: (once[g], coefs[5, g : g + 1, :]), coefs, turned, rows)
    finish(lows, moved, (decay, sun, lit, gather, products, losses, speeds), out, stage, sem)


def outer_kernel(
    once, coefs, of_other, of_pair, own, conc, of_next, of_near,
    gather, products, losses, speeds, decay, sun, lit, _, out, stage, columns, sem,
):
    rows, species, cells = conc.shape
    base = 2 * species
    band = lax.axis_index("lat")
    below = jnp.where(band > 0, 1.0, 0.0)
    above = jnp.where(band < lax.axis_size("lat") - 1, 1.0, 0.0)
    even_band = lax.rem(band, 2) == 0

    def of_south(span):
        return jnp.where(even_band, of_next[span, :], of_near[span, :])

    def of_north(span):
        return jnp.where(even_band, of_near[span, :], of_next[span, :])

    corners = [
        got(slice(base + 8 + k, base + 9 + k)) * inside
        for got, inside in ((of_south, below), (of_north, above))
        for k in range(2)
    ]
    turned = side_columns(of_pair, of_other, own, corners, columns)

    def halo(got, q, inside):
        return got(slice(q * species, (q + 1) * species)) * inside

    def across(got, k, inside):
        return got(slice(base + k, base + k + 1)) * inside

    def outside(got, near, far, beyond, home, back, inside):
        center = halo(got, near, inside)
        stay, west, east = [across(got, k, inside) for k in (0, 1, 3)]
        row = stay * center + west * pltpu.roll(center, 1, 1)
        row = row + east * pltpu.roll(center, cells - 1, 1)
        row = row + across(got, beyond, inside) * halo(got, far, inside)
        return row + across(got, back, inside) * home, across(got, 5, inside)

    def first(g):
        if g < 0:
            return outside(of_south, 1, 0, 2, conc[0], 4, below)
        if g >= rows:
            return outside(of_north, 0, 1, 4, conc[rows - 1], 2, above)
        row, side = once[g], coefs[5, g : g + 1, :]
        if g == 0:
            row = row + coefs[2, g : g + 1, :] * halo(of_south, 1, below)
        if g == rows - 1:
            row = row + coefs[4, g : g + 1, :] * halo(of_north, 0, above)
        return row, side

    lows = list(range(0, rows // 4, 2)) + list(range(rows - rows // 4, rows, 2))
    moved = mover(first, coefs, turned, rows)
    finish(lows, moved, (decay, sun, lit, gather, products, losses, speeds), out, stage, sem)


def local(conc, wind_lon, wind_lat, mixing, sun, rate, night_loss, stoich, plan):
    rows, species, cells = conc.shape
    reactions = rate.shape[0]
    lons = lax.axis_size("lon")
    lats = lax.axis_size("lat")
    params = pltpu.CompilerParams(vmem_limit_bytes=VMEM_LIMIT)
    vmem = pl.BlockSpec(memory_space=pltpu.VMEM)
    hbm = pl.BlockSpec(memory_space=pl.ANY)
    far = pl.BlockSpec(memory_space=pltpu.HBM)

    def pinned(x):
        return pltpu.with_memory_space_constraint(x, pltpu.HBM)

    def shape(*dims, dtype=f32):
        return KEPT(dims, dtype)

    side = shape(3, rows, species)
    ends = shape(2 * species + 16, cells)
    to_other, to_pair, own, to_next, to_near, held, coefs = pl.pallas_call(
        edge_kernel,
        out_shape=(
            side, side, shape(2, rows, species), ends, ends,
            shape(rows, species, cells), shape(6, rows, cells),
        ),
        in_specs=[far] * 4, out_specs=[vmem] * 7,
        scratch_shapes=[
            pltpu.VMEM((3, rows, cells), f32),
            pltpu.VMEM((cells, species), f32),
            pltpu.SemaphoreType.DMA((7,)),
        ],
        compiler_params=params, name="edges",
    )(*[pinned(x) for x in (conc, wind_lon, wind_lat, mixing)])

    pair = [(i, i ^ 1) for i in range(lons)]
    other = [(i, (i - 1) % lons if i % 2 == 0 else (i + 1) % lons) for i in range(lons)]
    near, after = [], []
    for b in range(lats):
        step_near, step_after = (1, -1) if b % 2 == 0 else (-1, 1)
        for perm, c in ((near, b + step_near), (after, b + step_after)):
            for i in range(lons):
                target = (c, i) if 0 <= c < lats else (b, i ^ 1)
                perm.append((b * lons + i, target[0] * lons + target[1]))
    of_other = lax.ppermute(to_other, "lon", other)
    of_pair = lax.ppermute(to_pair, "lon", pair)

    once, *tables = pl.pallas_call(
        table_kernel,
        out_shape=(
            shape(rows, species, cells),
            shape(2 * reactions, 2 * species, dtype=bf16),
            shape(species, 2 * reactions, dtype=bf16),
            shape(species, 6 * species, dtype=bf16),
            shape(reactions, LANES),
            shape(species, LANES),
            shape(rows, LANES),
            shape(SUBSTEPS, rows, LANES),
        ),
        in_specs=[vmem] * 2 + [far] * 5, out_specs=[vmem] * 8,
        scratch_shapes=[
            pltpu.VMEM(stoich.shape, jnp.int32),
            pltpu.VMEM((1, reactions), f32),
            pltpu.VMEM((plan.shape[0], plan.shape[2], plan.shape[1]), jnp.int32),
            pltpu.VMEM((1, species), f32),
            pltpu.VMEM((LANES, LANES), f32),
            pltpu.SemaphoreType.DMA((5,)),
        ],
        cost_estimate=pl.CostEstimate(flops=10**9, transcendentals=0, bytes_accessed=2 * 10**6),
        compiler_params=params, name="tables",
    )(
        held, coefs, pinned(stoich), pinned(rate.reshape(1, reactions)),
        pinned(jnp.swapaxes(plan, 1, 2)), pinned(night_loss.reshape(1, species)), pinned(sun),
    )

    to_next, to_near = pl.pallas_call(
        corner_kernel, out_shape=(ends, ends),
        in_specs=[vmem] * 2 + [hbm] * 3, out_specs=[hbm] * 2,
        scratch_shapes=[pltpu.VMEM((2, 8, species), f32), pltpu.SemaphoreType.DMA((2,))],
        input_output_aliases={2: 0, 3: 1},
        compiler_params=params, name="corners",
    )(of_other, of_pair, to_next, to_near, tables[5])
    of_next = lax.ppermute(to_next, ("lat", "lon"), after)
    of_near = lax.ppermute(to_near, ("lat", "lon"), near)

    shared = (once, coefs, of_other, of_pair, own)
    scratch = [
        pltpu.VMEM((rows // 2, species, cells), f32),
        pltpu.VMEM((LANES, species), f32),
        pltpu.SemaphoreType.DMA((rows // 4,)),
    ]
    inner = pl.pallas_call(
        inner_kernel, out_shape=jax.ShapeDtypeStruct(conc.shape, f32),
        in_specs=[vmem] * 12, out_specs=hbm, scratch_shapes=scratch,
        compiler_params=params, name="inner",
    )(*shared, *tables)
    return pl.pallas_call(
        outer_kernel, out_shape=jax.ShapeDtypeStruct(conc.shape, f32),
        in_specs=[vmem] * 15 + [hbm], out_specs=hbm, scratch_shapes=scratch,
        input_output_aliases={15: 0},
        compiler_params=params, name="outer",
    )(*shared, held, of_next, of_near, *tables, inner)


def solution(mesh):
    field = P("lat", None, "lon")
    cell = P("lat", "lon")
    return jax.shard_map(
        local,
        mesh=mesh,
        in_specs=(field, cell, cell, cell, P(), P(), P(), P(), P()),
        out_specs=field,
        check_vma=False,
    )
```

```python
import jax
import jax.numpy as jnp
from jax import lax
from jax.experimental import pallas as pl
from jax.experimental.pallas import tpu as pltpu
from jax.sharding import PartitionSpec as P

SUBSTEPS = 2
PICARD = 3
PHOT = 128
LANES = 128
VMEM_LIMIT = 48 << 20
KEPT = jax.ShapeDtypeStruct
CHUNK = 256
STAGGER = 2

f32 = jnp.float32
bf16 = jnp.bfloat16


def split(x):
    high = x.astype(bf16)
    return high, (x - high.astype(f32)).astype(bf16)


def twice(x):
    return jnp.concatenate([x, x], axis=1)


def dot(a, b):
    return jnp.dot(a, b, preferred_element_type=f32)


def iota(shape, axis):
    return lax.broadcasted_iota(jnp.int32, shape, axis)


def edge_kernel(
    conc_in, wlon_in, wlat_in, mix_in, to_other, to_pair, own, to_next, to_near, conc, coefs,
    winds, columns, sem,
):
    rows, species, cells = conc.shape
    fetches = [
        pltpu.make_async_copy(ref, winds.at[k], sem.at[k])
        for k, ref in enumerate((wlon_in, wlat_in, mix_in))
    ]
    part = rows // 4
    fetches += [
        pltpu.make_async_copy(
            conc_in.at[pl.ds(q * part, part)], conc.at[pl.ds(q * part, part)], sem.at[3 + q]
        )
        for q in range(4)
    ]
    for fetch in fetches:
        fetch.start()
    for fetch in fetches[:3]:
        fetch.wait()
    wlon, wlat, mix = [winds[k] for k in range(3)]
    place = iota((rows, cells), 1)
    stay = 1.0 - wlon - wlat - 4.0 * mix
    west, south = wlon + mix, wlat + mix
    coefs[0] = stay
    coefs[1] = jnp.where(place == 0, 0.0, west)
    coefs[2] = south
    coefs[3] = jnp.where(place == cells - 1, 0.0, mix)
    coefs[4] = mix
    coefs[5] = jnp.where(place == 0, west, jnp.where(place == cells - 1, mix, 0.0))
    even = lax.rem(lax.axis_index("lon"), 2) == 0

    def put(k, right, left):
        to_pair[k] = jnp.where(even, right, left)
        to_other[k] = jnp.where(even, left, right)

    right, left = jnp.zeros((rows, cells), f32), jnp.zeros((rows, cells), f32)
    for k, ref in enumerate((stay, west, south, mix)):
        right = jnp.where(place == k, ref[:, cells - 1 : cells], right)
        left = jnp.where(place == k, ref[:, 0:1], left)
    put(2, right, left)
    base = 2 * species
    pad = jnp.zeros((2, cells), f32)
    even_band = lax.rem(lax.axis_index("lat"), 2) == 0

    def send(span, north, south):
        to_near[span, :] = jnp.where(even_band, north, south)
        to_next[span, :] = jnp.where(even_band, south, north)

    send(
        slice(base, base + 8),
        *[
            jnp.concatenate([coefs[k, g : g + 1] for k in range(6)] + [pad])
            for g in (rows - 1, 0)
        ],
    )
    lane = iota((species, cells), 1)
    picked = jnp.zeros((species, cells), f32)
    for g in range(rows):
        if g % part == 0:
            fetches[3 + g // part].wait()
        turned = pltpu.roll(conc[g], (4 * g + 2) % cells, 1)
        picked = jnp.where((lane >= 4 * g) & (lane < 4 * g + 4), turned, picked)
    columns[...] = picked.T
    last2, last1, first1, first2 = [columns[pl.ds(q, rows, stride=4), :] for q in range(4)]
    put(0, last1, first1)
    put(1, last2, first2)
    own[0] = first1
    own[1] = last1
    for q in range(2):
        send(slice(q * species, (q + 1) * species), conc[rows - 2 + q], conc[q])


def sides(of_pair, of_other):
    even = lax.rem(lax.axis_index("lon"), 2) == 0
    return (
        lambda k: jnp.where(even, of_other[k], of_pair[k]),
        lambda k: jnp.where(even, of_pair[k], of_other[k]),
    )


def corner_kernel(of_other, of_pair, _, __, ___, to_next, to_near, ends, sem):
    rows = of_pair.shape[1]
    left, right = sides(of_pair, of_other)
    near_l, near_r = left(0), right(0)
    pad = jnp.zeros((6, near_l.shape[1]), f32)
    north, south = [
        jnp.concatenate([near_l[g : g + 1], near_r[g : g + 1], pad], axis=0) for g in (rows - 1, 0)
    ]
    even_band = lax.rem(lax.axis_index("lat"), 2) == 0
    ends[0] = jnp.where(even_band, south, north)
    ends[1] = jnp.where(even_band, north, south)
    copies = []
    for p, ref in enumerate((to_next, to_near)):
        dest = ref.at[pl.ds(ref.shape[0] - 8, 8), :]
        copies.append(pltpu.make_async_copy(ends.at[p], dest, sem.at[p]))
        copies[p].start()
    for c in copies:
        c.wait()


def table_kernel(
    conc, coefs, stoich_in, rate_in, plan_in, night_in, sun, once, gather, products, losses, speeds, decay, sun_own, lit,
    stoich, rate, plan, night, turned, sem,
):
    species = decay.shape[0]
    reactions = stoich_in.shape[1]
    rows = sun_own.shape[0]
    chunks = reactions // LANES
    band = lax.axis_index("lat")
    sector = lax.axis_index("lon")
    here = sun.at[
        pl.ds(pl.multiple_of(band * rows, 8), rows),
        pl.ds(pl.multiple_of(sector * LANES, LANES), LANES),
    ]
    moves = (
        (here, sun_own), (stoich_in, stoich), (rate_in, rate), (plan_in, plan), (night_in, night)
    )
    fetches = [pltpu.make_async_copy(a, b, sem.at[k]) for k, (a, b) in enumerate(moves)]
    for fetch in fetches:
        fetch.start()
    for g in range(rows):
        row = inner_step(conc[g], coefs, g)
        if g > 0:
            row = row + coefs[2, g : g + 1, :] * conc[g - 1]
        if g < rows - 1:
            row = row + coefs[4, g : g + 1, :] * conc[g + 1]
        once[g] = row
    for fetch in fetches:
        fetch.wait()
    down = iota((species, LANES), 0)
    across = iota((LANES, species), 1).astype(f32)
    mats = []
    for k in range(chunks):
        cols = pl.ds(k * LANES, LANES)
        codes = stoich[:, cols]
        row = rate[0:1, cols]
        small = jnp.concatenate([codes.astype(f32), row, jnp.zeros((3, LANES), f32)], axis=0).T
        hot = [(codes[q : q + 1, :] == down).astype(f32) for q in range(4)]
        seconds = None
        for q in range(2):
            picks = (small[:, q : q + 1] == across).astype(f32).astype(bf16)
            gather[pl.ds(q * reactions + k * LANES, LANES), :] = twice(picks)
            seconds = picks
        products[:, 2 * k * LANES : (2 * k + 2) * LANES] = twice((hot[2] + hot[3]).astype(bf16))
        speeds[pl.ds(k * LANES, LANES), :] = jnp.broadcast_to(small[:, 4:5], (LANES, LANES))
        parts = jnp.concatenate(split(hot[0] * row), axis=0)
        both = dot(parts, seconds)
        mats.append(both[:species] + both[species:])
    photo = sum(mats[1 : PHOT // LANES], mats[0])
    dark = sum(mats[PHOT // LANES + 1 :], mats[PHOT // LANES])
    for q, mat in enumerate((dark, photo)):
        high, low = split(mat + mat.T)
        losses[:, 2 * q * species : 2 * (q + 1) * species] = twice(high)
        losses[:, (4 + q) * species : (5 + q) * species] = low
    strip = []
    for s in range(SUBSTEPS):
        codes = plan[s]
        own = jnp.where(iota(codes.shape, 0) == sector, codes, 0).astype(f32)
        strip.append(jnp.sum(own, axis=0, keepdims=True))
    lats = plan.shape[2]
    flags = jnp.concatenate(strip + [jnp.zeros((8 - SUBSTEPS, lats), f32)], axis=0)
    flags = jnp.concatenate([flags, jnp.zeros((8, LANES - lats), f32)], axis=1)
    fade = jnp.exp(-night[...])
    spread = jnp.concatenate([flags, fade, jnp.zeros((7, LANES), f32)], axis=0).T
    decay[...] = jnp.broadcast_to(spread[:, 8:9], (species, LANES))
    for s in range(SUBSTEPS):
        turned[...] = jnp.broadcast_to(spread[:, s : s + 1], turned.shape)
        mine = turned[pl.ds(pl.multiple_of(band * rows, 8), rows), :]
        lit[s] = (mine >= -1.0).astype(f32)


def pair_steps(field, low, store, decay, sun, lit, gather, products, losses, speeds):
    reactions, species = speeds.shape[0], decay.shape[0]

    def both(ref):
        return jnp.concatenate([ref[low : low + 1, :], ref[low + 1 : low + 2, :]], axis=1)

    def begin(d):
        d["start"] = d["now"] = jnp.concatenate([field(low), field(low + 1)], axis=1)

    def prepare(d):
        photo = both(sun)
        high, low_part = split(d["now"])
        sun_high, sun_low = split(d["now"] * photo)
        d["weights"] = jnp.concatenate([high, low_part], axis=0)
        d["all"] = jnp.concatenate([high, low_part, sun_high, sun_low, high, sun_high], axis=0)
        d["made"] = []

    def lose(d):
        d["lost"] = dot(losses[...], d["all"])

    def react(k):
        def run(d):
            rows = slice(k * CHUNK, (k + 1) * CHUNK)
            later = slice(reactions + k * CHUNK, reactions + (k + 1) * CHUNK)
            first, second = dot(gather[rows, :], d["weights"]), dot(gather[later, :], d["weights"])
            for q in range(CHUNK // LANES):
                part = slice(q * LANES, (q + 1) * LANES)
                base = k * CHUNK + q * LANES
                flow = first[part] * twice(speeds[base : base + LANES, :]) * second[part]
                if base < PHOT:
                    flow = flow * both(sun)
                d["made"].extend(split(flow))

        return run

    def produce(d):
        d["produced"] = dot(products[...], jnp.concatenate(d["made"], axis=0))

    def close(s, last):
        def run(d):
            d["now"] = (d["start"] + d["produced"]) / (1.0 + d["lost"])
            if last:
                dark = d["start"] * twice(decay[...])
                d["now"] = d["start"] = jnp.where(both(lit.at[s]) > 0.0, d["now"], dark)

        return run

    steps = [begin]
    for s in range(SUBSTEPS):
        for sweep in range(PICARD):
            steps += [prepare, react(0), lose]
            steps += [react(k) for k in range(1, reactions // CHUNK)]
            steps += [produce, close(s, sweep == PICARD - 1)]
    steps.append(lambda d: store(low, d["now"]))
    return steps


def chemistry(lows, field, store, *refs):
    lists = [pair_steps(field, low, store, *refs) for low in lows]
    state = [{} for _ in lows]
    for t in range(len(lists[0]) + STAGGER * (len(lows) - 1)):
        for p, steps in enumerate(lists):
            at = t - STAGGER * p
            if 0 <= at < len(steps):
                steps[at](state[p])


def inner_step(center, coefs, g):
    cells = center.shape[1]
    stay, west, _, east = [coefs[k, g : g + 1, :] for k in range(4)]
    return stay * center + west * pltpu.roll(center, 1, 1) + east * pltpu.roll(center, cells - 1, 1)


def side_columns(of_pair, of_other, own, corners, columns):
    rows = of_pair.shape[1]
    left, right = sides(of_pair, of_other)
    near_l, near_r = left(0), right(0)
    zero = jnp.zeros((1, near_l.shape[1]), f32)
    sl, sr, nl, nr = corners if corners else (zero, zero, zero, zero)

    def moved(near, west, east, south, north, side):
        south = jnp.concatenate([south, near[:-1]], axis=0)
        north = jnp.concatenate([near[1:], north], axis=0)
        stay, w, s, e = [side(2)[:, k : k + 1] for k in range(4)]
        return stay * near + w * west + s * south + e * (east + north)

    columns[...] = jnp.zeros_like(columns)
    columns[pl.ds(0, rows, stride=2), :] = near_r
    columns[pl.ds(1, rows, stride=2), :] = near_l
    columns[pl.ds(2 * rows, rows, stride=2), :] = moved(near_r, own[1], right(1), sr, nr, right)
    columns[pl.ds(2 * rows + 1, rows, stride=2), :] = moved(near_l, left(1), own[0], sl, nl, left)
    for k, row in enumerate((sr, sl, nr, nl)):
        columns[4 * rows + k : 4 * rows + k + 1, :] = row
    return columns[...].T


def mover(first, coefs, turned, rows):
    def beside(i):
        return pltpu.roll(turned, LANES - 2 * i - 1, 1)

    known = {}

    def once(g):
        if g not in known:
            i = 2 * rows if g < 0 else 2 * rows + 1 if g >= rows else g
            row, side = first(g)
            known[g] = row + side * beside(i)
        return known[g]

    def moved(g):
        row = inner_step(once(g), coefs, g) + coefs[2, g : g + 1, :] * once(g - 1)
        row = row + coefs[4, g : g + 1, :] * once(g + 1)
        return row + coefs[5, g : g + 1, :] * beside(rows + g)

    return moved


def storer(lows, out, stage, sem):
    copies = []

    def store(low, pair):
        p = lows.index(low)
        stage[2 * p] = pair[:, :LANES]
        stage[2 * p + 1] = pair[:, LANES:]
        copies.append(
            pltpu.make_async_copy(stage.at[pl.ds(2 * p, 2)], out.at[pl.ds(low, 2)], sem.at[p])
        )
        copies[-1].start()

    return store, copies


def finish(lows, moved, refs, out, stage, sem):
    store, copies = storer(lows, out, stage, sem)
    chemistry(lows, moved, store, *refs)
    for c in copies:
        c.wait()


def inner_kernel(
    once, coefs, of_other, of_pair, own,
    gather, products, losses, speeds, decay, sun, lit, out, stage, columns, sem,
):
    rows = once.shape[0]
    turned = side_columns(of_pair, of_other, own, None, columns)
    lows = list(range(rows // 4, rows - rows // 4, 2))
    moved = mover(lambda g: (once[g], coefs[5, g : g + 1, :]), coefs, turned, rows)
    finish(lows, moved, (decay, sun, lit, gather, products, losses, speeds), out, stage, sem)


def outer_kernel(
    once, coefs, of_other, of_pair, own, conc, of_near, of_next,
    gather, products, losses, speeds, decay, sun, lit, _, out, stage, columns, sem,
):
    rows, species, cells = conc.shape
    base = 2 * species
    band = lax.axis_index("lat")
    below = jnp.where(band > 0, 1.0, 0.0)
    above = jnp.where(band < lax.axis_size("lat") - 1, 1.0, 0.0)
    even_band = lax.rem(band, 2) == 0

    def of_south(span):
        return jnp.where(even_band, of_next[span, :], of_near[span, :])

    def of_north(span):
        return jnp.where(even_band, of_near[span, :], of_next[span, :])

    corners = [
        got(slice(base + 8 + k, base + 9 + k)) * inside
        for got, inside in ((of_south, below), (of_north, above))
        for k in range(2)
    ]
    turned = side_columns(of_pair, of_other, own, corners, columns)

    def halo(got, q, inside):
        return got(slice(q * species, (q + 1) * species)) * inside

    def across(got, k, inside):
        return got(slice(base + k, base + k + 1)) * inside

    def outside(got, near, far, beyond, home, back, inside):
        center = halo(got, near, inside)
        stay, west, east = [across(got, k, inside) for k in (0, 1, 3)]
        row = stay * center + west * pltpu.roll(center, 1, 1)
        row = row + east * pltpu.roll(center, cells - 1, 1)
        row = row + across(got, beyond, inside) * halo(got, far, inside)
        return row + across(got, back, inside) * home, across(got, 5, inside)

    def first(g):
        if g < 0:
            return outside(of_south, 1, 0, 2, conc[0], 4, below)
        if g >= rows:
            return outside(of_north, 0, 1, 4, conc[rows - 1], 2, above)
        row, side = once[g], coefs[5, g : g + 1, :]
        if g == 0:
            row = row + coefs[2, g : g + 1, :] * halo(of_south, 1, below)
        if g == rows - 1:
            row = row + coefs[4, g : g + 1, :] * halo(of_north, 0, above)
        return row, side

    lows = list(range(0, rows // 4, 2)) + list(range(rows - rows // 4, rows, 2))
    moved = mover(first, coefs, turned, rows)
    finish(lows, moved, (decay, sun, lit, gather, products, losses, speeds), out, stage, sem)


def local(conc, wind_lon, wind_lat, mixing, sun, rate, night_loss, stoich, plan):
    rows, species, cells = conc.shape
    reactions = rate.shape[0]
    lons = lax.axis_size("lon")
    lats = lax.axis_size("lat")
    params = pltpu.CompilerParams(vmem_limit_bytes=VMEM_LIMIT)
    vmem = pl.BlockSpec(memory_space=pltpu.VMEM)
    hbm = pl.BlockSpec(memory_space=pl.ANY)
    far = pl.BlockSpec(memory_space=pltpu.HBM)

    def pinned(x):
        return pltpu.with_memory_space_constraint(x, pltpu.HBM)

    def shape(*dims, dtype=f32):
        return KEPT(dims, dtype)

    side = shape(3, rows, species)
    ends = shape(2 * species + 16, cells)
    to_other, to_pair, own, to_next, to_near, held, coefs = pl.pallas_call(
        edge_kernel,
        out_shape=(
            side, side, shape(2, rows, species), ends, ends,
            shape(rows, species, cells), shape(6, rows, cells),
        ),
        in_specs=[far] * 4, out_specs=[vmem] * 7,
        scratch_shapes=[
            pltpu.VMEM((3, rows, cells), f32),
            pltpu.VMEM((cells, species), f32),
            pltpu.SemaphoreType.DMA((7,)),
        ],
        compiler_params=params, name="edges",
    )(*[pinned(x) for x in (conc, wind_lon, wind_lat, mixing)])

    pair = [(i, i ^ 1) for i in range(lons)]
    other = [(i, (i - 1) % lons if i % 2 == 0 else (i + 1) % lons) for i in range(lons)]
    near, after = [], []
    for b in range(lats):
        step_near, step_after = (1, -1) if b % 2 == 0 else (-1, 1)
        for perm, c in ((near, b + step_near), (after, b + step_after)):
            for i in range(lons):
                target = (c, i) if 0 <= c < lats else (b, i ^ 1)
                perm.append((b * lons + i, target[0] * lons + target[1]))
    of_other = lax.ppermute(to_other, "lon", other)
    of_pair = lax.ppermute(to_pair, "lon", pair)

    once, *tables = pl.pallas_call(
        table_kernel,
        out_shape=(
            shape(rows, species, cells),
            shape(2 * reactions, 2 * species, dtype=bf16),
            shape(species, 2 * reactions, dtype=bf16),
            shape(species, 6 * species, dtype=bf16),
            shape(reactions, LANES),
            shape(species, LANES),
            shape(rows, LANES),
            shape(SUBSTEPS, rows, LANES),
        ),
        in_specs=[vmem] * 2 + [far] * 5, out_specs=[vmem] * 8,
        scratch_shapes=[
            pltpu.VMEM(stoich.shape, jnp.int32),
            pltpu.VMEM((1, reactions), f32),
            pltpu.VMEM((plan.shape[0], plan.shape[2], plan.shape[1]), jnp.int32),
            pltpu.VMEM((1, species), f32),
            pltpu.VMEM((LANES, LANES), f32),
            pltpu.SemaphoreType.DMA((5,)),
        ],
        cost_estimate=pl.CostEstimate(flops=10**9, transcendentals=0, bytes_accessed=2 * 10**6),
        compiler_params=params, name="tables",
    )(
        held, coefs, pinned(stoich), pinned(rate.reshape(1, reactions)),
        pinned(jnp.swapaxes(plan, 1, 2)), pinned(night_loss.reshape(1, species)), pinned(sun),
    )

    to_next, to_near = pl.pallas_call(
        corner_kernel, out_shape=(ends, ends),
        in_specs=[vmem] * 2 + [hbm] * 3, out_specs=[hbm] * 2,
        scratch_shapes=[pltpu.VMEM((2, 8, species), f32), pltpu.SemaphoreType.DMA((2,))],
        input_output_aliases={2: 0, 3: 1},
        compiler_params=params, name="corners",
    )(of_other, of_pair, to_next, to_near, tables[5])
    of_next = lax.ppermute(to_next, ("lat", "lon"), after)
    of_near = lax.ppermute(to_near, ("lat", "lon"), near)

    shared = (once, coefs, of_other, of_pair, own)
    scratch = [
        pltpu.VMEM((rows // 2, species, cells), f32),
        pltpu.VMEM((LANES, species), f32),
        pltpu.SemaphoreType.DMA((rows // 4,)),
    ]
    inner = pl.pallas_call(
        inner_kernel, out_shape=jax.ShapeDtypeStruct(conc.shape, f32),
        in_specs=[vmem] * 12, out_specs=hbm, scratch_shapes=scratch,
        compiler_params=params, name="inner",
    )(*shared, *tables)
    return pl.pallas_call(
        outer_kernel, out_shape=jax.ShapeDtypeStruct(conc.shape, f32),
        in_specs=[vmem] * 15 + [hbm], out_specs=hbm, scratch_shapes=scratch,
        input_output_aliases={15: 0},
        compiler_params=params, name="outer",
    )(*shared, held, of_near, of_next, *tables, inner)


def solution(mesh):
    field = P("lat", None, "lon")
    cell = P("lat", "lon")
    return jax.shard_map(
        local,
        mesh=mesh,
        in_specs=(field, cell, cell, cell, P(), P(), P(), P(), P()),
        out_specs=field,
        check_vma=False,
    )
```

```python
import jax
import jax.numpy as jnp
from jax import lax
from jax.experimental import pallas as pl
from jax.experimental.pallas import tpu as pltpu
from jax.sharding import PartitionSpec as P

SUBSTEPS = 2
PICARD = 3
PHOT = 128
LANES = 128
VMEM_LIMIT = 48 << 20
KEPT = jax.ShapeDtypeStruct
CHUNK = 256
STAGGER = 2

f32 = jnp.float32
bf16 = jnp.bfloat16


def split(x):
    high = x.astype(bf16)
    return high, (x - high.astype(f32)).astype(bf16)


def twice(x):
    return jnp.concatenate([x, x], axis=1)


def dot(a, b):
    return jnp.dot(a, b, preferred_element_type=f32)


def iota(shape, axis):
    return lax.broadcasted_iota(jnp.int32, shape, axis)


def edge_kernel(
    conc_in, wlon_in, wlat_in, mix_in, stoich_in, rate_in, plan_in, night_in, sun,
    to_other, to_pair, own, to_next, to_near, conc, coefs,
    stoich, rate, plan, night, sun_own, winds, columns, sem,
):
    rows, species, cells = conc.shape
    fetches = [
        pltpu.make_async_copy(ref, winds.at[k], sem.at[k])
        for k, ref in enumerate((wlon_in, wlat_in, mix_in))
    ]
    part = rows // 4
    fetches += [
        pltpu.make_async_copy(
            conc_in.at[pl.ds(q * part, part)], conc.at[pl.ds(q * part, part)], sem.at[3 + q]
        )
        for q in range(4)
    ]
    here = sun.at[
        pl.ds(pl.multiple_of(lax.axis_index("lat") * rows, 8), rows),
        pl.ds(pl.multiple_of(lax.axis_index("lon") * cells, LANES), cells),
    ]
    small = (
        (stoich_in, stoich), (rate_in, rate), (plan_in, plan), (night_in, night), (here, sun_own)
    )
    fetches += [pltpu.make_async_copy(a, b, sem.at[7 + k]) for k, (a, b) in enumerate(small)]
    for fetch in fetches:
        fetch.start()
    for fetch in fetches[:3]:
        fetch.wait()
    wlon, wlat, mix = [winds[k] for k in range(3)]
    place = iota((rows, cells), 1)
    stay = 1.0 - wlon - wlat - 4.0 * mix
    west, south = wlon + mix, wlat + mix
    coefs[0] = stay
    coefs[1] = jnp.where(place == 0, 0.0, west)
    coefs[2] = south
    coefs[3] = jnp.where(place == cells - 1, 0.0, mix)
    coefs[4] = mix
    coefs[5] = jnp.where(place == 0, west, jnp.where(place == cells - 1, mix, 0.0))
    even = lax.rem(lax.axis_index("lon"), 2) == 0

    def put(k, right, left):
        to_pair[k] = jnp.where(even, right, left)
        to_other[k] = jnp.where(even, left, right)

    right, left = jnp.zeros((rows, cells), f32), jnp.zeros((rows, cells), f32)
    for k, ref in enumerate((stay, west, south, mix)):
        right = jnp.where(place == k, ref[:, cells - 1 : cells], right)
        left = jnp.where(place == k, ref[:, 0:1], left)
    put(2, right, left)
    base = 2 * species
    pad = jnp.zeros((2, cells), f32)
    even_band = lax.rem(lax.axis_index("lat"), 2) == 0

    def send(span, north, south):
        to_near[span, :] = jnp.where(even_band, north, south)
        to_next[span, :] = jnp.where(even_band, south, north)

    send(
        slice(base, base + 8),
        *[
            jnp.concatenate([coefs[k, g : g + 1] for k in range(6)] + [pad])
            for g in (rows - 1, 0)
        ],
    )
    lane = iota((species, cells), 1)
    picked = jnp.zeros((species, cells), f32)
    for g in range(rows):
        if g % part == 0:
            fetches[3 + g // part].wait()
        turned = pltpu.roll(conc[g], (4 * g + 2) % cells, 1)
        picked = jnp.where((lane >= 4 * g) & (lane < 4 * g + 4), turned, picked)
    columns[...] = picked.T
    last2, last1, first1, first2 = [columns[pl.ds(q, rows, stride=4), :] for q in range(4)]
    put(0, last1, first1)
    put(1, last2, first2)
    own[0] = first1
    own[1] = last1
    for q in range(2):
        send(slice(q * species, (q + 1) * species), conc[rows - 2 + q], conc[q])
    for fetch in fetches[7:]:
        fetch.wait()


def sides(of_pair, of_other):
    even = lax.rem(lax.axis_index("lon"), 2) == 0
    return (
        lambda k: jnp.where(even, of_other[k], of_pair[k]),
        lambda k: jnp.where(even, of_pair[k], of_other[k]),
    )


def corner_kernel(of_other, of_pair, _, __, ___, to_next, to_near, ends, sem):
    rows = of_pair.shape[1]
    left, right = sides(of_pair, of_other)
    near_l, near_r = left(0), right(0)
    pad = jnp.zeros((6, near_l.shape[1]), f32)
    north, south = [
        jnp.concatenate([near_l[g : g + 1], near_r[g : g + 1], pad], axis=0) for g in (rows - 1, 0)
    ]
    even_band = lax.rem(lax.axis_index("lat"), 2) == 0
    ends[0] = jnp.where(even_band, south, north)
    ends[1] = jnp.where(even_band, north, south)
    copies = []
    for p, ref in enumerate((to_next, to_near)):
        dest = ref.at[pl.ds(ref.shape[0] - 8, 8), :]
        copies.append(pltpu.make_async_copy(ends.at[p], dest, sem.at[p]))
        copies[p].start()
    for c in copies:
        c.wait()


def table_kernel(
    conc, coefs, stoich, rate, plan, night, once, gather, products, losses, speeds, decay, lit,
    turned,
):
    species = decay.shape[0]
    reactions = stoich.shape[1]
    rows = conc.shape[0]
    chunks = reactions // LANES
    band = lax.axis_index("lat")
    sector = lax.axis_index("lon")
    for g in range(rows):
        row = inner_step(conc[g], coefs, g)
        if g > 0:
            row = row + coefs[2, g : g + 1, :] * conc[g - 1]
        if g < rows - 1:
            row = row + coefs[4, g : g + 1, :] * conc[g + 1]
        once[g] = row
    down = iota((species, LANES), 0)
    across = iota((LANES, species), 1).astype(f32)
    mats = []
    for k in range(chunks):
        cols = pl.ds(k * LANES, LANES)
        codes = stoich[:, cols]
        row = rate[0:1, cols]
        small = jnp.concatenate([codes.astype(f32), row, jnp.zeros((3, LANES), f32)], axis=0).T
        hot = [(codes[q : q + 1, :] == down).astype(f32) for q in range(4)]
        seconds = None
        for q in range(2):
            picks = (small[:, q : q + 1] == across).astype(f32).astype(bf16)
            gather[pl.ds(q * reactions + k * LANES, LANES), :] = twice(picks)
            seconds = picks
        products[:, 2 * k * LANES : (2 * k + 2) * LANES] = twice((hot[2] + hot[3]).astype(bf16))
        speeds[pl.ds(k * LANES, LANES), :] = jnp.broadcast_to(small[:, 4:5], (LANES, LANES))
        parts = jnp.concatenate(split(hot[0] * row), axis=0)
        both = dot(parts, seconds)
        mats.append(both[:species] + both[species:])
    photo = sum(mats[1 : PHOT // LANES], mats[0])
    dark = sum(mats[PHOT // LANES + 1 :], mats[PHOT // LANES])
    for q, mat in enumerate((dark, photo)):
        high, low = split(mat + mat.T)
        losses[:, 2 * q * species : 2 * (q + 1) * species] = twice(high)
        losses[:, (4 + q) * species : (5 + q) * species] = low
    strip = []
    for s in range(SUBSTEPS):
        codes = plan[s]
        own = jnp.where(iota(codes.shape, 0) == sector, codes, 0).astype(f32)
        strip.append(jnp.sum(own, axis=0, keepdims=True))
    lats = plan.shape[2]
    flags = jnp.concatenate(strip + [jnp.zeros((8 - SUBSTEPS, lats), f32)], axis=0)
    flags = jnp.concatenate([flags, jnp.zeros((8, LANES - lats), f32)], axis=1)
    fade = jnp.exp(-night[...])
    spread = jnp.concatenate([flags, fade, jnp.zeros((7, LANES), f32)], axis=0).T
    decay[...] = jnp.broadcast_to(spread[:, 8:9], (species, LANES))
    for s in range(SUBSTEPS):
        turned[...] = jnp.broadcast_to(spread[:, s : s + 1], turned.shape)
        mine = turned[pl.ds(pl.multiple_of(band * rows, 8), rows), :]
        lit[s] = (mine >= -1.0).astype(f32)


def pair_steps(field, low, store, decay, sun, lit, gather, products, losses, speeds):
    reactions, species = speeds.shape[0], decay.shape[0]

    def both(ref):
        return jnp.concatenate([ref[low : low + 1, :], ref[low + 1 : low + 2, :]], axis=1)

    def begin(d):
        d["start"] = d["now"] = jnp.concatenate([field(low), field(low + 1)], axis=1)

    def prepare(d):
        photo = both(sun)
        high, low_part = split(d["now"])
        sun_high, sun_low = split(d["now"] * photo)
        d["weights"] = jnp.concatenate([high, low_part], axis=0)
        d["all"] = jnp.concatenate([high, low_part, sun_high, sun_low, high, sun_high], axis=0)
        d["made"] = []

    def lose(d):
        d["lost"] = dot(losses[...], d["all"])

    def react(k):
        def run(d):
            rows = slice(k * CHUNK, (k + 1) * CHUNK)
            later = slice(reactions + k * CHUNK, reactions + (k + 1) * CHUNK)
            first, second = dot(gather[rows, :], d["weights"]), dot(gather[later, :], d["weights"])
            for q in range(CHUNK // LANES):
                part = slice(q * LANES, (q + 1) * LANES)
                base = k * CHUNK + q * LANES
                flow = first[part] * twice(speeds[base : base + LANES, :]) * second[part]
                if base < PHOT:
                    flow = flow * both(sun)
                d["made"].extend(split(flow))

        return run

    def produce(d):
        d["produced"] = dot(products[...], jnp.concatenate(d["made"], axis=0))

    def close(s, last):
        def run(d):
            d["now"] = (d["start"] + d["produced"]) / (1.0 + d["lost"])
            if last:
                dark = d["start"] * twice(decay[...])
                d["now"] = d["start"] = jnp.where(both(lit.at[s]) > 0.0, d["now"], dark)

        return run

    steps = [begin]
    for s in range(SUBSTEPS):
        for sweep in range(PICARD):
            steps += [prepare, react(0), lose]
            steps += [react(k) for k in range(1, reactions // CHUNK)]
            steps += [produce, close(s, sweep == PICARD - 1)]
    steps.append(lambda d: store(low, d["now"]))
    return steps


def chemistry(lows, field, store, *refs):
    lists = [pair_steps(field, low, store, *refs) for low in lows]
    state = [{} for _ in lows]
    for t in range(len(lists[0]) + STAGGER * (len(lows) - 1)):
        for p, steps in enumerate(lists):
            at = t - STAGGER * p
            if 0 <= at < len(steps):
                steps[at](state[p])


def inner_step(center, coefs, g):
    cells = center.shape[1]
    stay, west, _, east = [coefs[k, g : g + 1, :] for k in range(4)]
    return stay * center + west * pltpu.roll(center, 1, 1) + east * pltpu.roll(center, cells - 1, 1)


def side_columns(of_pair, of_other, own, corners, columns):
    rows = of_pair.shape[1]
    left, right = sides(of_pair, of_other)
    near_l, near_r = left(0), right(0)
    zero = jnp.zeros((1, near_l.shape[1]), f32)
    sl, sr, nl, nr = corners if corners else (zero, zero, zero, zero)

    def moved(near, west, east, south, north, side):
        south = jnp.concatenate([south, near[:-1]], axis=0)
        north = jnp.concatenate([near[1:], north], axis=0)
        stay, w, s, e = [side(2)[:, k : k + 1] for k in range(4)]
        return stay * near + w * west + s * south + e * (east + north)

    columns[...] = jnp.zeros_like(columns)
    columns[pl.ds(0, rows, stride=2), :] = near_r
    columns[pl.ds(1, rows, stride=2), :] = near_l
    columns[pl.ds(2 * rows, rows, stride=2), :] = moved(near_r, own[1], right(1), sr, nr, right)
    columns[pl.ds(2 * rows + 1, rows, stride=2), :] = moved(near_l, left(1), own[0], sl, nl, left)
    for k, row in enumerate((sr, sl, nr, nl)):
        columns[4 * rows + k : 4 * rows + k + 1, :] = row
    return columns[...].T


def mover(first, coefs, turned, rows):
    def beside(i):
        return pltpu.roll(turned, LANES - 2 * i - 1, 1)

    known = {}

    def once(g):
        if g not in known:
            i = 2 * rows if g < 0 else 2 * rows + 1 if g >= rows else g
            row, side = first(g)
            known[g] = row + side * beside(i)
        return known[g]

    def moved(g):
        row = inner_step(once(g), coefs, g) + coefs[2, g : g + 1, :] * once(g - 1)
        row = row + coefs[4, g : g + 1, :] * once(g + 1)
        return row + coefs[5, g : g + 1, :] * beside(rows + g)

    return moved


def storer(lows, out, stage, sem):
    copies = []

    def store(low, pair):
        p = lows.index(low)
        stage[2 * p] = pair[:, :LANES]
        stage[2 * p + 1] = pair[:, LANES:]
        copies.append(
            pltpu.make_async_copy(stage.at[pl.ds(2 * p, 2)], out.at[pl.ds(low, 2)], sem.at[p])
        )
        copies[-1].start()

    return store, copies


def finish(lows, moved, refs, out, stage, sem):
    store, copies = storer(lows, out, stage, sem)
    chemistry(lows, moved, store, *refs)
    for c in copies:
        c.wait()


def inner_kernel(
    once, coefs, of_other, of_pair, own,
    gather, products, losses, speeds, decay, sun, lit, out, stage, columns, sem,
):
    rows = once.shape[0]
    turned = side_columns(of_pair, of_other, own, None, columns)
    lows = list(range(rows // 4, rows - rows // 4, 2))
    moved = mover(lambda g: (once[g], coefs[5, g : g + 1, :]), coefs, turned, rows)
    finish(lows, moved, (decay, sun, lit, gather, products, losses, speeds), out, stage, sem)


def outer_kernel(
    once, coefs, of_other, of_pair, own, conc, of_near, of_next,
    gather, products, losses, speeds, decay, sun, lit, _, out, stage, columns, sem,
):
    rows, species, cells = conc.shape
    base = 2 * species
    band = lax.axis_index("lat")
    below = jnp.where(band > 0, 1.0, 0.0)
    above = jnp.where(band < lax.axis_size("lat") - 1, 1.0, 0.0)
    even_band = lax.rem(band, 2) == 0

    def of_south(span):
        return jnp.where(even_band, of_next[span, :], of_near[span, :])

    def of_north(span):
        return jnp.where(even_band, of_near[span, :], of_next[span, :])

    corners = [
        got(slice(base + 8 + k, base + 9 + k)) * inside
        for got, inside in ((of_south, below), (of_north, above))
        for k in range(2)
    ]
    turned = side_columns(of_pair, of_other, own, corners, columns)

    def halo(got, q, inside):
        return got(slice(q * species, (q + 1) * species)) * inside

    def across(got, k, inside):
        return got(slice(base + k, base + k + 1)) * inside

    def outside(got, near, far, beyond, home, back, inside):
        center = halo(got, near, inside)
        stay, west, east = [across(got, k, inside) for k in (0, 1, 3)]
        row = stay * center + west * pltpu.roll(center, 1, 1)
        row = row + east * pltpu.roll(center, cells - 1, 1)
        row = row + across(got, beyond, inside) * halo(got, far, inside)
        return row + across(got, back, inside) * home, across(got, 5, inside)

    def first(g):
        if g < 0:
            return outside(of_south, 1, 0, 2, conc[0], 4, below)
        if g >= rows:
            return outside(of_north, 0, 1, 4, conc[rows - 1], 2, above)
        row, side = once[g], coefs[5, g : g + 1, :]
        if g == 0:
            row = row + coefs[2, g : g + 1, :] * halo(of_south, 1, below)
        if g == rows - 1:
            row = row + coefs[4, g : g + 1, :] * halo(of_north, 0, above)
        return row, side

    lows = list(range(0, rows // 4, 2)) + list(range(rows - rows // 4, rows, 2))
    moved = mover(first, coefs, turned, rows)
    finish(lows, moved, (decay, sun, lit, gather, products, losses, speeds), out, stage, sem)


def local(conc, wind_lon, wind_lat, mixing, sun, rate, night_loss, stoich, plan):
    rows, species, cells = conc.shape
    reactions = rate.shape[0]
    lons = lax.axis_size("lon")
    lats = lax.axis_size("lat")
    params = pltpu.CompilerParams(vmem_limit_bytes=VMEM_LIMIT)
    vmem = pl.BlockSpec(memory_space=pltpu.VMEM)
    hbm = pl.BlockSpec(memory_space=pl.ANY)
    far = pl.BlockSpec(memory_space=pltpu.HBM)

    def pinned(x):
        return pltpu.with_memory_space_constraint(x, pltpu.HBM)

    def shape(*dims, dtype=f32):
        return KEPT(dims, dtype)

    side = shape(3, rows, species)
    ends = shape(2 * species + 16, cells)
    to_other, to_pair, own, to_next, to_near, held, coefs, *small, sun_own = pl.pallas_call(
        edge_kernel,
        out_shape=(
            side, side, shape(2, rows, species), ends, ends,
            shape(rows, species, cells), shape(6, rows, cells),
            shape(*stoich.shape, dtype=jnp.int32), shape(1, reactions),
            shape(plan.shape[0], plan.shape[2], plan.shape[1], dtype=jnp.int32),
            shape(1, species), shape(rows, cells),
        ),
        in_specs=[far] * 9, out_specs=[vmem] * 12,
        scratch_shapes=[
            pltpu.VMEM((3, rows, cells), f32),
            pltpu.VMEM((cells, species), f32),
            pltpu.SemaphoreType.DMA((12,)),
        ],
        compiler_params=params, name="edges",
    )(
        *[
            pinned(x)
            for x in (
                conc, wind_lon, wind_lat, mixing, stoich, rate.reshape(1, reactions),
                jnp.swapaxes(plan, 1, 2), night_loss.reshape(1, species), sun,
            )
        ]
    )

    pair = [(i, i ^ 1) for i in range(lons)]
    other = [(i, (i - 1) % lons if i % 2 == 0 else (i + 1) % lons) for i in range(lons)]
    near, after = [], []
    for b in range(lats):
        step_near, step_after = (1, -1) if b % 2 == 0 else (-1, 1)
        for perm, c in ((near, b + step_near), (after, b + step_after)):
            for i in range(lons):
                target = (c, i) if 0 <= c < lats else (b, i ^ 1)
                perm.append((b * lons + i, target[0] * lons + target[1]))
    of_other = lax.ppermute(to_other, "lon", other)
    of_pair = lax.ppermute(to_pair, "lon", pair)

    once, *tables = pl.pallas_call(
        table_kernel,
        out_shape=(
            shape(rows, species, cells),
            shape(2 * reactions, 2 * species, dtype=bf16),
            shape(species, 2 * reactions, dtype=bf16),
            shape(species, 6 * species, dtype=bf16),
            shape(reactions, LANES),
            shape(species, LANES),
            shape(SUBSTEPS, rows, LANES),
        ),
        in_specs=[vmem] * 6, out_specs=[vmem] * 7,
        scratch_shapes=[
            pltpu.VMEM((LANES, LANES), f32),
        ],
        cost_estimate=pl.CostEstimate(flops=10**9, transcendentals=0, bytes_accessed=2 * 10**6),
        compiler_params=params, name="tables",
    )(
        held, coefs, *small,
    )

    to_next, to_near = pl.pallas_call(
        corner_kernel, out_shape=(ends, ends),
        in_specs=[vmem] * 2 + [hbm] * 3, out_specs=[hbm] * 2,
        scratch_shapes=[pltpu.VMEM((2, 8, species), f32), pltpu.SemaphoreType.DMA((2,))],
        input_output_aliases={2: 0, 3: 1},
        compiler_params=params, name="corners",
    )(of_other, of_pair, to_next, to_near, tables[-1])
    of_next = lax.ppermute(to_next, ("lat", "lon"), after)
    of_near = lax.ppermute(to_near, ("lat", "lon"), near)

    tables.insert(5, sun_own)
    shared = (once, coefs, of_other, of_pair, own)
    scratch = [
        pltpu.VMEM((rows // 2, species, cells), f32),
        pltpu.VMEM((LANES, species), f32),
        pltpu.SemaphoreType.DMA((rows // 4,)),
    ]
    inner = pl.pallas_call(
        inner_kernel, out_shape=jax.ShapeDtypeStruct(conc.shape, f32),
        in_specs=[vmem] * 12, out_specs=hbm, scratch_shapes=scratch,
        compiler_params=params, name="inner",
    )(*shared, *tables)
    return pl.pallas_call(
        outer_kernel, out_shape=jax.ShapeDtypeStruct(conc.shape, f32),
        in_specs=[vmem] * 15 + [hbm], out_specs=hbm, scratch_shapes=scratch,
        input_output_aliases={15: 0},
        compiler_params=params, name="outer",
    )(*shared, held, of_near, of_next, *tables, inner)


def solution(mesh):
    field = P("lat", None, "lon")
    cell = P("lat", "lon")
    return jax.shard_map(
        local,
        mesh=mesh,
        in_specs=(field, cell, cell, cell, P(), P(), P(), P(), P()),
        out_specs=field,
        check_vma=False,
    )
```

```python
import jax
import jax.numpy as jnp
from jax import lax
from jax.experimental import pallas as pl
from jax.experimental.pallas import tpu as pltpu
from jax.sharding import PartitionSpec as P

SUBSTEPS = 2
PICARD = 3
PHOT = 128
LANES = 128
VMEM_LIMIT = 48 << 20
KEPT = jax.ShapeDtypeStruct
CHUNK = 512
STAGGER = 1

f32 = jnp.float32
bf16 = jnp.bfloat16


def split(x):
    high = x.astype(bf16)
    return high, (x - high.astype(f32)).astype(bf16)


def twice(x):
    return jnp.concatenate([x, x], axis=1)


def dot(a, b):
    return jnp.dot(a, b, preferred_element_type=f32)


def iota(shape, axis):
    return lax.broadcasted_iota(jnp.int32, shape, axis)


def edge_kernel(
    conc_in, wlon_in, wlat_in, mix_in, to_other, to_pair, own, to_next, to_near, conc, coefs,
    winds, columns, sem,
):
    rows, species, cells = conc.shape
    fetches = [
        pltpu.make_async_copy(ref, winds.at[k], sem.at[k])
        for k, ref in enumerate((wlon_in, wlat_in, mix_in))
    ]
    part = rows // 4
    fetches += [
        pltpu.make_async_copy(
            conc_in.at[pl.ds(q * part, part)], conc.at[pl.ds(q * part, part)], sem.at[3 + q]
        )
        for q in range(4)
    ]
    for fetch in fetches:
        fetch.start()
    for fetch in fetches[:3]:
        fetch.wait()
    wlon, wlat, mix = [winds[k] for k in range(3)]
    place = iota((rows, cells), 1)
    stay = 1.0 - wlon - wlat - 4.0 * mix
    west, south = wlon + mix, wlat + mix
    coefs[0] = stay
    coefs[1] = jnp.where(place == 0, 0.0, west)
    coefs[2] = south
    coefs[3] = jnp.where(place == cells - 1, 0.0, mix)
    coefs[4] = mix
    coefs[5] = jnp.where(place == 0, west, jnp.where(place == cells - 1, mix, 0.0))
    even = lax.rem(lax.axis_index("lon"), 2) == 0

    def put(k, right, left):
        to_pair[k] = jnp.where(even, right, left)
        to_other[k] = jnp.where(even, left, right)

    right, left = jnp.zeros((rows, cells), f32), jnp.zeros((rows, cells), f32)
    for k, ref in enumerate((stay, west, south, mix)):
        right = jnp.where(place == k, ref[:, cells - 1 : cells], right)
        left = jnp.where(place == k, ref[:, 0:1], left)
    put(2, right, left)
    base = 2 * species
    pad = jnp.zeros((2, cells), f32)
    even_band = lax.rem(lax.axis_index("lat"), 2) == 0

    def send(span, north, south):
        to_near[span, :] = jnp.where(even_band, north, south)
        to_next[span, :] = jnp.where(even_band, south, north)

    send(
        slice(base, base + 8),
        *[
            jnp.concatenate([coefs[k, g : g + 1] for k in range(6)] + [pad])
            for g in (rows - 1, 0)
        ],
    )
    lane = iota((species, cells), 1)
    picked = jnp.zeros((species, cells), f32)
    for g in range(rows):
        if g % part == 0:
            fetches[3 + g // part].wait()
        turned = pltpu.roll(conc[g], (4 * g + 2) % cells, 1)
        picked = jnp.where((lane >= 4 * g) & (lane < 4 * g + 4), turned, picked)
    columns[...] = picked.T
    last2, last1, first1, first2 = [columns[pl.ds(q, rows, stride=4), :] for q in range(4)]
    put(0, last1, first1)
    put(1, last2, first2)
    own[0] = first1
    own[1] = last1
    for q in range(2):
        send(slice(q * species, (q + 1) * species), conc[rows - 2 + q], conc[q])


def sides(of_pair, of_other):
    even = lax.rem(lax.axis_index("lon"), 2) == 0
    return (
        lambda k: jnp.where(even, of_other[k], of_pair[k]),
        lambda k: jnp.where(even, of_pair[k], of_other[k]),
    )


def corner_kernel(of_other, of_pair, _, __, ___, to_next, to_near, ends, sem):
    rows = of_pair.shape[1]
    left, right = sides(of_pair, of_other)
    near_l, near_r = left(0), right(0)
    pad = jnp.zeros((6, near_l.shape[1]), f32)
    north, south = [
        jnp.concatenate([near_l[g : g + 1], near_r[g : g + 1], pad], axis=0) for g in (rows - 1, 0)
    ]
    even_band = lax.rem(lax.axis_index("lat"), 2) == 0
    ends[0] = jnp.where(even_band, south, north)
    ends[1] = jnp.where(even_band, north, south)
    copies = []
    for p, ref in enumerate((to_next, to_near)):
        dest = ref.at[pl.ds(ref.shape[0] - 8, 8), :]
        copies.append(pltpu.make_async_copy(ends.at[p], dest, sem.at[p]))
        copies[p].start()
    for c in copies:
        c.wait()


def table_kernel(
    conc, coefs, stoich_in, rate_in, plan_in, night_in, sun, once, gather, products, losses, speeds, decay, sun_own, lit,
    stoich, rate, plan, night, turned, sem,
):
    species = decay.shape[0]
    reactions = stoich_in.shape[1]
    rows = sun_own.shape[0]
    chunks = reactions // LANES
    band = lax.axis_index("lat")
    sector = lax.axis_index("lon")
    here = sun.at[
        pl.ds(pl.multiple_of(band * rows, 8), rows),
        pl.ds(pl.multiple_of(sector * LANES, LANES), LANES),
    ]
    moves = (
        (here, sun_own), (stoich_in, stoich), (rate_in, rate), (plan_in, plan), (night_in, night)
    )
    fetches = [pltpu.make_async_copy(a, b, sem.at[k]) for k, (a, b) in enumerate(moves)]
    for fetch in fetches:
        fetch.start()
    for g in range(rows):
        row = inner_step(conc[g], coefs, g)
        if g > 0:
            row = row + coefs[2, g : g + 1, :] * conc[g - 1]
        if g < rows - 1:
            row = row + coefs[4, g : g + 1, :] * conc[g + 1]
        once[g] = row
    for fetch in fetches:
        fetch.wait()
    down = iota((species, LANES), 0)
    across = iota((LANES, species), 1).astype(f32)
    mats = []
    for k in range(chunks):
        cols = pl.ds(k * LANES, LANES)
        codes = stoich[:, cols]
        row = rate[0:1, cols]
        small = jnp.concatenate([codes.astype(f32), row, jnp.zeros((3, LANES), f32)], axis=0).T
        hot = [(codes[q : q + 1, :] == down).astype(f32) for q in range(4)]
        seconds = None
        for q in range(2):
            picks = (small[:, q : q + 1] == across).astype(f32).astype(bf16)
            gather[pl.ds(q * reactions + k * LANES, LANES), :] = twice(picks)
            seconds = picks
        products[:, 2 * k * LANES : (2 * k + 2) * LANES] = twice((hot[2] + hot[3]).astype(bf16))
        speeds[pl.ds(k * LANES, LANES), :] = jnp.broadcast_to(small[:, 4:5], (LANES, LANES))
        parts = jnp.concatenate(split(hot[0] * row), axis=0)
        both = dot(parts, seconds)
        mats.append(both[:species] + both[species:])
    photo = sum(mats[1 : PHOT // LANES], mats[0])
    dark = sum(mats[PHOT // LANES + 1 :], mats[PHOT // LANES])
    for q, mat in enumerate((dark, photo)):
        high, low = split(mat + mat.T)
        losses[:, 2 * q * species : 2 * (q + 1) * species] = twice(high)
        losses[:, (4 + q) * species : (5 + q) * species] = low
    strip = []
    for s in range(SUBSTEPS):
        codes = plan[s]
        own = jnp.where(iota(codes.shape, 0) == sector, codes, 0).astype(f32)
        strip.append(jnp.sum(own, axis=0, keepdims=True))
    lats = plan.shape[2]
    flags = jnp.concatenate(strip + [jnp.zeros((8 - SUBSTEPS, lats), f32)], axis=0)
    flags = jnp.concatenate([flags, jnp.zeros((8, LANES - lats), f32)], axis=1)
    fade = jnp.exp(-night[...])
    spread = jnp.concatenate([flags, fade, jnp.zeros((7, LANES), f32)], axis=0).T
    decay[...] = jnp.broadcast_to(spread[:, 8:9], (species, LANES))
    for s in range(SUBSTEPS):
        turned[...] = jnp.broadcast_to(spread[:, s : s + 1], turned.shape)
        mine = turned[pl.ds(pl.multiple_of(band * rows, 8), rows), :]
        lit[s] = (mine >= -1.0).astype(f32)


def pair_steps(field, low, store, decay, sun, lit, gather, products, losses, speeds):
    reactions, species = speeds.shape[0], decay.shape[0]

    def both(ref):
        return jnp.concatenate([ref[low : low + 1, :], ref[low + 1 : low + 2, :]], axis=1)

    def begin(d):
        d["start"] = d["now"] = jnp.concatenate([field(low), field(low + 1)], axis=1)

    def prepare(d):
        photo = both(sun)
        high, low_part = split(d["now"])
        sun_high, sun_low = split(d["now"] * photo)
        d["weights"] = jnp.concatenate([high, low_part], axis=0)
        d["all"] = jnp.concatenate([high, low_part, sun_high, sun_low, high, sun_high], axis=0)
        d["made"] = []

    def lose(d):
        d["lost"] = dot(losses[...], d["all"])

    def react(k):
        def run(d):
            rows = slice(k * CHUNK, (k + 1) * CHUNK)
            later = slice(reactions + k * CHUNK, reactions + (k + 1) * CHUNK)
            first, second = dot(gather[rows, :], d["weights"]), dot(gather[later, :], d["weights"])
            for q in range(CHUNK // LANES):
                part = slice(q * LANES, (q + 1) * LANES)
                base = k * CHUNK + q * LANES
                flow = first[part] * twice(speeds[base : base + LANES, :]) * second[part]
                if base < PHOT:
                    flow = flow * both(sun)
                d["made"].extend(split(flow))

        return run

    def produce(d):
        d["produced"] = dot(products[...], jnp.concatenate(d["made"], axis=0))

    def close(s, last):
        def run(d):
            d["now"] = (d["start"] + d["produced"]) / (1.0 + d["lost"])
            if last:
                dark = d["start"] * twice(decay[...])
                d["now"] = d["start"] = jnp.where(both(lit.at[s]) > 0.0, d["now"], dark)

        return run

    steps = [begin]
    for s in range(SUBSTEPS):
        for sweep in range(PICARD):
            steps += [prepare, react(0), lose]
            steps += [react(k) for k in range(1, reactions // CHUNK)]
            steps += [produce, close(s, sweep == PICARD - 1)]
    steps.append(lambda d: store(low, d["now"]))
    return steps


def chemistry(lows, field, store, *refs):
    lists = [pair_steps(field, low, store, *refs) for low in lows]
    state = [{} for _ in lows]
    for t in range(len(lists[0]) + STAGGER * (len(lows) - 1)):
        for p, steps in enumerate(lists):
            at = t - STAGGER * p
            if 0 <= at < len(steps):
                steps[at](state[p])


def inner_step(center, coefs, g):
    cells = center.shape[1]
    stay, west, _, east = [coefs[k, g : g + 1, :] for k in range(4)]
    return stay * center + west * pltpu.roll(center, 1, 1) + east * pltpu.roll(center, cells - 1, 1)


def side_columns(of_pair, of_other, own, corners, columns):
    rows = of_pair.shape[1]
    left, right = sides(of_pair, of_other)
    near_l, near_r = left(0), right(0)
    zero = jnp.zeros((1, near_l.shape[1]), f32)
    sl, sr, nl, nr = corners if corners else (zero, zero, zero, zero)

    def moved(near, west, east, south, north, side):
        south = jnp.concatenate([south, near[:-1]], axis=0)
        north = jnp.concatenate([near[1:], north], axis=0)
        stay, w, s, e = [side(2)[:, k : k + 1] for k in range(4)]
        return stay * near + w * west + s * south + e * (east + north)

    columns[...] = jnp.zeros_like(columns)
    columns[pl.ds(0, rows, stride=2), :] = near_r
    columns[pl.ds(1, rows, stride=2), :] = near_l
    columns[pl.ds(2 * rows, rows, stride=2), :] = moved(near_r, own[1], right(1), sr, nr, right)
    columns[pl.ds(2 * rows + 1, rows, stride=2), :] = moved(near_l, left(1), own[0], sl, nl, left)
    for k, row in enumerate((sr, sl, nr, nl)):
        columns[4 * rows + k : 4 * rows + k + 1, :] = row
    return columns[...].T


def mover(first, coefs, turned, rows):
    def beside(i):
        return pltpu.roll(turned, LANES - 2 * i - 1, 1)

    known = {}

    def once(g):
        if g not in known:
            i = 2 * rows if g < 0 else 2 * rows + 1 if g >= rows else g
            row, side = first(g)
            known[g] = row + side * beside(i)
        return known[g]

    def moved(g):
        row = inner_step(once(g), coefs, g) + coefs[2, g : g + 1, :] * once(g - 1)
        row = row + coefs[4, g : g + 1, :] * once(g + 1)
        return row + coefs[5, g : g + 1, :] * beside(rows + g)

    return moved


def storer(lows, out, stage, sem):
    copies = []

    def store(low, pair):
        p = lows.index(low)
        stage[2 * p] = pair[:, :LANES]
        stage[2 * p + 1] = pair[:, LANES:]
        copies.append(
            pltpu.make_async_copy(stage.at[pl.ds(2 * p, 2)], out.at[pl.ds(low, 2)], sem.at[p])
        )
        copies[-1].start()

    return store, copies


def finish(lows, moved, refs, out, stage, sem):
    store, copies = storer(lows, out, stage, sem)
    chemistry(lows, moved, store, *refs)
    for c in copies:
        c.wait()


def inner_kernel(
    once, coefs, of_other, of_pair, own,
    gather, products, losses, speeds, decay, sun, lit, out, stage, columns, sem,
):
    rows = once.shape[0]
    turned = side_columns(of_pair, of_other, own, None, columns)
    lows = list(range(rows // 4, rows - rows // 4, 2))
    moved = mover(lambda g: (once[g], coefs[5, g : g + 1, :]), coefs, turned, rows)
    finish(lows, moved, (decay, sun, lit, gather, products, losses, speeds), out, stage, sem)


def outer_kernel(
    once, coefs, of_other, of_pair, own, conc, of_near, of_next,
    gather, products, losses, speeds, decay, sun, lit, _, out, stage, columns, sem,
):
    rows, species, cells = conc.shape
    base = 2 * species
    band = lax.axis_index("lat")
    below = jnp.where(band > 0, 1.0, 0.0)
    above = jnp.where(band < lax.axis_size("lat") - 1, 1.0, 0.0)
    even_band = lax.rem(band, 2) == 0

    def of_south(span):
        return jnp.where(even_band, of_next[span, :], of_near[span, :])

    def of_north(span):
        return jnp.where(even_band, of_near[span, :], of_next[span, :])

    corners = [
        got(slice(base + 8 + k, base + 9 + k)) * inside
        for got, inside in ((of_south, below), (of_north, above))
        for k in range(2)
    ]
    turned = side_columns(of_pair, of_other, own, corners, columns)

    def halo(got, q, inside):
        return got(slice(q * species, (q + 1) * species)) * inside

    def across(got, k, inside):
        return got(slice(base + k, base + k + 1)) * inside

    def outside(got, near, far, beyond, home, back, inside):
        center = halo(got, near, inside)
        stay, west, east = [across(got, k, inside) for k in (0, 1, 3)]
        row = stay * center + west * pltpu.roll(center, 1, 1)
        row = row + east * pltpu.roll(center, cells - 1, 1)
        row = row + across(got, beyond, inside) * halo(got, far, inside)
        return row + across(got, back, inside) * home, across(got, 5, inside)

    def first(g):
        if g < 0:
            return outside(of_south, 1, 0, 2, conc[0], 4, below)
        if g >= rows:
            return outside(of_north, 0, 1, 4, conc[rows - 1], 2, above)
        row, side = once[g], coefs[5, g : g + 1, :]
        if g == 0:
            row = row + coefs[2, g : g + 1, :] * halo(of_south, 1, below)
        if g == rows - 1:
            row = row + coefs[4, g : g + 1, :] * halo(of_north, 0, above)
        return row, side

    lows = list(range(0, rows // 4, 2)) + list(range(rows - rows // 4, rows, 2))
    moved = mover(first, coefs, turned, rows)
    finish(lows, moved, (decay, sun, lit, gather, products, losses, speeds), out, stage, sem)


def local(conc, wind_lon, wind_lat, mixing, sun, rate, night_loss, stoich, plan):
    rows, species, cells = conc.shape
    reactions = rate.shape[0]
    lons = lax.axis_size("lon")
    lats = lax.axis_size("lat")
    params = pltpu.CompilerParams(vmem_limit_bytes=VMEM_LIMIT)
    vmem = pl.BlockSpec(memory_space=pltpu.VMEM)
    hbm = pl.BlockSpec(memory_space=pl.ANY)
    far = pl.BlockSpec(memory_space=pltpu.HBM)

    def pinned(x):
        return pltpu.with_memory_space_constraint(x, pltpu.HBM)

    def shape(*dims, dtype=f32):
        return KEPT(dims, dtype)

    side = shape(3, rows, species)
    ends = shape(2 * species + 16, cells)
    to_other, to_pair, own, to_next, to_near, held, coefs = pl.pallas_call(
        edge_kernel,
        out_shape=(
            side, side, shape(2, rows, species), ends, ends,
            shape(rows, species, cells), shape(6, rows, cells),
        ),
        in_specs=[far] * 4, out_specs=[vmem] * 7,
        scratch_shapes=[
            pltpu.VMEM((3, rows, cells), f32),
            pltpu.VMEM((cells, species), f32),
            pltpu.SemaphoreType.DMA((7,)),
        ],
        compiler_params=params, name="edges",
    )(*[pinned(x) for x in (conc, wind_lon, wind_lat, mixing)])

    pair = [(i, i ^ 1) for i in range(lons)]
    other = [(i, (i - 1) % lons if i % 2 == 0 else (i + 1) % lons) for i in range(lons)]
    near, after = [], []
    for b in range(lats):
        step_near, step_after = (1, -1) if b % 2 == 0 else (-1, 1)
        for perm, c in ((near, b + step_near), (after, b + step_after)):
            for i in range(lons):
                target = (c, i) if 0 <= c < lats else (b, i ^ 1)
                perm.append((b * lons + i, target[0] * lons + target[1]))
    of_other = lax.ppermute(to_other, "lon", other)
    of_pair = lax.ppermute(to_pair, "lon", pair)

    once, *tables = pl.pallas_call(
        table_kernel,
        out_shape=(
            shape(rows, species, cells),
            shape(2 * reactions, 2 * species, dtype=bf16),
            shape(species, 2 * reactions, dtype=bf16),
            shape(species, 6 * species, dtype=bf16),
            shape(reactions, LANES),
            shape(species, LANES),
            shape(rows, LANES),
            shape(SUBSTEPS, rows, LANES),
        ),
        in_specs=[vmem] * 2 + [far] * 5, out_specs=[vmem] * 8,
        scratch_shapes=[
            pltpu.VMEM(stoich.shape, jnp.int32),
            pltpu.VMEM((1, reactions), f32),
            pltpu.VMEM((plan.shape[0], plan.shape[2], plan.shape[1]), jnp.int32),
            pltpu.VMEM((1, species), f32),
            pltpu.VMEM((LANES, LANES), f32),
            pltpu.SemaphoreType.DMA((5,)),
        ],
        cost_estimate=pl.CostEstimate(flops=10**9, transcendentals=0, bytes_accessed=2 * 10**6),
        compiler_params=params, name="tables",
    )(
        held, coefs, pinned(stoich), pinned(rate.reshape(1, reactions)),
        pinned(jnp.swapaxes(plan, 1, 2)), pinned(night_loss.reshape(1, species)), pinned(sun),
    )

    to_next, to_near = pl.pallas_call(
        corner_kernel, out_shape=(ends, ends),
        in_specs=[vmem] * 2 + [hbm] * 3, out_specs=[hbm] * 2,
        scratch_shapes=[pltpu.VMEM((2, 8, species), f32), pltpu.SemaphoreType.DMA((2,))],
        input_output_aliases={2: 0, 3: 1},
        compiler_params=params, name="corners",
    )(of_other, of_pair, to_next, to_near, tables[5])
    of_next = lax.ppermute(to_next, ("lat", "lon"), after)
    of_near = lax.ppermute(to_near, ("lat", "lon"), near)

    shared = (once, coefs, of_other, of_pair, own)
    scratch = [
        pltpu.VMEM((rows // 2, species, cells), f32),
        pltpu.VMEM((LANES, species), f32),
        pltpu.SemaphoreType.DMA((rows // 4,)),
    ]
    inner = pl.pallas_call(
        inner_kernel, out_shape=jax.ShapeDtypeStruct(conc.shape, f32),
        in_specs=[vmem] * 12, out_specs=hbm, scratch_shapes=scratch,
        compiler_params=params, name="inner",
    )(*shared, *tables)
    return pl.pallas_call(
        outer_kernel, out_shape=jax.ShapeDtypeStruct(conc.shape, f32),
        in_specs=[vmem] * 15 + [hbm], out_specs=hbm, scratch_shapes=scratch,
        input_output_aliases={15: 0},
        compiler_params=params, name="outer",
    )(*shared, held, of_near, of_next, *tables, inner)


def solution(mesh):
    field = P("lat", None, "lon")
    cell = P("lat", "lon")
    return jax.shard_map(
        local,
        mesh=mesh,
        in_specs=(field, cell, cell, cell, P(), P(), P(), P(), P()),
        out_specs=field,
        check_vma=False,
    )
```

```python
import jax
import jax.numpy as jnp
from jax import lax
from jax.experimental import pallas as pl
from jax.experimental.pallas import tpu as pltpu
from jax.sharding import PartitionSpec as P

SUBSTEPS = 2
PICARD = 3
PHOT = 128
LANES = 128
VMEM_LIMIT = 48 << 20
KEPT = jax.ShapeDtypeStruct
CHUNK = 256
STAGGER = 2

f32 = jnp.float32
bf16 = jnp.bfloat16


def split(x):
    high = x.astype(bf16)
    return high, (x - high.astype(f32)).astype(bf16)


def twice(x):
    return jnp.concatenate([x, x], axis=1)


def dot(a, b):
    return jnp.dot(a, b, preferred_element_type=f32)


def iota(shape, axis):
    return lax.broadcasted_iota(jnp.int32, shape, axis)


def edge_kernel(
    conc_in, wlon_in, wlat_in, mix_in, to_other, to_pair, own, to_next, to_near, conc, coefs,
    winds, columns, sem,
):
    rows, species, cells = conc.shape
    fetches = [
        pltpu.make_async_copy(ref, winds.at[k], sem.at[k])
        for k, ref in enumerate((wlon_in, wlat_in, mix_in))
    ]
    part = rows // 4
    fetches += [
        pltpu.make_async_copy(
            conc_in.at[pl.ds(q * part, part)], conc.at[pl.ds(q * part, part)], sem.at[3 + q]
        )
        for q in range(4)
    ]
    for fetch in fetches:
        fetch.start()
    for fetch in fetches[:3]:
        fetch.wait()
    wlon, wlat, mix = [winds[k] for k in range(3)]
    place = iota((rows, cells), 1)
    stay = 1.0 - wlon - wlat - 4.0 * mix
    west, south = wlon + mix, wlat + mix
    coefs[0] = stay
    coefs[1] = jnp.where(place == 0, 0.0, west)
    coefs[2] = south
    coefs[3] = jnp.where(place == cells - 1, 0.0, mix)
    coefs[4] = mix
    coefs[5] = jnp.where(place == 0, west, jnp.where(place == cells - 1, mix, 0.0))
    even = lax.rem(lax.axis_index("lon"), 2) == 0

    def put(k, right, left):
        to_pair[k] = jnp.where(even, right, left)
        to_other[k] = jnp.where(even, left, right)

    right, left = jnp.zeros((rows, cells), f32), jnp.zeros((rows, cells), f32)
    for k, ref in enumerate((stay, west, south, mix)):
        right = jnp.where(place == k, ref[:, cells - 1 : cells], right)
        left = jnp.where(place == k, ref[:, 0:1], left)
    put(2, right, left)
    base = 2 * species
    pad = jnp.zeros((2, cells), f32)
    even_band = lax.rem(lax.axis_index("lat"), 2) == 0

    def send(span, north, south):
        to_near[span, :] = jnp.where(even_band, north, south)
        to_next[span, :] = jnp.where(even_band, south, north)

    send(
        slice(base, base + 8),
        *[
            jnp.concatenate([coefs[k, g : g + 1] for k in range(6)] + [pad])
            for g in (rows - 1, 0)
        ],
    )
    lane = iota((species, cells), 1)
    picked = jnp.zeros((species, cells), f32)
    for g in range(rows):
        if g % part == 0:
            fetches[3 + g // part].wait()
        turned = pltpu.roll(conc[g], (4 * g + 2) % cells, 1)
        picked = jnp.where((lane >= 4 * g) & (lane < 4 * g + 4), turned, picked)
    columns[...] = picked.T
    last2, last1, first1, first2 = [columns[pl.ds(q, rows, stride=4), :] for q in range(4)]
    put(0, last1, first1)
    put(1, last2, first2)
    own[0] = first1
    own[1] = last1
    for q in range(2):
        send(slice(q * species, (q + 1) * species), conc[rows - 2 + q], conc[q])


def sides(of_pair, of_other):
    even = lax.rem(lax.axis_index("lon"), 2) == 0
    return (
        lambda k: jnp.where(even, of_other[k], of_pair[k]),
        lambda k: jnp.where(even, of_pair[k], of_other[k]),
    )


def corner_kernel(of_other, of_pair, _, __, ___, to_next, to_near, ends, sem):
    rows = of_pair.shape[1]
    left, right = sides(of_pair, of_other)
    near_l, near_r = left(0), right(0)
    pad = jnp.zeros((6, near_l.shape[1]), f32)
    north, south = [
        jnp.concatenate([near_l[g : g + 1], near_r[g : g + 1], pad], axis=0) for g in (rows - 1, 0)
    ]
    even_band = lax.rem(lax.axis_index("lat"), 2) == 0
    ends[0] = jnp.where(even_band, south, north)
    ends[1] = jnp.where(even_band, north, south)
    copies = []
    for p, ref in enumerate((to_next, to_near)):
        dest = ref.at[pl.ds(ref.shape[0] - 8, 8), :]
        copies.append(pltpu.make_async_copy(ends.at[p], dest, sem.at[p]))
        copies[p].start()
    for c in copies:
        c.wait()


def table_kernel(
    conc, coefs, stoich_in, rate_in, plan_in, night_in, sun, once, gather, products, losses, speeds, decay, sun_own, lit,
    stoich, rate, plan, night, turned, sem,
):
    species = decay.shape[0]
    reactions = stoich_in.shape[1]
    rows = sun_own.shape[0]
    chunks = reactions // LANES
    band = lax.axis_index("lat")
    sector = lax.axis_index("lon")
    here = sun.at[
        pl.ds(pl.multiple_of(band * rows, 8), rows),
        pl.ds(pl.multiple_of(sector * LANES, LANES), LANES),
    ]
    moves = (
        (here, sun_own), (stoich_in, stoich), (rate_in, rate), (plan_in, plan), (night_in, night)
    )
    fetches = [pltpu.make_async_copy(a, b, sem.at[k]) for k, (a, b) in enumerate(moves)]
    for fetch in fetches:
        fetch.start()
    for g in range(rows):
        row = inner_step(conc[g], coefs, g)
        if g > 0:
            row = row + coefs[2, g : g + 1, :] * conc[g - 1]
        if g < rows - 1:
            row = row + coefs[4, g : g + 1, :] * conc[g + 1]
        once[g] = row
    for fetch in fetches:
        fetch.wait()
    down = iota((species, LANES), 0)
    across = iota((LANES, species), 1).astype(f32)
    mats = []
    for k in range(chunks):
        cols = pl.ds(k * LANES, LANES)
        codes = stoich[:, cols]
        row = rate[0:1, cols]
        small = jnp.concatenate([codes.astype(f32), row, jnp.zeros((3, LANES), f32)], axis=0).T
        hot = [(codes[q : q + 1, :] == down).astype(f32) for q in range(4)]
        seconds = None
        for q in range(2):
            picks = (small[:, q : q + 1] == across).astype(f32).astype(bf16)
            gather[pl.ds(q * reactions + k * LANES, LANES), :] = twice(picks)
            seconds = picks
        products[:, 2 * k * LANES : (2 * k + 2) * LANES] = twice((hot[2] + hot[3]).astype(bf16))
        speeds[pl.ds(k * LANES, LANES), :] = jnp.broadcast_to(small[:, 4:5], (LANES, LANES))
        parts = jnp.concatenate(split(hot[0] * row), axis=0)
        mats.append((parts, seconds))

    def total(pairs):
        both = dot(
            jnp.concatenate([p for p, _ in pairs], axis=1),
            jnp.concatenate([q for _, q in pairs], axis=0),
        )
        return both[:species] + both[species:]

    photo, dark = total(mats[: PHOT // LANES]), total(mats[PHOT // LANES :])
    for q, mat in enumerate((dark, photo)):
        high, low = split(mat + mat.T)
        losses[:, 2 * q * species : 2 * (q + 1) * species] = twice(high)
        losses[:, (4 + q) * species : (5 + q) * species] = low
    strip = []
    for s in range(SUBSTEPS):
        codes = plan[s]
        own = jnp.where(iota(codes.shape, 0) == sector, codes, 0).astype(f32)
        strip.append(jnp.sum(own, axis=0, keepdims=True))
    lats = plan.shape[2]
    flags = jnp.concatenate(strip + [jnp.zeros((8 - SUBSTEPS, lats), f32)], axis=0)
    flags = jnp.concatenate([flags, jnp.zeros((8, LANES - lats), f32)], axis=1)
    fade = jnp.exp(-night[...])
    spread = jnp.concatenate([flags, fade, jnp.zeros((7, LANES), f32)], axis=0).T
    decay[...] = jnp.broadcast_to(spread[:, 8:9], (species, LANES))
    for s in range(SUBSTEPS):
        turned[...] = jnp.broadcast_to(spread[:, s : s + 1], turned.shape)
        mine = turned[pl.ds(pl.multiple_of(band * rows, 8), rows), :]
        lit[s] = (mine >= -1.0).astype(f32)


def pair_steps(field, low, store, decay, sun, lit, gather, products, losses, speeds):
    reactions, species = speeds.shape[0], decay.shape[0]

    def both(ref):
        return jnp.concatenate([ref[low : low + 1, :], ref[low + 1 : low + 2, :]], axis=1)

    def begin(d):
        d["start"] = d["now"] = jnp.concatenate([field(low), field(low + 1)], axis=1)

    def prepare(d):
        photo = both(sun)
        high, low_part = split(d["now"])
        sun_high, sun_low = split(d["now"] * photo)
        d["weights"] = jnp.concatenate([high, low_part], axis=0)
        d["all"] = jnp.concatenate([high, low_part, sun_high, sun_low, high, sun_high], axis=0)
        d["made"] = []

    def lose(d):
        d["lost"] = dot(losses[...], d["all"])

    def react(k):
        def run(d):
            rows = slice(k * CHUNK, (k + 1) * CHUNK)
            later = slice(reactions + k * CHUNK, reactions + (k + 1) * CHUNK)
            first, second = dot(gather[rows, :], d["weights"]), dot(gather[later, :], d["weights"])
            for q in range(CHUNK // LANES):
                part = slice(q * LANES, (q + 1) * LANES)
                base = k * CHUNK + q * LANES
                flow = first[part] * twice(speeds[base : base + LANES, :]) * second[part]
                if base < PHOT:
                    flow = flow * both(sun)
                d["made"].extend(split(flow))

        return run

    def produce(d):
        d["produced"] = dot(products[...], jnp.concatenate(d["made"], axis=0))

    def close(s, last):
        def run(d):
            d["now"] = (d["start"] + d["produced"]) / (1.0 + d["lost"])
            if last:
                dark = d["start"] * twice(decay[...])
                d["now"] = d["start"] = jnp.where(both(lit.at[s]) > 0.0, d["now"], dark)

        return run

    steps = [begin]
    for s in range(SUBSTEPS):
        for sweep in range(PICARD):
            steps += [prepare, react(0), lose]
            steps += [react(k) for k in range(1, reactions // CHUNK)]
            steps += [produce, close(s, sweep == PICARD - 1)]
    steps.append(lambda d: store(low, d["now"]))
    return steps


def chemistry(lows, field, store, *refs):
    lists = [pair_steps(field, low, store, *refs) for low in lows]
    state = [{} for _ in lows]
    for t in range(len(lists[0]) + STAGGER * (len(lows) - 1)):
        for p, steps in enumerate(lists):
            at = t - STAGGER * p
            if 0 <= at < len(steps):
                steps[at](state[p])


def inner_step(center, coefs, g):
    cells = center.shape[1]
    stay, west, _, east = [coefs[k, g : g + 1, :] for k in range(4)]
    return stay * center + west * pltpu.roll(center, 1, 1) + east * pltpu.roll(center, cells - 1, 1)


def side_columns(of_pair, of_other, own, corners, columns):
    rows = of_pair.shape[1]
    left, right = sides(of_pair, of_other)
    near_l, near_r = left(0), right(0)
    zero = jnp.zeros((1, near_l.shape[1]), f32)
    sl, sr, nl, nr = corners if corners else (zero, zero, zero, zero)

    def moved(near, west, east, south, north, side):
        south = jnp.concatenate([south, near[:-1]], axis=0)
        north = jnp.concatenate([near[1:], north], axis=0)
        stay, w, s, e = [side(2)[:, k : k + 1] for k in range(4)]
        return stay * near + w * west + s * south + e * (east + north)

    columns[...] = jnp.zeros_like(columns)
    columns[pl.ds(0, rows, stride=2), :] = near_r
    columns[pl.ds(1, rows, stride=2), :] = near_l
    columns[pl.ds(2 * rows, rows, stride=2), :] = moved(near_r, own[1], right(1), sr, nr, right)
    columns[pl.ds(2 * rows + 1, rows, stride=2), :] = moved(near_l, left(1), own[0], sl, nl, left)
    for k, row in enumerate((sr, sl, nr, nl)):
        columns[4 * rows + k : 4 * rows + k + 1, :] = row
    return columns[...].T


def mover(first, coefs, turned, rows):
    def beside(i):
        return pltpu.roll(turned, LANES - 2 * i - 1, 1)

    known = {}

    def once(g):
        if g not in known:
            i = 2 * rows if g < 0 else 2 * rows + 1 if g >= rows else g
            row, side = first(g)
            known[g] = row + side * beside(i)
        return known[g]

    def moved(g):
        row = inner_step(once(g), coefs, g) + coefs[2, g : g + 1, :] * once(g - 1)
        row = row + coefs[4, g : g + 1, :] * once(g + 1)
        return row + coefs[5, g : g + 1, :] * beside(rows + g)

    return moved


def storer(lows, out, stage, sem):
    copies = []

    def store(low, pair):
        p = lows.index(low)
        stage[2 * p] = pair[:, :LANES]
        stage[2 * p + 1] = pair[:, LANES:]
        copies.append(
            pltpu.make_async_copy(stage.at[pl.ds(2 * p, 2)], out.at[pl.ds(low, 2)], sem.at[p])
        )
        copies[-1].start()

    return store, copies


def finish(lows, moved, refs, out, stage, sem):
    store, copies = storer(lows, out, stage, sem)
    chemistry(lows, moved, store, *refs)
    for c in copies:
        c.wait()


def inner_kernel(
    once, coefs, of_other, of_pair, own,
    gather, products, losses, speeds, decay, sun, lit, out, stage, columns, sem,
):
    rows = once.shape[0]
    turned = side_columns(of_pair, of_other, own, None, columns)
    lows = list(range(rows // 4, rows - rows // 4, 2))
    moved = mover(lambda g: (once[g], coefs[5, g : g + 1, :]), coefs, turned, rows)
    finish(lows, moved, (decay, sun, lit, gather, products, losses, speeds), out, stage, sem)


def outer_kernel(
    once, coefs, of_other, of_pair, own, conc, of_near, of_next,
    gather, products, losses, speeds, decay, sun, lit, _, out, stage, columns, sem,
):
    rows, species, cells = conc.shape
    base = 2 * species
    band = lax.axis_index("lat")
    below = jnp.where(band > 0, 1.0, 0.0)
    above = jnp.where(band < lax.axis_size("lat") - 1, 1.0, 0.0)
    even_band = lax.rem(band, 2) == 0

    def of_south(span):
        return jnp.where(even_band, of_next[span, :], of_near[span, :])

    def of_north(span):
        return jnp.where(even_band, of_near[span, :], of_next[span, :])

    corners = [
        got(slice(base + 8 + k, base + 9 + k)) * inside
        for got, inside in ((of_south, below), (of_north, above))
        for k in range(2)
    ]
    turned = side_columns(of_pair, of_other, own, corners, columns)

    def halo(got, q, inside):
        return got(slice(q * species, (q + 1) * species)) * inside

    def across(got, k, inside):
        return got(slice(base + k, base + k + 1)) * inside

    def outside(got, near, far, beyond, home, back, inside):
        center = halo(got, near, inside)
        stay, west, east = [across(got, k, inside) for k in (0, 1, 3)]
        row = stay * center + west * pltpu.roll(center, 1, 1)
        row = row + east * pltpu.roll(center, cells - 1, 1)
        row = row + across(got, beyond, inside) * halo(got, far, inside)
        return row + across(got, back, inside) * home, across(got, 5, inside)

    def first(g):
        if g < 0:
            return outside(of_south, 1, 0, 2, conc[0], 4, below)
        if g >= rows:
            return outside(of_north, 0, 1, 4, conc[rows - 1], 2, above)
        row, side = once[g], coefs[5, g : g + 1, :]
        if g == 0:
            row = row + coefs[2, g : g + 1, :] * halo(of_south, 1, below)
        if g == rows - 1:
            row = row + coefs[4, g : g + 1, :] * halo(of_north, 0, above)
        return row, side

    lows = list(range(0, rows // 4, 2)) + list(range(rows - rows // 4, rows, 2))
    moved = mover(first, coefs, turned, rows)
    finish(lows, moved, (decay, sun, lit, gather, products, losses, speeds), out, stage, sem)


def local(conc, wind_lon, wind_lat, mixing, sun, rate, night_loss, stoich, plan):
    rows, species, cells = conc.shape
    reactions = rate.shape[0]
    lons = lax.axis_size("lon")
    lats = lax.axis_size("lat")
    params = pltpu.CompilerParams(vmem_limit_bytes=VMEM_LIMIT)
    vmem = pl.BlockSpec(memory_space=pltpu.VMEM)
    hbm = pl.BlockSpec(memory_space=pl.ANY)
    far = pl.BlockSpec(memory_space=pltpu.HBM)

    def pinned(x):
        return pltpu.with_memory_space_constraint(x, pltpu.HBM)

    def shape(*dims, dtype=f32):
        return KEPT(dims, dtype)

    side = shape(3, rows, species)
    ends = shape(2 * species + 16, cells)
    to_other, to_pair, own, to_next, to_near, held, coefs = pl.pallas_call(
        edge_kernel,
        out_shape=(
            side, side, shape(2, rows, species), ends, ends,
            shape(rows, species, cells), shape(6, rows, cells),
        ),
        in_specs=[far] * 4, out_specs=[vmem] * 7,
        scratch_shapes=[
            pltpu.VMEM((3, rows, cells), f32),
            pltpu.VMEM((cells, species), f32),
            pltpu.SemaphoreType.DMA((7,)),
        ],
        compiler_params=params, name="edges",
    )(*[pinned(x) for x in (conc, wind_lon, wind_lat, mixing)])

    pair = [(i, i ^ 1) for i in range(lons)]
    other = [(i, (i - 1) % lons if i % 2 == 0 else (i + 1) % lons) for i in range(lons)]
    near, after = [], []
    for b in range(lats):
        step_near, step_after = (1, -1) if b % 2 == 0 else (-1, 1)
        for perm, c in ((near, b + step_near), (after, b + step_after)):
            for i in range(lons):
                target = (c, i) if 0 <= c < lats else (b, i ^ 1)
                perm.append((b * lons + i, target[0] * lons + target[1]))
    of_other = lax.ppermute(to_other, "lon", other)
    of_pair = lax.ppermute(to_pair, "lon", pair)

    once, *tables = pl.pallas_call(
        table_kernel,
        out_shape=(
            shape(rows, species, cells),
            shape(2 * reactions, 2 * species, dtype=bf16),
            shape(species, 2 * reactions, dtype=bf16),
            shape(species, 6 * species, dtype=bf16),
            shape(reactions, LANES),
            shape(species, LANES),
            shape(rows, LANES),
            shape(SUBSTEPS, rows, LANES),
        ),
        in_specs=[vmem] * 2 + [far] * 5, out_specs=[vmem] * 8,
        scratch_shapes=[
            pltpu.VMEM(stoich.shape, jnp.int32),
            pltpu.VMEM((1, reactions), f32),
            pltpu.VMEM((plan.shape[0], plan.shape[2], plan.shape[1]), jnp.int32),
            pltpu.VMEM((1, species), f32),
            pltpu.VMEM((LANES, LANES), f32),
            pltpu.SemaphoreType.DMA((5,)),
        ],
        cost_estimate=pl.CostEstimate(flops=10**9, transcendentals=0, bytes_accessed=2 * 10**6),
        compiler_params=params, name="tables",
    )(
        held, coefs, pinned(stoich), pinned(rate.reshape(1, reactions)),
        pinned(jnp.swapaxes(plan, 1, 2)), pinned(night_loss.reshape(1, species)), pinned(sun),
    )

    to_next, to_near = pl.pallas_call(
        corner_kernel, out_shape=(ends, ends),
        in_specs=[vmem] * 2 + [hbm] * 3, out_specs=[hbm] * 2,
        scratch_shapes=[pltpu.VMEM((2, 8, species), f32), pltpu.SemaphoreType.DMA((2,))],
        input_output_aliases={2: 0, 3: 1},
        compiler_params=params, name="corners",
    )(of_other, of_pair, to_next, to_near, tables[5])
    of_next = lax.ppermute(to_next, ("lat", "lon"), after)
    of_near = lax.ppermute(to_near, ("lat", "lon"), near)

    shared = (once, coefs, of_other, of_pair, own)
    scratch = [
        pltpu.VMEM((rows // 2, species, cells), f32),
        pltpu.VMEM((LANES, species), f32),
        pltpu.SemaphoreType.DMA((rows // 4,)),
    ]
    inner = pl.pallas_call(
        inner_kernel, out_shape=jax.ShapeDtypeStruct(conc.shape, f32),
        in_specs=[vmem] * 12, out_specs=hbm, scratch_shapes=scratch,
        compiler_params=params, name="inner",
    )(*shared, *tables)
    return pl.pallas_call(
        outer_kernel, out_shape=jax.ShapeDtypeStruct(conc.shape, f32),
        in_specs=[vmem] * 15 + [hbm], out_specs=hbm, scratch_shapes=scratch,
        input_output_aliases={15: 0},
        compiler_params=params, name="outer",
    )(*shared, held, of_near, of_next, *tables, inner)


def solution(mesh):
    field = P("lat", None, "lon")
    cell = P("lat", "lon")
    return jax.shard_map(
        local,
        mesh=mesh,
        in_specs=(field, cell, cell, cell, P(), P(), P(), P(), P()),
        out_specs=field,
        check_vma=False,
    )
```
